512 devices in a mesh: gx: 16 (over x_lo, y, core), gy: 32 (over z, x_hi).
Axes of the slice: x: 4 (x_hi: 2, x_lo: 2; x = x_hi * 2 + x_lo), y: 4, z: 16, core: 2. Of those that a mesh axis runs over, the one named last changes fastest.
Arguments:
- phase: float32 [128, 256, 256], P('gx', 'gy'), may hold values from -1 to 1
- solute: float32 [128, 256, 256], P('gx', 'gy'), may hold values from 0 to 1
- undercool: float32 [128, 256, 256], P('gx', 'gy'), may hold values from -1 to 1
- lift_weight: float32 [32, 2], replicated, may hold values from -4 to 4
- spectral_weight: float32 [2, 32, 32, 32, 1024], P(None, 'gx', 'gy'), may hold values from -6 to 6
- local_weight: float32 [32, 32], replicated, may hold values from -1 to 1
- local_bias: float32 [32], replicated, may hold values from -4 to 4
- proj_weight: float32 [32], replicated, may hold values from -1 to 1
- cotangent: float32 [128, 256, 256], P('gx', 'gy'), may hold values from -6 to 6
Outputs:
- phase_next: float32 [128, 256, 256], P('gx', 'gy')
- solute_next: float32 [128, 256, 256], P('gx', 'gy')
- predicted: float32 [128, 256, 256], P('gx', 'gy')
- grad_spectral: float32 [2, 32, 32, 32, 1024], P(None, 'gx', 'gy')
- grad_local: float32 [32, 32], replicated
- grad_proj: float32 [32], replicated
The draws below stay inside these ranges and needn't reach their ends.
All inputs are finite; a program needn't handle non-finite values.
Results may differ from the reference program's by a relative error of at most 0.00029.
Values sent between devices are 32-bit elements; how exact they have to be, the bound alone decides.
A program may use at most 64 MiB of HBM per device.

```python
import math
from functools import reduce
import jax
import jax.numpy as jnp
from jax import lax

NZ = 256
WIDTH = 32
KX = 32
KY = 32
KZ = 32
NX = 128
NY = 256


def steps_of(rng, shape, pieces, smallest, high):
    def one(position, blocks):
        heights = jax.random.uniform(jax.random.fold_in(jax.random.fold_in(rng, 6), position), (blocks,), jnp.float32, smallest / len(pieces), high / len(pieces))
        return jnp.repeat(jnp.exp(heights), shape[position] // blocks).reshape((-1,) + (1,) * (len(shape) - position - 1))

    gain = one(*pieces[0])
    for cut in pieces[1:]:
        gain = gain * one(*cut)
    return gain


def normal_values(own_key, dims, deviation, limit, cuts=(), held_as=jnp.bfloat16):
    loudness = steps_of(own_key, dims, cuts, -0.22, 0.18) if cuts else 1.0
    entries = jax.random.normal(own_key, dims, jnp.float32) * deviation * loudness
    return jnp.minimum(jnp.maximum(entries, -limit), limit).astype(held_as)


def setup_inputs(seed: int = 0) -> dict:
    key_of = jax.random.split(jax.random.key(seed), 10)
    return {
        "phase": jnp.clip(jax.random.uniform(key_of[0], (NX, NY, NZ), jnp.float32, -1.0, 1.0) * steps_of(key_of[0], (NX, NY, NZ), ((0, 16), (1, 32)), -0.4, 0.0), -1.0, 1.0),
        "solute": jnp.clip(1.0 * jax.random.uniform(key_of[1], (NX, NY, NZ), jnp.float32) ** steps_of(key_of[1], (NX, NY, NZ), ((0, 16), (1, 32)), -0.2, 0.2), 0.0, 1.0),
        "undercool": jnp.clip(jax.random.uniform(key_of[2], (NX, NY, NZ), jnp.float32, -1.0, 1.0) * steps_of(key_of[2], (NX, NY, NZ), ((0, 16), (1, 32)), -0.4, 0.0), -1.0, 1.0),
        "lift_weight": normal_values(key_of[3], (WIDTH, 2), 2 ** -0.5, 4.0, (), jnp.float32),
        "spectral_weight": normal_values(key_of[4], (2, KX, KY, KZ, WIDTH * WIDTH), ((NX * NY * NZ / (2 * KX * KY * KZ * WIDTH)) ** 0.5), 6.0, ((1, 16), (2, 32)), jnp.float32),
        "local_weight": normal_values(key_of[5], (WIDTH, WIDTH), WIDTH ** -0.5, 1.0, (), jnp.float32),
        "local_bias": normal_values(key_of[6], (WIDTH,), 1.0, 4.0, (), jnp.float32),
        "proj_weight": normal_values(key_of[7], (WIDTH,), WIDTH ** -0.5, 1.0, (), jnp.float32),
        "cotangent": normal_values(key_of[8], (NX, NY, NZ), 1.0, 6.0, ((0, 16), (1, 32)), jnp.float32),
    }


TIME_STEP = 0.05
COUPLING = 2.0
SOLID_DIFF = 0.05
LIQUID_DIFF = 1.0
PARTITION = 0.15
TRAP_RATE = 4.0
SOLUTE_MEAN = 0.5

def diffusivity(phase_now):
    return SOLID_DIFF + (LIQUID_DIFF - SOLID_DIFF) * 0.5 * (1.0 - jnp.tanh(phase_now))

def update(phase_now, solute_now, undercool, phase_nb, solute_nb, diff_now, diff_nb):
    lap = reduce(jnp.add, phase_nb) - 6.0 * phase_now
    squares = 1.0 - phase_now * phase_now
    rate = lap + phase_now - phase_now * phase_now * phase_now + COUPLING * squares * squares * (undercool - solute_now)
    fluxes = [0.5 * (diff_now + diff_nb[index]) * (solute_nb[index] - solute_now) for index in range(6)]
    divergence = reduce(jnp.add, fluxes)
    speed = TRAP_RATE * jnp.abs(rate)
    keff = (PARTITION + speed) / (1.0 + speed)
    phase_new = phase_now + TIME_STEP * rate
    solute_new = solute_now + TIME_STEP * (divergence + 0.5 * (1.0 - keff) * solute_now * rate)
    return (phase_new, solute_new)

def neighbours(field):
    return [jnp.roll(field, -1, 0), jnp.roll(field, 1, 0), jnp.roll(field, -1, 1), jnp.roll(field, 1, 1), jnp.roll(field, -1, 2), jnp.roll(field, 1, 2)]

def phase_sweep(phase_now, solute_now, undercool):
    diff_now = diffusivity(phase_now)
    return update(phase_now, solute_now, undercool, neighbours(phase_now), neighbours(solute_now), diff_now, neighbours(diff_now))

def freq_index(amount, length):
    index = jnp.arange(amount, dtype=jnp.int32)
    return jnp.where(index < amount // 2, index, index + length - amount).astype(jnp.int32)

def forward_spec(field, zfactor, xfactor, yfactor):
    along_z = jnp.fft.rfft(field, axis=2)[:, :, :KZ] * zfactor
    along_x = jnp.take(jnp.fft.fft(along_z, axis=0), freq_index(KX, NX), axis=0) * xfactor
    along_y = jnp.take(jnp.fft.fft(along_x, axis=1), freq_index(KY, NY), axis=1) * yfactor
    return jnp.stack([jnp.real(along_y), jnp.imag(along_y)]).astype(jnp.float32)

def inverse_spec(spec):
    values = spec[0] + 1j * spec[1]
    full_y = jnp.zeros((KX, NY, KZ), values.dtype).at[:, freq_index(KY, NY)].set(values)
    back_y = jnp.fft.ifft(full_y, axis=1)
    full_x = jnp.zeros((NX, NY, KZ), values.dtype).at[freq_index(KX, NX)].set(back_y)
    back_x = jnp.fft.ifft(full_x, axis=0)
    full_z = jnp.zeros((NX, NY, NZ // 2 + 1), values.dtype).at[:, :, :KZ].set(back_x)
    return jnp.fft.irfft(full_z, n=NZ, axis=2).astype(jnp.float32)

def contract(weights, values):
    return jnp.einsum('abzoi,iabz->oabz', weights, values, precision=lax.Precision.HIGHEST)

def outer(left, right):
    return jnp.einsum('oabz,iabz->abzoi', left, right, precision=lax.Precision.HIGHEST)

def reference(phase, solute, undercool, lift_weight, spectral_weight, local_weight, local_bias, proj_weight, cotangent):
    phase_mid, solute_mid = phase_sweep(phase, solute, undercool)
    phase_next, solute_next = phase_sweep(phase_mid, solute_mid, undercool)
    centred = solute_next - SOLUTE_MEAN
    unit_z = jnp.ones((KZ,), jnp.float32)
    modes_z = jnp.arange(KZ, dtype=jnp.int32)
    weights_z = jnp.where(modes_z == 0, 1.0, 2.0).astype(jnp.float32) / NZ

    def lift_one(row):
        return forward_spec(row[0] * phase_next + row[1] * centred, unit_z, 1.0, 1.0)
    spectrum = lax.map(lift_one, lift_weight)
    spec_t = jnp.transpose(spectrum, (1, 0, 2, 3, 4))
    shaped = spectral_weight.reshape(2, KX, KY, KZ, WIDTH, WIDTH)
    out_real = contract(shaped[0], spec_t[0]) - contract(shaped[1], spec_t[1])
    out_imag = contract(shaped[0], spec_t[1]) + contract(shaped[1], spec_t[0])
    spectral_out = jnp.stack([out_real, out_imag], axis=1)
    mixed = jnp.dot(local_weight, lift_weight, precision=lax.Precision.HIGHEST)

    def channel(total, items):
        spec_o, mix_o, bias_o, proj_o = items
        spectral_field = inverse_spec(spec_o)
        pre_act = spectral_field + mix_o[0] * phase_next + mix_o[1] * centred + bias_o
        activated, gelu_back = jax.vjp(jax.nn.gelu, pre_act)
        grad_pre = gelu_back(proj_o * cotangent)[0]
        grad_modes = forward_spec(grad_pre, weights_z, 1.0 / NX, 1.0 / NY)
        sums = jnp.stack([jnp.sum(grad_pre * phase_next), jnp.sum(grad_pre * centred)])
        proj_sum = jnp.sum(activated * cotangent)
        return (total + proj_o * activated, (grad_modes, sums, proj_sum))
    predicted, (grad_modes, sums, proj_sums) = lax.scan(channel, jnp.zeros((NX, NY, NZ), jnp.float32), (spectral_out, mixed, local_bias, proj_weight))
    grad_t = jnp.transpose(grad_modes, (1, 0, 2, 3, 4))
    grad_real = outer(grad_t[0], spec_t[0]) + outer(grad_t[1], spec_t[1])
    grad_imag = outer(grad_t[1], spec_t[0]) - outer(grad_t[0], spec_t[1])
    grad_spectral = jnp.stack([grad_real, grad_imag]).reshape(2, KX, KY, KZ, WIDTH * WIDTH)
    scale = 1.0 / math.sqrt(NX * NY * NZ)
    grad_local = jnp.dot(sums, lift_weight.T, precision=lax.Precision.HIGHEST) * scale
    grad_proj = proj_sums * scale
    return (phase_next, solute_next, predicted, grad_spectral, grad_local, grad_proj)
```

```python
import math

import numpy as np

import jax
import jax.numpy as jnp
from jax import lax
from jax.sharding import PartitionSpec as P

TIME_STEP = 0.05
COUPLING = 2.0
SOLID_DIFF = 0.05
LIQUID_DIFF = 1.0
PARTITION = 0.15
TRAP_RATE = 4.0
SOLUTE_MEAN = 0.5
GELU_K = math.sqrt(2.0 / math.pi)
GELU_C = 0.044715
F32 = jnp.float32


def mm(a, b):
    return jnp.dot(a, b, precision=lax.Precision.HIGH, preferred_element_type=F32)


def signed(count):
    index = np.arange(count)
    return np.where(index < count // 2, index, index - count)


def trig(freqs, places, length, factor=1.0):
    angle = 2.0 * np.pi * ((freqs[:, None] * places[None, :]) % length) / length
    return np.cos(angle) * factor, np.sin(angle) * factor


def z_tables(modes, depth):
    cos, sin = trig(np.arange(modes), np.arange(depth), depth)
    lanes = 2 * modes
    weight = np.where(np.arange(modes) == 0, 1.0, 2.0) / depth
    both = np.stack([cos, -sin])

    def blocks(one):
        full = np.zeros((2 * depth, 2 * lanes))
        full[:depth, :lanes] = one
        full[depth:, lanes:] = one
        return full

    plain = both.reshape(lanes, depth).T
    heavy = (both * weight[None, :, None]).reshape(lanes, depth).T
    return blocks(plain), blocks(heavy), blocks(heavy).T


def rot(v, quarter):
    lane = lax.broadcasted_iota(jnp.int32, v.shape, v.ndim - 1)
    imag = (lane // quarter) % 2 == 1
    return jnp.where(imag, -jnp.roll(v, quarter, v.ndim - 1), jnp.roll(v, -quarter, v.ndim - 1))


def diffusivity(phase_now):
    return SOLID_DIFF + (LIQUID_DIFF - SOLID_DIFF) * 0.5 * (1.0 - jnp.tanh(phase_now))


def around(f):
    centre = f[1:-1, 1:-1]
    return [
        f[2:, 1:-1],
        f[:-2, 1:-1],
        f[1:-1, 2:],
        f[1:-1, :-2],
        jnp.roll(centre, -1, 2),
        jnp.roll(centre, 1, 2),
    ]


def sweep(phase, solute, undercool):
    diff = diffusivity(phase)
    p, c, d = phase[1:-1, 1:-1], solute[1:-1, 1:-1], diff[1:-1, 1:-1]
    lap = sum(around(phase)) - 6.0 * p
    squares = 1.0 - p * p
    rate = lap + p - p * p * p + COUPLING * squares * squares * (undercool - c)
    div = sum(0.5 * (d + dn) * (cn - c) for dn, cn in zip(around(diff), around(solute)))
    speed = TRAP_RATE * jnp.abs(rate)
    keff = (PARTITION + speed) / (1.0 + speed)
    return p + TIME_STEP * rate, c + TIME_STEP * (div + 0.5 * (1.0 - keff) * c * rate)


def extended(cells, axis, dim, width):
    count = lax.axis_size(axis)
    head = lax.slice_in_dim(cells, 0, width, axis=dim)
    tail = lax.slice_in_dim(cells, cells.shape[dim] - width, cells.shape[dim], axis=dim)
    up = lax.ppermute(tail, axis, [(i, (i + 1) % count) for i in range(count)])
    down = lax.ppermute(head, axis, [((i + 1) % count, i) for i in range(count)])
    return jnp.concatenate([up, cells, down], axis=dim)


def swap(data, axis):
    shape = data.shape
    flat = data.reshape(shape[0], -1)
    return lax.all_to_all(flat, axis, split_axis=0, concat_axis=0, tiled=True).reshape(shape)


def per_device(phase, solute, undercool, lift, weight, local_weight, bias, proj, cotangent):
    gx, gy = lax.axis_size("gx"), lax.axis_size("gy")
    ix, iy = lax.axis_index("gx"), lax.axis_index("gy")
    cx, cy, depth = phase.shape
    own_kx, own_ky, kz = weight.shape[1:4]
    width = lift.shape[0]
    nx, ny, kx, ky = gx * cx, gy * cy, gx * own_kx, gy * own_ky
    pairs = width // 2
    assert pairs == gx and pairs * own_kx == gy and own_ky == 1
    lanes = 4 * kz
    fx, fy = signed(kx), signed(ky)
    zf, zg, zi = (jnp.asarray(t, F32) for t in z_tables(kz, depth))
    cosx, sinx = trig(fx, np.arange(nx), nx)
    cosy, siny = trig(fy, np.arange(ny), ny)

    def own(cos, sin, count, size, at):
        both = np.concatenate([cos, sin]).reshape(-1, count, size).transpose(1, 0, 2)
        return jnp.asarray(both, F32)[at]

    stack = jnp.stack([phase, solute, undercool])
    stack = extended(extended(stack, "gx", 1, 2), "gy", 2, 2)
    mid_p, mid_c = sweep(stack[0], stack[1], stack[2, 1:-1, 1:-1])
    phase_next, solute_next = sweep(mid_p, mid_c, undercool)

    pf = jnp.swapaxes(phase_next, 0, 1).reshape(cy * cx, depth)
    cf = jnp.swapaxes(solute_next - SOLUTE_MEAN, 0, 1).reshape(cy * cx, depth)
    along = mm(jnp.concatenate([pf, cf], 1), zf).reshape(cy, cx, lanes)
    wave = jnp.einsum("kx,yxl->kyl", own(cosx, sinx, gx, cx, ix), along, precision=lax.Precision.HIGH)
    wave = wave[:kx] + rot(wave[kx:], kz)
    got = swap(wave.reshape(gx, own_kx, cy, lanes), "gx").sum(0)
    wave = jnp.einsum("ky,xyl->kxl", own(cosy, siny, gy, cy, iy), got, precision=lax.Precision.HIGH)
    wave = wave[:ky] + rot(wave[ky:], kz)
    spec = swap(wave.reshape(gy, own_kx, lanes), "gy").sum(0)
    spec = spec.reshape(own_kx, 2, 2, kz)

    shaped = weight.reshape(2, own_kx, kz, width, width)
    both = jnp.einsum("rxzoi,ic->rxcoz", shaped, lift, precision=lax.Precision.HIGH)
    re, im = spec[:, :, 0, None, :], spec[:, :, 1, None, :]
    out_re = (both[0] * re - both[1] * im).sum(1)
    out_im = (both[0] * im + both[1] * re).sum(1)
    out = jnp.stack([out_re, out_im], 2).reshape(own_kx, 2, pairs, 2, kz)
    out = out.transpose(2, 0, 1, 3, 4).reshape(gy, lanes)

    got = swap(out, "gy")
    table = jnp.asarray(np.concatenate([cosy, -siny]).T / ny, F32)
    lines = mm(table, jnp.concatenate([got, rot(got, kz)], 0))
    got = swap(lines.reshape(gy, cy, lanes), "gy")
    got = swap(got.reshape(gx, own_kx, cy, lanes), "gx").reshape(kx, cy * lanes)
    turned = rot(got.reshape(kx, cy, lanes), kz).reshape(kx, cy * lanes)
    table = jnp.asarray(np.concatenate([cosx, -sinx]).T / nx, F32)
    lines = mm(table, jnp.concatenate([got, turned], 0))
    lines = lines.reshape(gx, cx, cy, lanes).transpose(0, 2, 1, 3)
    got = swap(lines, "gx").reshape(pairs * cy * cx, lanes)
    field = mm(got, zi).reshape(pairs, cy * cx, 2, depth)

    mixed = jnp.dot(local_weight, lift, precision=lax.Precision.HIGHEST)

    def per_channel(v):
        return v.reshape(2, pairs).T[:, None, :, None]

    pre = field + per_channel(mixed[:, 0]) * pf[:, None] + per_channel(mixed[:, 1]) * cf[:, None] + per_channel(bias)
    cot = jnp.swapaxes(cotangent, 0, 1).reshape(cy * cx, 1, depth)
    square = pre * pre
    tanh = jnp.tanh(GELU_K * (pre + GELU_C * (square * pre)))
    half = 0.5 * (1.0 + tanh)
    act = pre * half
    slope = half + 0.5 * GELU_K * pre * (1.0 - tanh * tanh) * (1.0 + 3.0 * GELU_C * square)
    predicted = (per_channel(proj) * act).sum((0, 2)).reshape(cy, cx, depth)
    predicted = jnp.swapaxes(predicted, 0, 1)
    grad = per_channel(proj) * cot * slope
    sums = jnp.stack(
        [(grad * pf[:, None]).sum((1, 3)), (grad * cf[:, None]).sum((1, 3)), (act * cot).sum((1, 3))]
    )

    along = mm(grad.reshape(pairs * cy * cx, 2 * depth), zg).reshape(gx, cy, cx, lanes)
    got = swap(along, "gx").transpose(0, 2, 1, 3).reshape(nx, cy * lanes)
    wave = mm(jnp.asarray(np.concatenate([cosx, sinx]) / nx, F32), got).reshape(2, kx, cy, lanes)
    wave = wave[0] + rot(wave[1], kz)
    row = jnp.pad(sums.reshape(-1), (0, lanes - 3 * width)) if lanes >= 3 * width else sums.reshape(-1)
    row = jnp.pad(row.reshape(1, lanes), ((0, cy - 1), (0, 0)))
    wave = jnp.concatenate([wave.reshape(gx, own_kx * cy, lanes), jnp.broadcast_to(row, (gx, cy, lanes))], 1)
    got = swap(wave, "gx")
    row = got[:, own_kx * cy].sum(0)
    got = swap(got[:, : own_kx * cy].reshape(gy, cy, lanes), "gy").reshape(ny, lanes)
    wave = mm(jnp.asarray(np.concatenate([cosy, siny]) / ny, F32), got)
    wave = wave[:ky] + rot(wave[ky:], kz)
    wave = jnp.stack([wave, jnp.broadcast_to(row, (gy, lanes))], 1)
    got = swap(wave, "gy")
    sums = got[:, 1].sum(0)[: 3 * width].reshape(3, pairs, 2).transpose(0, 2, 1).reshape(3, width)
    modes = got[:, 0].reshape(pairs, own_kx, 2, 2, kz).transpose(3, 1, 4, 2, 0).reshape(2, own_kx, kz, width)

    source = jnp.einsum("xcrz,ic->rxzi", spec, lift, precision=lax.Precision.HIGH)
    g, s = modes[:, :, :, :, None], source[:, :, :, None, :]
    grad_spectral = jnp.stack([g[0] * s[0] + g[1] * s[1], g[1] * s[0] - g[0] * s[1]])
    grad_spectral = grad_spectral.reshape(2, own_kx, 1, kz, width * width)
    scale = 1.0 / math.sqrt(nx * ny * depth)
    grad_local = jnp.dot(sums[:2].T, lift.T, precision=lax.Precision.HIGHEST) * scale
    return phase_next, solute_next, predicted, grad_spectral, grad_local, sums[2] * scale


def solution(mesh):
    tile, modes = P("gx", "gy", None), P(None, "gx", "gy", None, None)
    return jax.shard_map(
        per_device,
        mesh=mesh,
        in_specs=(tile, tile, tile, P(), modes, P(), P(), P(), tile),
        out_specs=(tile, tile, tile, modes, P(), P()),
        check_vma=False,
    )
```

```python
import math

import numpy as np

import jax
import jax.numpy as jnp
from jax import lax
from jax.experimental import pallas as pl
from jax.experimental.pallas import tpu as pltpu
from jax.sharding import PartitionSpec as P

TIME_STEP = 0.05
COUPLING = 2.0
SOLID_DIFF = 0.05
LIQUID_DIFF = 1.0
PARTITION = 0.15
TRAP_RATE = 4.0
SOLUTE_MEAN = 0.5
GELU_K = math.sqrt(2.0 / math.pi)
GELU_C = 0.044715
F32 = jnp.float32
MESH = pl.DeviceIdType.MESH


def signed(count):
    index = np.arange(count)
    return np.where(index < count // 2, index, index - count)


def trig(freqs, places, length, factor=1.0):
    angle = 2.0 * np.pi * ((freqs[:, None] * places[None, :]) % length) / length
    return np.cos(angle) * factor, np.sin(angle) * factor


def z_tables(modes, depth):
    cos, sin = trig(np.arange(modes), np.arange(depth), depth)
    lanes = 2 * modes
    weight = np.where(np.arange(modes) == 0, 1.0, 2.0) / depth
    both = np.stack([cos, -sin])

    def blocks(one):
        full = np.zeros((2 * depth, 2 * lanes))
        full[:depth, :lanes] = one
        full[depth:, lanes:] = one
        return full

    plain = both.reshape(lanes, depth).T
    heavy = (both * weight[None, :, None]).reshape(lanes, depth).T
    return blocks(plain), blocks(heavy), blocks(heavy).T


def tables(gx, gy, cx, cy, depth, kx, ky, kz):
    nx, ny = gx * cx, gy * cy
    own = kx // gx
    zf, zg, zi = z_tables(kz, depth)
    cosx, sinx = trig(signed(kx), np.arange(nx), nx)
    cosy, siny = trig(signed(ky), np.arange(ny), ny)
    tx = np.concatenate([cosx, sinx]).reshape(2 * kx, gx, cx).transpose(1, 2, 0)
    ty = np.zeros((gy, own, cy, 2, ky, own))
    both = np.stack([cosy, siny]).reshape(2, ky, gy, cy).transpose(2, 3, 0, 1)
    for k in range(own):
        ty[:, k, :, :, :, k] = both
    ty = ty.reshape(gy, own * cy, 2 * ky * own)
    tyi = np.concatenate([cosy, -siny]).T / ny
    txi = np.concatenate([cosx, -sinx]).T / nx
    txf = np.stack([cosx, sinx]).reshape(2, gx, own, nx).transpose(0, 2, 1, 3).reshape(2 * kx, nx) / nx
    tyf = np.concatenate([cosy, siny]) / ny
    return [np.asarray(t, np.float32) for t in (zf, zg, zi, tx, ty, tyi, txi, txf, tyf)]


def dot(a, b, dims=((1,), (0,))):
    return lax.dot_general(a, b, (dims, ((), ())), precision=lax.Precision.HIGHEST, preferred_element_type=F32)


def iota(shape, dim):
    return lax.broadcasted_iota(jnp.int32, shape, dim)


def rot(v):
    imag = (iota(v.shape, 1) // 32) % 2 == 1
    return jnp.where(imag, -pltpu.roll(v, 32, 1), pltpu.roll(v, 96, 1))


def diffusivity(p):
    return SOLID_DIFF + (LIQUID_DIFF - SOLID_DIFF) * 0.5 * (1.0 - jnp.tanh(p))


def around(ref, x):
    centre = ref[x]
    rows, depth = centre.shape
    return centre, [
        ref[x + 1],
        ref[x - 1],
        pltpu.roll(centre, rows - 1, 0),
        pltpu.roll(centre, 1, 0),
        pltpu.roll(centre, depth - 1, 1),
        pltpu.roll(centre, 1, 1),
    ]


def advance(p_ref, c_ref, d_ref, undercool, x):
    p, p_nb = around(p_ref, x)
    c, c_nb = around(c_ref, x)
    d, d_nb = around(d_ref, x)
    total = p_nb[0]
    for one in p_nb[1:]:
        total = total + one
    squares = 1.0 - p * p
    rate = total - 6.0 * p + p - p * p * p + COUPLING * squares * squares * (undercool - c)
    div = 0.0
    for dn, cn in zip(d_nb, c_nb):
        div = div + 0.5 * (d + dn) * (cn - c)
    speed = TRAP_RATE * jnp.abs(rate)
    keff = (PARTITION + speed) / (1.0 + speed)
    return p + TIME_STEP * rate, c + TIME_STEP * (div + 0.5 * (1.0 - keff) * c * rate)


def kernel(
    dims, phase, solute, undercool, cotangent, weight, lift, local, bias, proj,
    zf, zg, zi, tx, ty, tyi, txi, txf, tyf,
    phase_out, solute_out, predicted_out, spectral_out, local_out, proj_out,
    yhi, ylo, from_ylo, from_yhi, from_corner, from_xlo, from_xhi,
    pad_p, pad_c, pad_d, pad_u, mid_p, mid_c, mid_d, flat, cells, cot, total, coef, lifted, blend, source, field, sums,
    send1, recv1, send2, recv2, send3, recv3, send4, recv4, recv5, send6, recv6, send7, recv7,
    send8, recv8, recv9, send10, recv10, send11, recv11, modes,
    halo_send, halo_recv, send_sem, recv_sem, recv6_sem,
):
    gx, gy, group = dims
    ix, iy = lax.axis_index("gx"), lax.axis_index("gy")
    east, west = lax.rem(ix + 1, gx), lax.rem(ix + gx - 1, gx)
    north, south = lax.rem(iy + 1, gy), lax.rem(iy + gy - 1, gy)
    width = lift.shape[0]
    pairs = width // 2
    kx, ky = 2 * gx, gy
    square = width * width
    barrier = pltpu.get_barrier_semaphore()

    def greet(axis, mine, count):
        def one(j, carry):
            pl.semaphore_signal(barrier, inc=1, device_id={axis: lax.rem(mine + j, count)}, device_id_type=MESH)
            return carry

        lax.fori_loop(1, count, one, 0)

    for a in (east, west):
        for b in (north, south):
            pl.semaphore_signal(barrier, inc=1, device_id={"gx": a, "gy": b}, device_id_type=MESH)
    greet("gx", ix, gx)
    greet("gy", iy, gy)

    row = iota((8, 8, phase.shape[2]), 1)
    p, c, u = phase[...], solute[...], undercool[...]
    yhi[...] = jnp.where(row >= 6, p, jnp.where(row >= 4, pltpu.roll(c, 6, 1), pltpu.roll(u, 4, 1)))
    ylo[...] = jnp.where(row < 2, p, jnp.where(row < 4, pltpu.roll(c, 2, 1), pltpu.roll(u, 4, 1)))
    pad_p[2:10, 8:16, :] = p
    pad_c[2:10, 8:16, :] = c
    pad_u[1:9, 8:16, :] = u

    lane = iota((width, square), 1)
    inner = lane % width == iota((width, square), 0)
    for k in range(2):
        spread = jnp.where(inner, jnp.broadcast_to(lift[:, k : k + 1], (width, square)), 0.0)
        lifted[k : k + 1, :] = jnp.sum(spread, axis=0, keepdims=True)
        column = jnp.broadcast_to(lift[:, k : k + 1], (width, 128))
        coef[k * width : (k + 1) * width] = dot(local[...], column).reshape(width, 1, 128)
    eye = iota((width, width), 0) == iota((width, width), 1)
    for k, vector in ((2, bias), (3, proj)):
        diagonal = jnp.where(eye, jnp.broadcast_to(vector[...], (width, width)), 0.0)
        coef[k * width : (k + 1) * width] = dot(diagonal, jnp.ones((width, 128), F32)).reshape(width, 1, 128)
    outer = jnp.where(lane // width == iota((width, square), 0), 1.0, 0.0)
    src, dst = iota((128, 128), 0), iota((128, 128), 1)
    for k in range(2):
        both = dot(outer, weight[...] * lifted[k : k + 1, :], ((1,), (1,)))
        for part in range(2):
            for x in range(2):
                value = 0.0
                for par in range(2):
                    pick = (src % 32 == dst % 32) & (src // 32 == part * 2 + x) & (dst // 64 == par)
                    value = value + dot(both[par * pairs : (par + 1) * pairs], jnp.where(pick, 1.0, 0.0))
                blend[2 * k + part, pl.ds(x, pairs, stride=2), :] = value
    sums[...] = jnp.zeros_like(sums)
    total[...] = jnp.zeros_like(total)
    depth = phase.shape[2]
    for x in range(8):
        for h in range(2):
            flat[h, 8 * x : 8 * x + 8, :] = cotangent[x, :, 128 * h : 128 * h + 128]
    for y in range(8):
        for h in range(2):
            cot[8 * y : 8 * y + 8, 128 * h : 128 * h + 128] = flat[h, pl.ds(y, 8, stride=8), :]

    pl.semaphore_wait(barrier, 4 + gx - 1 + gy - 1)

    def push(source_ref, target_ref, slot, where):
        copy = pltpu.make_async_remote_copy(
            src_ref=source_ref,
            dst_ref=target_ref,
            send_sem=halo_send.at[slot],
            recv_sem=halo_recv.at[slot],
            device_id=where,
            device_id_type=MESH,
        )
        copy.start()
        return copy

    copies = [
        push(yhi, from_ylo, 0, {"gy": north}),
        push(ylo, from_yhi, 1, {"gy": south}),
        push(yhi.at[7], from_corner.at[0], 2, {"gx": east, "gy": north}),
        push(yhi.at[0], from_corner.at[1], 3, {"gx": west, "gy": north}),
        push(ylo.at[7], from_corner.at[2], 4, {"gx": east, "gy": south}),
        push(ylo.at[0], from_corner.at[3], 5, {"gx": west, "gy": south}),
        push(phase.at[6:8], from_xlo.at[0:2], 6, {"gx": east}),
        push(solute.at[6:8], from_xlo.at[2:4], 7, {"gx": east}),
        push(undercool.at[7:8], from_xlo.at[4:5], 8, {"gx": east}),
        push(phase.at[0:2], from_xhi.at[0:2], 9, {"gx": west}),
        push(solute.at[0:2], from_xhi.at[2:4], 10, {"gx": west}),
        push(undercool.at[0:1], from_xhi.at[4:5], 11, {"gx": west}),
    ]
    for copy in copies:
        copy.wait_recv()

    def lay(rows, low, planes):
        at = slice(0, 8) if low else slice(16, 24)
        turn = 1 if low else -1
        pad_p[planes, at, :] = rows
        pad_c[planes, at, :] = pltpu.roll(rows, (2 * turn) % 8, 1)
        pad_u[slice(planes.start - 1, planes.stop - 1), at, :] = pltpu.roll(rows, 4, 1)

    lay(from_ylo[...], True, slice(2, 10))
    lay(from_yhi[...], False, slice(2, 10))
    lay(from_corner[0:1], True, slice(1, 2))
    lay(from_corner[1:2], True, slice(10, 11))
    lay(from_corner[2:3], False, slice(1, 2))
    lay(from_corner[3:4], False, slice(10, 11))
    pad_p[0:2, 8:16, :] = from_xlo[0:2]
    pad_c[0:2, 8:16, :] = from_xlo[2:4]
    pad_u[0:1, 8:16, :] = from_xlo[4:5]
    pad_p[10:12, 8:16, :] = from_xhi[0:2]
    pad_c[10:12, 8:16, :] = from_xhi[2:4]
    pad_u[9:10, 8:16, :] = from_xhi[4:5]

    def first_diff(x, carry):
        pad_d[x] = diffusivity(pad_p[x])
        return carry

    def first(x, carry):
        new_p, new_c = advance(pad_p, pad_c, pad_d, pad_u[x], x + 1)
        mid_p[x] = new_p
        mid_c[x] = new_c
        mid_d[x] = diffusivity(new_p)
        return carry

    def second(x, carry):
        new_p, new_c = advance(mid_p, mid_c, mid_d, pad_u[x + 1], x + 1)
        new_p, new_c = new_p[8:16], new_c[8:16]
        phase_out[x] = new_p
        solute_out[x] = new_c
        at = pl.multiple_of(8 * x, 8)
        for h in range(2):
            flat[h, pl.ds(at, 8), :] = new_p[:, 128 * h : 128 * h + 128]
            flat[2 + h, pl.ds(at, 8), :] = new_c[:, 128 * h : 128 * h + 128] - SOLUTE_MEAN
        return carry

    lax.fori_loop(0, 12, first_diff, 0)
    lax.fori_loop(0, 10, first, 0)
    lax.fori_loop(0, 8, second, 0)
    for y in range(8):
        for h in range(4):
            cells[8 * y : 8 * y + 8, 128 * h : 128 * h + 128] = flat[h, pl.ds(y, 8, stride=8), :]

    def exchange(axis, phase_id, sends, receives):
        mine, count = (ix, gx) if axis == "gx" else (iy, gy)
        pltpu.make_async_copy(sends(mine), receives(mine), recv_sem.at[phase_id]).start()

        def one(j, carry):
            peer = lax.rem(mine + j, count)
            pltpu.make_async_remote_copy(
                src_ref=sends(peer),
                dst_ref=receives(mine),
                send_sem=send_sem.at[phase_id],
                recv_sem=recv_sem.at[phase_id],
                device_id={axis: peer},
                device_id_type=MESH,
            ).start()
            return carry

        lax.fori_loop(1, count, one, 0)

    def arrived(phase_id, whole):
        pltpu.make_async_copy(whole, whole, recv_sem.at[phase_id]).wait()

    along = dot(cells[...], zf[...])
    lines = jnp.concatenate([along[8 * y : 8 * y + 8] for y in range(8)], axis=1)
    wave = dot(tx[ix].T, lines)
    for y in range(8):
        at = slice(128 * y, 128 * y + 128)
        send1[pl.ds(y, kx, stride=8), :] = wave[:kx, at] + rot(wave[kx:, at])
    exchange("gx", 1, lambda q: send1.at[pl.ds(pl.multiple_of(16 * q, 16), 16)], lambda q: recv1.at[q])
    arrived(1, recv1)
    got = recv1[0]
    for q in range(1, gx):
        got = got + recv1[q]
    wave = dot(ty[iy].T, got)
    wave = wave[: 2 * ky] + rot(wave[2 * ky :])
    send2[...] = wave.reshape(2 * ky, 1, 128)
    exchange("gy", 2, lambda q: send2.at[pl.ds(2 * q, 2)], lambda q: recv2.at[pl.ds(2 * q, 2)])
    arrived(2, recv2)
    got = recv2[...].reshape(gy, 2, 128).sum(0)

    even = iota((gy, 128), 0) % 2 == 0
    spread = jnp.where(even, jnp.broadcast_to(got[0:1], (gy, 128)), jnp.broadcast_to(got[1:2], (gy, 128)))
    turned = pltpu.roll(spread, 64, 1)
    low = iota((gy, 128), 1) < 64
    value = 0.0
    for k in range(2):
        one = jnp.where(low, spread, turned) if k == 0 else jnp.where(low, turned, spread)
        value = value + blend[2 * k] * one - blend[2 * k + 1] * rot(one)
    send3[...] = value.reshape(gy, 1, 128)
    exchange("gy", 3, lambda q: send3.at[pl.ds(q, 1)], lambda q: recv3.at[pl.ds(q, 1)])

    for x in range(2):
        diagonal = jnp.where(src == dst, jnp.broadcast_to(got[x : x + 1], (128, 128)), 0.0)
        column = jnp.sum(diagonal, axis=1, keepdims=True)
        source[64 * x : 64 * x + 64, :] = column[:64] * lifted[0:1, :] + column[64:] * lifted[1:2, :]

    arrived(3, recv3)
    got = recv3[...].reshape(ky, 128)
    send4[...] = dot(tyi[...], jnp.concatenate([got, rot(got)], axis=0)).reshape(gy, 8, 128)
    exchange("gy", 4, lambda q: send4.at[q], lambda q: recv4.at[q])
    arrived(4, recv4)
    exchange("gx", 5, lambda q: recv4.at[pl.ds(2 * q, 2)], lambda q: recv5.at[pl.ds(2 * q, 2)])
    arrived(5, recv5)
    lines = []
    for y in range(8):
        got = recv5[:, y, :]
        lines.append(jnp.concatenate([got, rot(got)], axis=0))
    wave = dot(txi[...], jnp.concatenate(lines, axis=1))
    for y in range(8):
        send6[:, y] = wave[:, 128 * y : 128 * y + 128].reshape(gx, 8, 128)

    pltpu.make_async_copy(send6.at[ix], recv6.at[ix], recv6_sem.at[ix]).start()

    def give(j, carry):
        peer = lax.rem(ix + j, gx)
        pltpu.make_async_remote_copy(
            src_ref=send6.at[peer],
            dst_ref=recv6.at[ix],
            send_sem=send_sem.at[6],
            recv_sem=recv6_sem.at[ix],
            device_id={"gx": peer},
            device_id_type=MESH,
        ).start()
        return carry

    lax.fori_loop(1, gx, give, 0)

    def wide(o):
        one = coef[o]
        return jnp.concatenate([one, one], axis=1)

    def step(j, carry):
        owners = [lax.rem(ix + gx - (j * group + t), gx) for t in range(group)]
        for owner in owners:
            pltpu.make_async_copy(recv6.at[owner], recv6.at[owner], recv6_sem.at[owner]).wait()
        got = jnp.concatenate([recv6[owner].reshape(64, 128) for owner in owners], axis=0)
        field[...] = dot(got, zi[...])
        for t, owner in enumerate(owners):
            factors = [[wide(k * width + par * pairs + owner) for k in range(4)] for par in range(2)]

            def block(r, acc):
                at = pl.multiple_of(8 * r, 8)
                here = pl.ds(pl.multiple_of(64 * t + 8 * r, 8), 8)
                p, c, w = cells[pl.ds(at, 8), :depth], cells[pl.ds(at, 8), depth:], cot[pl.ds(at, 8), :]
                acc = list(acc)
                out = total[pl.ds(at, 8), :]
                for par in range(2):
                    m0, m1, b, q = factors[par]
                    side = slice(par * depth, (par + 1) * depth)
                    pre = field[here, side] + m0 * p + m1 * c + b
                    power = pre * pre
                    tanh = jnp.tanh(GELU_K * (pre + GELU_C * (power * pre)))
                    half = 0.5 * (1.0 + tanh)
                    act = pre * half
                    slope = half + (0.5 * GELU_K) * pre * (1.0 - tanh * tanh) * (1.0 + (3.0 * GELU_C) * power)
                    out = out + q * act
                    grad = q * w * slope
                    field[here, side] = grad
                    acc[3 * par] = acc[3 * par] + grad * p
                    acc[3 * par + 1] = acc[3 * par + 1] + grad * c
                    acc[3 * par + 2] = acc[3 * par + 2] + act * w
                total[pl.ds(at, 8), :] = out
                return tuple(acc)

            zero = jnp.zeros((8, depth), F32)
            acc = lax.fori_loop(0, 8, block, (zero,) * 6)
            for par in range(2):
                for k in range(3):
                    one = jnp.sum(acc[3 * par + k], axis=0, keepdims=True)
                    sums[k * width + par * pairs + owner] = one[:, :128] + one[:, 128:]
        wave = dot(field[...], zg[...])
        for t, owner in enumerate(owners):
            send7[owner] = wave[64 * t : 64 * t + 64].reshape(8, 8, 128)

            @pl.when(owner == ix)
            def _():
                pltpu.make_async_copy(send7.at[owner], recv7.at[ix], recv_sem.at[7]).start()

            @pl.when(owner != ix)
            def _():
                pltpu.make_async_remote_copy(
                    src_ref=send7.at[owner],
                    dst_ref=recv7.at[ix],
                    send_sem=send_sem.at[7],
                    recv_sem=recv_sem.at[7],
                    device_id={"gx": owner},
                    device_id_type=MESH,
                ).start()

        return carry

    lax.fori_loop(0, gx // group, step, 0)
    for h in range(2):
        flat[h] = total[:, 128 * h : 128 * h + 128]
    for x in range(8):
        for h in range(2):
            predicted_out[x, :, 128 * h : 128 * h + 128] = flat[h, pl.ds(x, 8, stride=8), :]
    added = dot(jnp.ones((8, 128), F32), sums[...].reshape(128, 128), ((1,), (1,)))
    for q in range(gx):
        send8[24 * q + 16 : 24 * q + 24, :] = added

    arrived(7, recv7)
    lines = [recv7[:, y].reshape(8 * gx, 128) for y in range(8)]
    wave = dot(txf[...], jnp.concatenate(lines, axis=1))
    for y in range(8):
        at = slice(128 * y, 128 * y + 128)
        one = wave[:kx, at] + rot(wave[kx:, at])
        for k in range(2):
            send8[pl.ds(8 * k + y, gx, stride=24), :] = one[k * gx : (k + 1) * gx]
    exchange("gx", 8, lambda q: send8.at[pl.ds(pl.multiple_of(24 * q, 8), 24)], lambda q: recv8.at[pl.ds(pl.multiple_of(24 * q, 8), 24)])
    arrived(8, recv8)

    def part(q):
        return recv8.at[pl.ds(pl.multiple_of(24 * (q // 2) + 8 * (q % 2), 8), 8)]

    exchange("gy", 9, part, lambda q: recv9.at[q])
    added = recv8[pl.ds(16, gx, stride=24), :].sum(0, keepdims=True)
    send11[...] = added.reshape(1, 1, 128)
    exchange("gy", 11, lambda q: send11, lambda q: recv11.at[pl.ds(q, 1)])
    arrived(9, recv9)
    wave = dot(tyf[...], recv9[...].reshape(8 * gy, 128))
    wave = wave[:ky] + rot(wave[ky:])
    send10[...] = wave.reshape(ky, 1, 128)
    exchange("gy", 10, lambda q: send10.at[pl.ds(q, 1)], lambda q: recv10.at[pl.ds(q, 1)])

    scale = 1.0 / math.sqrt(8 * gx * 8 * gy * depth)
    arrived(11, recv11)
    added = recv11[...].reshape(gy, 128).sum(0, keepdims=True) * scale
    place = iota((width, 128), 1) - iota((width, 128), 0)
    value = 0.0
    for k in range(2):
        picked = jnp.where(place == k * width, jnp.broadcast_to(added, (width, 128)), 0.0)
        value = value + jnp.sum(picked, axis=1, keepdims=True) * lifted[k : k + 1, :width]
    local_out[...] = value
    pick = iota((128, width), 0) - iota((128, width), 1) == 2 * width
    proj_out[...] = dot(jnp.broadcast_to(added, (8, 128)), jnp.where(pick, 1.0, 0.0))[0:1]

    arrived(10, recv10)
    modes[...] = recv10[...].reshape(gy, 128)
    for x in range(2):
        got = modes[pl.ds(x, pairs, stride=2), :]
        got = jnp.concatenate([got, pltpu.roll(got, 64, 1)], axis=0).T[:64]
        grad = dot(got, outer)
        re, im = grad[:32], grad[32:]
        base = 64 * x
        s_re, s_im = source[base : base + 32, :], source[base + 32 : base + 64, :]
        spectral_out[0, x, 0] = re * s_re + im * s_im
        spectral_out[1, x, 0] = im * s_re - re * s_im

    for copy in copies:
        copy.wait_send()
    for phase_id, whole in (
        (1, recv1.at[1:gx]),
        (2, send2.at[2 : 2 * gy]),
        (3, send3.at[1:gy]),
        (4, send4.at[1:gy]),
        (5, recv4.at[2 : 2 * gx]),
        (6, send6.at[1:gx]),
        (7, send7.at[1:gx]),
        (8, send8.at[24 : 24 * gx]),
        (9, recv9.at[1:gy]),
        (10, send10.at[1:gy]),
        (11, recv11.at[1:gy]),
    ):
        pltpu.make_async_copy(whole, whole, send_sem.at[phase_id]).wait()


def per_device(phase, solute, undercool, lift, weight, local, bias, proj, cotangent):
    gx, gy = lax.axis_size("gx"), lax.axis_size("gy")
    cx, cy, depth = phase.shape
    own_kx, own_ky, kz = weight.shape[1:4]
    width = lift.shape[0]
    square = width * width
    assert width == 2 * gx and gy == 2 * gx and (cx, cy, own_kx, own_ky, kz) == (8, 8, 2, 1, 32)
    consts = tables(gx, gy, cx, cy, depth, gx * own_kx, gy * own_ky, kz)
    group = min(4, gx)
    vmem = pl.BlockSpec(memory_space=pltpu.VMEM)
    buf = lambda *shape: pltpu.VMEM(shape, F32)
    tile = jax.ShapeDtypeStruct((cx, cy, depth), F32)
    outs = (
        tile, tile, tile,
        jax.ShapeDtypeStruct(weight.shape, F32),
        jax.ShapeDtypeStruct((width, width), F32),
        jax.ShapeDtypeStruct((1, width), F32),
    )
    scratch = [
        buf(8, 8, depth), buf(8, 8, depth), buf(8, 8, depth), buf(8, 8, depth), buf(4, 8, depth), buf(5, 8, depth), buf(5, 8, depth),
        buf(12, 24, depth), buf(12, 24, depth), buf(12, 24, depth), buf(10, 24, depth),
        buf(10, 24, depth), buf(10, 24, depth), buf(10, 24, depth),
        buf(4, 64, 128), buf(64, 2 * depth), buf(64, depth), buf(64, depth),
        buf(4 * width, 1, 128), buf(2, square), buf(4, gy, 128), buf(128, square), buf(64 * group, 2 * depth), buf(128, 1, 128),
        buf(16 * gx, 128), buf(gx, 16, 128), buf(2 * gy, 1, 128), buf(2 * gy, 1, 128), buf(gy, 1, 128), buf(gy, 1, 128),
        buf(gy, 8, 128), buf(gy, 8, 128), buf(2 * gx, 8, 128), buf(gx, 8, 8, 128), buf(gx, 8, 8, 128),
        buf(gx, 8, 8, 128), buf(gx, 8, 8, 128), buf(24 * gx, 128), buf(24 * gx, 128), buf(gy, 8, 128),
        buf(gy, 1, 128), buf(gy, 1, 128), buf(1, 1, 128), buf(gy, 1, 128), buf(gy, 128),
        pltpu.SemaphoreType.DMA((12,)), pltpu.SemaphoreType.DMA((12,)),
        pltpu.SemaphoreType.DMA((12,)), pltpu.SemaphoreType.DMA((12,)), pltpu.SemaphoreType.DMA((gx,)),
    ]
    args = [phase, solute, undercool, cotangent, weight.reshape(128, square), lift, local, bias.reshape(1, -1), proj.reshape(1, -1)]
    args += [jnp.asarray(t) for t in consts]
    got = pl.pallas_call(
        lambda *refs: kernel((gx, gy, group), *refs),
        out_shape=outs,
        in_specs=[vmem] * len(args),
        out_specs=(vmem,) * len(outs),
        scratch_shapes=scratch,
        compiler_params=pltpu.CompilerParams(collective_id=0, has_side_effects=True, vmem_limit_bytes=48 * 2**20),
        name="layer",
    )(*args)
    return (*got[:5], got[5].reshape(width))


def solution(mesh):
    tile, modes = P("gx", "gy", None), P(None, "gx", "gy", None, None)
    return jax.shard_map(
        per_device,
        mesh=mesh,
        in_specs=(tile, tile, tile, P(), modes, P(), P(), P(), tile),
        out_specs=(tile, tile, tile, modes, P(), P()),
        check_vma=False,
    )
```

```python
import math

import numpy as np

import jax
import jax.numpy as jnp
from jax import lax
from jax.experimental import pallas as pl
from jax.experimental.pallas import tpu as pltpu
from jax.sharding import PartitionSpec as P

TIME_STEP = 0.05
COUPLING = 2.0
SOLID_DIFF = 0.05
LIQUID_DIFF = 1.0
PARTITION = 0.15
TRAP_RATE = 4.0
SOLUTE_MEAN = 0.5
GELU_K = math.sqrt(2.0 / math.pi)
GELU_C = 0.044715
F32 = jnp.float32
MESH = pl.DeviceIdType.MESH


def signed(count):
    index = np.arange(count)
    return np.where(index < count // 2, index, index - count)


def trig(freqs, places, length, factor=1.0):
    angle = 2.0 * np.pi * ((freqs[:, None] * places[None, :]) % length) / length
    return np.cos(angle) * factor, np.sin(angle) * factor


def z_tables(modes, depth):
    cos, sin = trig(np.arange(modes), np.arange(depth), depth)
    lanes = 2 * modes
    weight = np.where(np.arange(modes) == 0, 1.0, 2.0) / depth
    both = np.stack([cos, -sin])

    def blocks(one):
        full = np.zeros((2 * depth, 2 * lanes))
        full[:depth, :lanes] = one
        full[depth:, lanes:] = one
        return full

    plain = both.reshape(lanes, depth).T
    heavy = (both * weight[None, :, None]).reshape(lanes, depth).T
    return blocks(plain), blocks(heavy), blocks(heavy).T


def tables(gx, gy, cx, cy, depth, kx, ky, kz):
    nx, ny = gx * cx, gy * cy
    own = kx // gx
    zf, zg, zi = z_tables(kz, depth)
    cosx, sinx = trig(signed(kx), np.arange(nx), nx)
    cosy, siny = trig(signed(ky), np.arange(ny), ny)
    tx = np.concatenate([cosx, sinx]).reshape(2 * kx, gx, cx).transpose(1, 2, 0)
    ty = np.zeros((gy, own, cy, 2, ky, own))
    both = np.stack([cosy, siny]).reshape(2, ky, gy, cy).transpose(2, 3, 0, 1)
    for k in range(own):
        ty[:, k, :, :, :, k] = both
    ty = ty.reshape(gy, own * cy, 2 * ky * own)
    tyi = np.concatenate([cosy, -siny]).T / ny
    txi = np.concatenate([cosx, -sinx]).T / nx
    txf = np.stack([cosx, sinx]).reshape(2, gx, own, nx).transpose(0, 2, 1, 3).reshape(2 * kx, nx) / nx
    tyf = np.concatenate([cosy, siny]) / ny
    right = [in_three(t, 0) for t in (zf, zg, zi)]
    left = [in_three(t, 1) for t in (tyi, txi, txf, tyf)]
    return right + [np.asarray(tx, np.float32), np.asarray(ty, np.float32)] + left


def in_three(table, axis):
    table = np.asarray(table, np.float32)
    high = table.astype(jnp.bfloat16)
    low = (table - high.astype(np.float32)).astype(jnp.bfloat16)
    return np.concatenate([high, low, high], axis=axis)


def parts(v, axis, order):
    high = v.astype(jnp.bfloat16)
    low = (v - high.astype(F32)).astype(jnp.bfloat16)
    return jnp.concatenate([(high, low)[k] for k in order], axis=axis)


def dot_right(v, table):
    return jnp.dot(parts(v, 1, (0, 0, 1)), table, preferred_element_type=F32)


def dot_left(table, v):
    return jnp.dot(table, parts(v, 0, (0, 0, 1)), preferred_element_type=F32)


def dot_pick(v, pick):
    high = v.astype(jnp.bfloat16)
    low = (v - high.astype(F32)).astype(jnp.bfloat16)
    pick = pick.astype(jnp.bfloat16)
    return jnp.dot(high, pick, preferred_element_type=F32) + jnp.dot(low, pick, preferred_element_type=F32)


def dot(a, b, dims=((1,), (0,))):
    return lax.dot_general(a, b, (dims, ((), ())), precision=lax.Precision.HIGHEST, preferred_element_type=F32)


def iota(shape, dim):
    return lax.broadcasted_iota(jnp.int32, shape, dim)


def rot(v):
    imag = (iota(v.shape, 1) // 32) % 2 == 1
    return jnp.where(imag, -pltpu.roll(v, 32, 1), pltpu.roll(v, 96, 1))


def diffusivity(p):
    return SOLID_DIFF + (LIQUID_DIFF - SOLID_DIFF) * 0.5 * (1.0 - jnp.tanh(p))


def around(ref, x):
    centre = ref[x]
    rows, depth = centre.shape
    return centre, [
        ref[x + 1],
        ref[x - 1],
        pltpu.roll(centre, rows - 1, 0),
        pltpu.roll(centre, 1, 0),
        pltpu.roll(centre, depth - 1, 1),
        pltpu.roll(centre, 1, 1),
    ]


def advance(p_ref, c_ref, d_ref, undercool, x):
    p, p_nb = around(p_ref, x)
    c, c_nb = around(c_ref, x)
    d, d_nb = around(d_ref, x)
    total = p_nb[0]
    for one in p_nb[1:]:
        total = total + one
    squares = 1.0 - p * p
    rate = total - 6.0 * p + p - p * p * p + COUPLING * squares * squares * (undercool - c)
    div = 0.0
    for dn, cn in zip(d_nb, c_nb):
        div = div + 0.5 * (d + dn) * (cn - c)
    speed = TRAP_RATE * jnp.abs(rate)
    keff = (PARTITION + speed) / (1.0 + speed)
    return p + TIME_STEP * rate, c + TIME_STEP * (div + 0.5 * (1.0 - keff) * c * rate)


def kernel(
    dims, ready, phase, solute, undercool, cotangent, weight, lift, local, bias, proj,
    zf, zg, zi, tx, ty, tyi, txi, txf, tyf,
    phase_far, solute_far, predicted_far, modes_far, spec_far, added_far,
    phase_out, solute_out, predicted_out, spec_out, added_out, out_sem,
    yhi, ylo, from_ylo, from_yhi, from_corner, from_xlo, from_xhi,
    pad_p, pad_c, pad_d, pad_u, mid_p, mid_c, mid_d, flat, cells, cot, total, coef, lifted, blend, field, sums,
    send1, recv1, send2, recv2, send3, recv3, send4, recv4, recv5, send6, recv6, send7, recv7,
    send8, recv8, recv9, send10, recv10, send11, recv11,
    halo_send, halo_recv, send_sem, recv_sem, recv6_sem,
):
    gx, gy, group = dims
    ix, iy = lax.axis_index("gx"), lax.axis_index("gy")
    east, west = lax.rem(ix + 1, gx), lax.rem(ix + gx - 1, gx)
    north, south = lax.rem(iy + 1, gy), lax.rem(iy + gy - 1, gy)
    width = lift.shape[1]
    pairs = width // 2
    kx, ky = 2 * gx, gy
    square = width * width
    barrier = pltpu.get_barrier_semaphore()

    def greet(axis, mine, count):
        def one(j, carry):
            pl.semaphore_signal(barrier, inc=1, device_id={axis: lax.rem(mine + j, count)}, device_id_type=MESH)
            return carry

        lax.fori_loop(1, count, one, 0)

    for a in (east, west):
        for b in (north, south):
            pl.semaphore_signal(barrier, inc=1, device_id={"gx": a, "gy": b}, device_id_type=MESH)
    greet("gx", ix, gx)
    greet("gy", iy, gy)

    ready(0, 1, 2)
    row = iota((8, 8, phase.shape[2]), 1)
    p, c, u = phase[...], solute[...], undercool[...]
    yhi[...] = jnp.where(row >= 6, p, jnp.where(row >= 4, pltpu.roll(c, 6, 1), pltpu.roll(u, 4, 1)))
    ylo[...] = jnp.where(row < 2, p, jnp.where(row < 4, pltpu.roll(c, 2, 1), pltpu.roll(u, 4, 1)))
    pad_p[2:10, 8:16, :] = p
    pad_c[2:10, 8:16, :] = c
    pad_u[1:9, 8:16, :] = u

    depth = phase.shape[2]
    src, dst = iota((128, 128), 0), iota((128, 128), 1)
    outer = jnp.where(iota((width, square), 1) // width == iota((width, square), 0), 1.0, 0.0)

    def factors_of_channels():
        ready(5, 6, 7, 8, 3)
        inner = iota((width, square), 1) % width == iota((width, square), 0)
        eye = iota((width, width), 0) == iota((width, width), 1)

        def column(v):
            return jnp.sum(jnp.where(eye, jnp.broadcast_to(v, (width, width)), 0.0), axis=1, keepdims=True)

        for k in range(2):
            one = column(lift[k : k + 1, :])
            lifted[k : k + 1, :] = jnp.sum(jnp.where(inner, one, 0.0), axis=0, keepdims=True)
            mixed = jnp.sum(local[...] * lift[k : k + 1, :], axis=1, keepdims=True)
            coef[k * width : (k + 1) * width] = jnp.broadcast_to(mixed, (width, 128)).reshape(width, 1, 128)
        for k, vector in ((2, bias), (3, proj)):
            one = column(vector[...])
            coef[k * width : (k + 1) * width] = jnp.broadcast_to(one, (width, 128)).reshape(width, 1, 128)
        sums[...] = jnp.zeros_like(sums)
        total[...] = jnp.zeros_like(total)
        for x in range(8):
            for h in range(2):
                flat[h, 8 * x : 8 * x + 8, :] = cotangent[x, :, 128 * h : 128 * h + 128]
        for y in range(8):
            for h in range(2):
                cot[8 * y : 8 * y + 8, 128 * h : 128 * h + 128] = flat[h, pl.ds(y, 8, stride=8), :]

    def weights_of_fields():
        ready(4)
        fold = jnp.where(iota((square, width), 0) // width == iota((square, width), 1), 1.0, 0.0)
        for k in range(2):
            both = dot_pick(weight[...] * lifted[k : k + 1, :], fold)
            both = jnp.concatenate([both, jnp.zeros((128, 128 - width), F32)], axis=1).T
            for part in range(2):
                for x in range(2):
                    value = 0.0
                    for par in range(2):
                        pick = (src % 32 == dst % 32) & (src // 32 == part * 2 + x) & (dst // 64 == par)
                        value = value + dot_pick(both[par * pairs : (par + 1) * pairs], jnp.where(pick, 1.0, 0.0))
                    blend[2 * k + part, pl.ds(x, pairs, stride=2), :] = value

    factors_of_channels()
    pl.semaphore_wait(barrier, 4 + gx - 1 + gy - 1)

    def push(source_ref, target_ref, slot, where):
        copy = pltpu.make_async_remote_copy(
            src_ref=source_ref,
            dst_ref=target_ref,
            send_sem=halo_send.at[slot],
            recv_sem=halo_recv.at[slot],
            device_id=where,
            device_id_type=MESH,
        )
        copy.start()
        return copy

    copies = [
        push(yhi, from_ylo, 0, {"gy": north}),
        push(ylo, from_yhi, 1, {"gy": south}),
        push(yhi.at[7], from_corner.at[0], 2, {"gx": east, "gy": north}),
        push(yhi.at[0], from_corner.at[1], 3, {"gx": west, "gy": north}),
        push(ylo.at[7], from_corner.at[2], 4, {"gx": east, "gy": south}),
        push(ylo.at[0], from_corner.at[3], 5, {"gx": west, "gy": south}),
        push(phase.at[6:8], from_xlo.at[0:2], 6, {"gx": east}),
        push(solute.at[6:8], from_xlo.at[2:4], 7, {"gx": east}),
        push(undercool.at[7:8], from_xlo.at[4:5], 8, {"gx": east}),
        push(phase.at[0:2], from_xhi.at[0:2], 9, {"gx": west}),
        push(solute.at[0:2], from_xhi.at[2:4], 10, {"gx": west}),
        push(undercool.at[0:1], from_xhi.at[4:5], 11, {"gx": west}),
    ]
    for copy in copies:
        copy.wait_recv()

    def lay(rows, low, planes):
        at = slice(0, 8) if low else slice(16, 24)
        turn = 1 if low else -1
        pad_p[planes, at, :] = rows
        pad_c[planes, at, :] = pltpu.roll(rows, (2 * turn) % 8, 1)
        pad_u[slice(planes.start - 1, planes.stop - 1), at, :] = pltpu.roll(rows, 4, 1)

    lay(from_ylo[...], True, slice(2, 10))
    lay(from_yhi[...], False, slice(2, 10))
    lay(from_corner[0:1], True, slice(1, 2))
    lay(from_corner[1:2], True, slice(10, 11))
    lay(from_corner[2:3], False, slice(1, 2))
    lay(from_corner[3:4], False, slice(10, 11))
    pad_p[0:2, 8:16, :] = from_xlo[0:2]
    pad_c[0:2, 8:16, :] = from_xlo[2:4]
    pad_u[0:1, 8:16, :] = from_xlo[4:5]
    pad_p[10:12, 8:16, :] = from_xhi[0:2]
    pad_c[10:12, 8:16, :] = from_xhi[2:4]
    pad_u[9:10, 8:16, :] = from_xhi[4:5]

    def first_diff(x, carry):
        pad_d[x] = diffusivity(pad_p[x])
        return carry

    def first(x, carry):
        new_p, new_c = advance(pad_p, pad_c, pad_d, pad_u[x], x + 1)
        mid_p[x] = new_p
        mid_c[x] = new_c
        mid_d[x] = diffusivity(new_p)
        return carry

    def second(x, carry):
        new_p, new_c = advance(mid_p, mid_c, mid_d, pad_u[x + 1], x + 1)
        new_p, new_c = new_p[8:16], new_c[8:16]
        phase_out[x] = new_p
        solute_out[x] = new_c
        at = pl.multiple_of(8 * x, 8)
        for h in range(2):
            flat[h, pl.ds(at, 8), :] = new_p[:, 128 * h : 128 * h + 128]
            flat[2 + h, pl.ds(at, 8), :] = new_c[:, 128 * h : 128 * h + 128] - SOLUTE_MEAN
        return carry

    lax.fori_loop(0, 12, first_diff, 0)
    lax.fori_loop(0, 10, first, 0)
    lax.fori_loop(0, 8, second, 0)
    writes = [pltpu.make_async_copy(phase_out, phase_far, out_sem.at[0]), pltpu.make_async_copy(solute_out, solute_far, out_sem.at[1])]
    for one in writes:
        one.start()
    for y in range(8):
        for h in range(4):
            cells[8 * y : 8 * y + 8, 128 * h : 128 * h + 128] = flat[h, pl.ds(y, 8, stride=8), :]

    def exchange(axis, phase_id, sends, receives):
        mine, count = (ix, gx) if axis == "gx" else (iy, gy)
        pltpu.make_async_copy(sends(mine), receives(mine), recv_sem.at[phase_id]).start()

        def one(j, carry):
            peer = lax.rem(mine + j, count)
            pltpu.make_async_remote_copy(
                src_ref=sends(peer),
                dst_ref=receives(mine),
                send_sem=send_sem.at[phase_id],
                recv_sem=recv_sem.at[phase_id],
                device_id={axis: peer},
                device_id_type=MESH,
            ).start()
            return carry

        lax.fori_loop(1, count, one, 0)

    def arrived(phase_id, whole):
        pltpu.make_async_copy(whole, whole, recv_sem.at[phase_id]).wait()

    ready(9, 12, 13)
    along = dot_right(cells[...], zf[...])
    lines = jnp.concatenate([along[8 * y : 8 * y + 8] for y in range(8)], axis=1)
    wave = dot(tx[ix].T, lines)
    for y in range(8):
        at = slice(128 * y, 128 * y + 128)
        send1[pl.ds(y, kx, stride=8), :] = wave[:kx, at] + rot(wave[kx:, at])
    exchange("gx", 1, lambda q: send1.at[pl.ds(pl.multiple_of(16 * q, 16), 16)], lambda q: recv1.at[q])
    weights_of_fields()
    arrived(1, recv1)
    got = recv1[0]
    for q in range(1, gx):
        got = got + recv1[q]
    wave = dot(ty[iy].T, got)
    wave = wave[: 2 * ky] + rot(wave[2 * ky :])
    send2[...] = wave.reshape(2 * ky, 1, 128)
    exchange("gy", 2, lambda q: send2.at[pl.ds(2 * q, 2)], lambda q: recv2.at[pl.ds(2 * q, 2)])
    arrived(2, recv2)
    got = recv2[...].reshape(gy, 2, 128).sum(0)
    spec_out[...] = got

    even = iota((gy, 128), 0) % 2 == 0
    spread = jnp.where(even, jnp.broadcast_to(got[0:1], (gy, 128)), jnp.broadcast_to(got[1:2], (gy, 128)))
    turned = pltpu.roll(spread, 64, 1)
    low = iota((gy, 128), 1) < 64
    value = 0.0
    for k in range(2):
        one = jnp.where(low, spread, turned) if k == 0 else jnp.where(low, turned, spread)
        value = value + blend[2 * k] * one - blend[2 * k + 1] * rot(one)
    send3[...] = value.reshape(gy, 1, 128)
    exchange("gy", 3, lambda q: send3.at[pl.ds(q, 1)], lambda q: recv3.at[pl.ds(q, 1)])

    arrived(3, recv3)
    got = recv3[...].reshape(ky, 128)
    ready(14, 15, 16, 17, 10, 11)
    send4[...] = dot_left(tyi[...], jnp.concatenate([got, rot(got)], axis=0)).reshape(gy, 8, 128)
    exchange("gy", 4, lambda q: send4.at[q], lambda q: recv4.at[q])
    arrived(4, recv4)
    exchange("gx", 5, lambda q: recv4.at[pl.ds(2 * q, 2)], lambda q: recv5.at[pl.ds(2 * q, 2)])
    arrived(5, recv5)
    lines = []
    for y in range(8):
        got = recv5[:, y, :]
        lines.append(jnp.concatenate([got, rot(got)], axis=0))
    wave = dot_left(txi[...], jnp.concatenate(lines, axis=1))
    for y in range(8):
        send6[:, y] = wave[:, 128 * y : 128 * y + 128].reshape(gx, 8, 128)

    pltpu.make_async_copy(send6.at[ix], recv6.at[ix], recv6_sem.at[ix]).start()

    def give(j, carry):
        peer = lax.rem(ix + j, gx)
        pltpu.make_async_remote_copy(
            src_ref=send6.at[peer],
            dst_ref=recv6.at[ix],
            send_sem=send_sem.at[6],
            recv_sem=recv6_sem.at[ix],
            device_id={"gx": peer},
            device_id_type=MESH,
        ).start()
        return carry

    lax.fori_loop(1, gx, give, 0)

    def wide(o):
        one = coef[o]
        return jnp.concatenate([one, one], axis=1)

    def step(j, carry):
        owners = [lax.rem(ix + gx - (j * group + t), gx) for t in range(group)]
        for owner in owners:
            pltpu.make_async_copy(recv6.at[owner], recv6.at[owner], recv6_sem.at[owner]).wait()
        got = jnp.concatenate([recv6[owner].reshape(64, 128) for owner in owners], axis=0)
        field[...] = dot_right(got, zi[...])
        for t, owner in enumerate(owners):
            factors = [[wide(k * width + par * pairs + owner) for k in range(4)] for par in range(2)]

            def block(r, acc):
                at = pl.multiple_of(8 * r, 8)
                here = pl.ds(pl.multiple_of(64 * t + 8 * r, 8), 8)
                p, c, w = cells[pl.ds(at, 8), :depth], cells[pl.ds(at, 8), depth:], cot[pl.ds(at, 8), :]
                acc = list(acc)
                out = total[pl.ds(at, 8), :]
                for par in range(2):
                    m0, m1, b, q = factors[par]
                    side = slice(par * depth, (par + 1) * depth)
                    pre = field[here, side] + m0 * p + m1 * c + b
                    power = pre * pre
                    tanh = jnp.tanh(GELU_K * (pre + GELU_C * (power * pre)))
                    half = 0.5 * (1.0 + tanh)
                    act = pre * half
                    slope = half + (0.5 * GELU_K) * pre * (1.0 - tanh * tanh) * (1.0 + (3.0 * GELU_C) * power)
                    out = out + q * act
                    grad = q * w * slope
                    field[here, side] = grad
                    acc[3 * par] = acc[3 * par] + grad * p
                    acc[3 * par + 1] = acc[3 * par + 1] + grad * c
                    acc[3 * par + 2] = acc[3 * par + 2] + act * w
                total[pl.ds(at, 8), :] = out
                return tuple(acc)

            zero = jnp.zeros((8, depth), F32)
            acc = lax.fori_loop(0, 8, block, (zero,) * 6)
            for par in range(2):
                for k in range(3):
                    one = jnp.sum(acc[3 * par + k], axis=0, keepdims=True)
                    sums[k * width + par * pairs + owner] = one[:, :128] + one[:, 128:]
        wave = dot_right(field[...], zg[...])
        for t, owner in enumerate(owners):
            send7[owner] = wave[64 * t : 64 * t + 64].reshape(8, 8, 128)

            @pl.when(owner == ix)
            def _():
                pltpu.make_async_copy(send7.at[owner], recv7.at[ix], recv_sem.at[7]).start()

            @pl.when(owner != ix)
            def _():
                pltpu.make_async_remote_copy(
                    src_ref=send7.at[owner],
                    dst_ref=recv7.at[ix],
                    send_sem=send_sem.at[7],
                    recv_sem=recv_sem.at[7],
                    device_id={"gx": owner},
                    device_id_type=MESH,
                ).start()

        return carry

    lax.fori_loop(0, gx // group, step, 0)
    for h in range(2):
        flat[h] = total[:, 128 * h : 128 * h + 128]
    for x in range(8):
        for h in range(2):
            predicted_out[x, :, 128 * h : 128 * h + 128] = flat[h, pl.ds(x, 8, stride=8), :]
    writes.append(pltpu.make_async_copy(predicted_out, predicted_far, out_sem.at[2]))
    added = dot(jnp.ones((8, 128), F32), sums[...].reshape(128, 128), ((1,), (1,)))
    for q in range(gx):
        send8[24 * q + 16 : 24 * q + 24, :] = added

    writes.append(pltpu.make_async_copy(spec_out, spec_far, out_sem.at[3]))
    for one in writes[2:]:
        one.start()

    arrived(7, recv7)
    lines = [recv7[:, y].reshape(8 * gx, 128) for y in range(8)]
    wave = dot_left(txf[...], jnp.concatenate(lines, axis=1))
    for y in range(8):
        at = slice(128 * y, 128 * y + 128)
        one = wave[:kx, at] + rot(wave[kx:, at])
        for k in range(2):
            send8[pl.ds(8 * k + y, gx, stride=24), :] = one[k * gx : (k + 1) * gx]
    exchange("gx", 8, lambda q: send8.at[pl.ds(pl.multiple_of(24 * q, 8), 24)], lambda q: recv8.at[pl.ds(pl.multiple_of(24 * q, 8), 24)])
    arrived(8, recv8)

    def part(q):
        return recv8.at[pl.ds(pl.multiple_of(24 * (q // 2) + 8 * (q % 2), 8), 8)]

    exchange("gy", 9, part, lambda q: recv9.at[q])
    added = recv8[pl.ds(16, gx, stride=24), :].sum(0, keepdims=True)
    send11[...] = added.reshape(1, 1, 128)
    exchange("gy", 11, lambda q: send11, lambda q: recv11.at[pl.ds(q, 1)])
    arrived(9, recv9)
    wave = dot_left(tyf[...], recv9[...].reshape(8 * gy, 128))
    wave = wave[:ky] + rot(wave[ky:])
    send10[...] = wave.reshape(ky, 1, 128)
    exchange("gy", 10, lambda q: send10.at[pl.ds(q, 1)], lambda q: recv10.at[pl.ds(q, 1)])

    arrived(11, recv11)
    added_out[...] = recv11[...].reshape(gy, 128).sum(0, keepdims=True)
    writes.append(pltpu.make_async_copy(added_out, added_far, out_sem.at[4]))
    writes[4].start()
    arrived(10, recv10)
    writes.append(pltpu.make_async_copy(recv10, modes_far, out_sem.at[5]))
    writes[5].start()
    for one in writes:
        one.wait()

    for copy in copies:
        copy.wait_send()
    for phase_id, whole in (
        (1, recv1.at[1:gx]),
        (2, send2.at[2 : 2 * gy]),
        (3, send3.at[1:gy]),
        (4, send4.at[1:gy]),
        (5, recv4.at[2 : 2 * gx]),
        (6, send6.at[1:gx]),
        (7, send7.at[1:gx]),
        (8, send8.at[24 : 24 * gx]),
        (9, recv9.at[1:gy]),
        (10, send10.at[1:gy]),
        (11, recv11.at[1:gy]),
    ):
        pltpu.make_async_copy(whole, whole, send_sem.at[phase_id]).wait()


def finish(
    scale, phase_in, solute_in, predicted_in, modes_in, spec_in, added_in, lift_in,
    phase_far, solute_far, predicted_far, spectral_far, local_far, proj_far,
    phase, solute, predicted, modes, spec, added, lift, spectral, local, proj, flat, in_sem, out_sem,
):
    far_in = (phase_in, solute_in, predicted_in, modes_in, spec_in, added_in, lift_in)
    near = (phase, solute, predicted, modes, spec, added, lift)
    reads = [pltpu.make_async_copy(a, b, in_sem.at[k]) for k, (a, b) in enumerate(zip(far_in, near))]
    far_out = (phase_far, solute_far, predicted_far, spectral_far, local_far, proj_far)
    made = (phase, solute, predicted, spectral, local, proj)
    writes = [pltpu.make_async_copy(a, b, out_sem.at[k]) for k, (a, b) in enumerate(zip(made, far_out))]
    for k in (6, 4, 3, 5, 0, 1, 2):
        reads[k].start()
    width = lift.shape[1]
    pairs, square = width // 2, width * width
    outer = jnp.where(iota((width, square), 1) // width == iota((width, square), 0), 1.0, 0.0)
    inner = iota((width, square), 1) % width == iota((width, square), 0)
    eye = iota((width, width), 0) == iota((width, width), 1)
    src, dst = iota((128, 128), 0), iota((128, 128), 1)
    reads[6].wait()
    lifted = []
    for k in range(2):
        one = jnp.sum(jnp.where(eye, jnp.broadcast_to(lift[k : k + 1, :], (width, width)), 0.0), axis=1, keepdims=True)
        lifted.append(jnp.sum(jnp.where(inner, one, 0.0), axis=0, keepdims=True))
    reads[4].wait()
    reads[3].wait()
    flat[...] = modes[...].reshape(2 * pairs, 128)
    for x in range(2):
        diagonal = jnp.where(src == dst, jnp.broadcast_to(spec[x : x + 1, :], (128, 128)), 0.0)
        column = jnp.sum(diagonal, axis=1, keepdims=True)
        source = column[:64] * lifted[0] + column[64:] * lifted[1]
        got = flat[pl.ds(x, pairs, stride=2), :]
        got = jnp.concatenate([got, pltpu.roll(got, 64, 1)], axis=0).T[:64]
        grad = dot_pick(got, outer)
        re, im = grad[:32], grad[32:]
        s_re, s_im = source[:32], source[32:]
        spectral[0, x, 0] = re * s_re + im * s_im
        spectral[1, x, 0] = im * s_re - re * s_im
    writes[3].start()
    for k in range(3):
        reads[k].wait()
        writes[k].start()
    reads[5].wait()
    scaled = added[...] * scale
    place = iota((width, 128), 1) - iota((width, 128), 0)
    value = 0.0
    for k in range(2):
        picked = jnp.where(place == k * width, jnp.broadcast_to(scaled, (width, 128)), 0.0)
        value = value + jnp.sum(picked, axis=1, keepdims=True) * lift[k : k + 1, :]
    local[...] = value
    pick = iota((128, width), 0) - iota((128, width), 1) == 2 * width
    column = jnp.sum(jnp.where(src == dst, jnp.broadcast_to(scaled, (128, 128)), 0.0), axis=1, keepdims=True)
    proj[...] = jnp.sum(jnp.where(pick, column, 0.0), axis=0, keepdims=True)
    writes[4].start()
    writes[5].start()
    for one in writes:
        one.wait()


def per_device(phase, solute, undercool, lift, weight, local, bias, proj, cotangent):
    gx, gy = lax.axis_size("gx"), lax.axis_size("gy")
    cx, cy, depth = phase.shape
    own_kx, own_ky, kz = weight.shape[1:4]
    width = lift.shape[0]
    square = width * width
    assert width == 2 * gx and gy == 2 * gx and (cx, cy, own_kx, own_ky, kz) == (8, 8, 2, 1, 32)
    consts = tables(gx, gy, cx, cy, depth, gx * own_kx, gy * own_ky, kz)
    group = min(4, gx)
    far_spec = pl.BlockSpec(memory_space=pl.ANY)
    buf = lambda *shape: pltpu.VMEM(shape, F32)
    tile = jax.ShapeDtypeStruct((cx, cy, depth), F32)
    shape = lambda *dims: jax.ShapeDtypeStruct(dims, F32)
    outs = (tile, tile, tile, shape(gy, 1, 128), shape(2, 128), shape(1, 128))
    scratch = [
        buf(8, 8, depth), buf(8, 8, depth), buf(8, 8, depth), buf(2, 128), buf(1, 128), pltpu.SemaphoreType.DMA((6,)),
        buf(8, 8, depth), buf(8, 8, depth), buf(8, 8, depth), buf(8, 8, depth), buf(4, 8, depth), buf(5, 8, depth), buf(5, 8, depth),
        buf(12, 24, depth), buf(12, 24, depth), buf(12, 24, depth), buf(10, 24, depth),
        buf(10, 24, depth), buf(10, 24, depth), buf(10, 24, depth),
        buf(4, 64, 128), buf(64, 2 * depth), buf(64, depth), buf(64, depth),
        buf(4 * width, 1, 128), buf(2, square), buf(4, gy, 128), buf(64 * group, 2 * depth), buf(128, 1, 128),
        buf(16 * gx, 128), buf(gx, 16, 128), buf(2 * gy, 1, 128), buf(2 * gy, 1, 128), buf(gy, 1, 128), buf(gy, 1, 128),
        buf(gy, 8, 128), buf(gy, 8, 128), buf(2 * gx, 8, 128), buf(gx, 8, 8, 128), buf(gx, 8, 8, 128),
        buf(gx, 8, 8, 128), buf(gx, 8, 8, 128), buf(24 * gx, 128), buf(24 * gx, 128), buf(gy, 8, 128),
        buf(gy, 1, 128), buf(gy, 1, 128), buf(1, 1, 128), buf(gy, 1, 128),
        pltpu.SemaphoreType.DMA((12,)), pltpu.SemaphoreType.DMA((12,)),
        pltpu.SemaphoreType.DMA((12,)), pltpu.SemaphoreType.DMA((12,)), pltpu.SemaphoreType.DMA((gx,)),
    ]
    args = [phase, solute, undercool, cotangent, weight.reshape(128, square), lift.T, local, bias.reshape(1, -1), proj.reshape(1, -1)]
    args += [jnp.asarray(t) for t in consts]
    scratch += [pltpu.VMEM(one.shape, one.dtype) for one in args] + [pltpu.SemaphoreType.DMA((len(args),))]
    count = len(args)

    def body(*refs):
        far, rest, near, sems = refs[:count], refs[count : -count - 1], refs[-count - 1 : -1], refs[-1]
        loads = [pltpu.make_async_copy(far[k], near[k], sems.at[k]) for k in range(count)]
        for k in (0, 1, 2, 5, 6, 7, 8, 3, 4, 9, 12, 13, 14, 15, 11, 10, 16, 17):
            loads[k].start()

        def ready(*which):
            for k in which:
                loads[k].wait()

        kernel((gx, gy, group), ready, *near, *rest)

    got = pl.pallas_call(
        body,
        out_shape=outs,
        in_specs=[far_spec] * count,
        out_specs=(far_spec,) * len(outs),
        scratch_shapes=scratch,
        compiler_params=pltpu.CompilerParams(collective_id=0, has_side_effects=True, vmem_limit_bytes=60 * 2**20),
        name="layer",
    )(*args)
    scale = 1.0 / math.sqrt(8 * gx * 8 * gy * depth)
    finals = (tile, tile, tile, shape(*weight.shape), shape(width, width), shape(1, width))
    got = pl.pallas_call(
        lambda *refs: finish(scale, *refs),
        out_shape=finals,
        in_specs=[far_spec] * 7,
        out_specs=(far_spec,) * 6,
        scratch_shapes=[
            buf(8, 8, depth), buf(8, 8, depth), buf(8, 8, depth), buf(gy, 1, 128), buf(2, 128), buf(1, 128), buf(2, width),
            buf(*weight.shape), buf(width, width), buf(1, width), buf(gy, 128),
            pltpu.SemaphoreType.DMA((7,)), pltpu.SemaphoreType.DMA((6,)),
        ],
        compiler_params=pltpu.CompilerParams(vmem_limit_bytes=60 * 2**20),
        name="finish",
    )(*got, lift.T)
    return (*got[:5], got[5].reshape(width))


def solution(mesh):
    tile, modes = P("gx", "gy", None), P(None, "gx", "gy", None, None)
    return jax.shard_map(
        per_device,
        mesh=mesh,
        in_specs=(tile, tile, tile, P(), modes, P(), P(), P(), tile),
        out_specs=(tile, tile, tile, modes, P(), P()),
        check_vma=False,
    )
```

```python
import math

import numpy as np

import jax
import jax.numpy as jnp
from jax import lax
from jax.experimental import pallas as pl
from jax.experimental.pallas import tpu as pltpu
from jax.sharding import PartitionSpec as P

TIME_STEP = 0.05
COUPLING = 2.0
SOLID_DIFF = 0.05
LIQUID_DIFF = 1.0
PARTITION = 0.15
TRAP_RATE = 4.0
SOLUTE_MEAN = 0.5
GELU_K = math.sqrt(2.0 / math.pi)
GELU_C = 0.044715
F32 = jnp.float32
MESH = pl.DeviceIdType.MESH


def signed(count):
    index = np.arange(count)
    return np.where(index < count // 2, index, index - count)


def trig(freqs, places, length, factor=1.0):
    angle = 2.0 * np.pi * ((freqs[:, None] * places[None, :]) % length) / length
    return np.cos(angle) * factor, np.sin(angle) * factor


def z_tables(modes, depth):
    cos, sin = trig(np.arange(modes), np.arange(depth), depth)
    lanes = 2 * modes
    weight = np.where(np.arange(modes) == 0, 1.0, 2.0) / depth
    both = np.stack([cos, -sin])

    def blocks(one):
        full = np.zeros((2 * depth, 2 * lanes))
        full[:depth, :lanes] = one
        full[depth:, lanes:] = one
        return full

    plain = both.reshape(lanes, depth).T
    heavy = (both * weight[None, :, None]).reshape(lanes, depth).T
    return blocks(plain), blocks(heavy), blocks(heavy).T


def tables(gx, gy, cx, cy, depth, kx, ky, kz):
    nx, ny = gx * cx, gy * cy
    own = kx // gx
    zf, zg, zi = z_tables(kz, depth)
    cosx, sinx = trig(signed(kx), np.arange(nx), nx)
    cosy, siny = trig(signed(ky), np.arange(ny), ny)
    tx = np.concatenate([cosx, sinx]).reshape(2 * kx, gx, cx).transpose(1, 2, 0)
    ty = np.zeros((gy, own, cy, 2, ky, own))
    both = np.stack([cosy, siny]).reshape(2, ky, gy, cy).transpose(2, 3, 0, 1)
    for k in range(own):
        ty[:, k, :, :, :, k] = both
    ty = ty.reshape(gy, own * cy, 2 * ky * own)
    team = 4 * cy
    tyi = (np.concatenate([cosy, -siny]).T / ny).reshape(ny // team, team, 2 * ky)
    txi = np.concatenate([cosx, -sinx]).T / nx
    txf = np.stack([cosx, sinx]).reshape(2, gx, own, nx).transpose(0, 2, 1, 3).reshape(2 * kx, nx) / nx
    tyf = (np.concatenate([cosy, siny]) / ny).reshape(2 * ky, ny // team, team).transpose(1, 0, 2)
    right = [in_three(t, 0) for t in (zf, zg, zi)]
    left = [in_three(t, t.ndim - 1) for t in (tyi, txi, txf, tyf)]
    return right + [np.asarray(tx, np.float32), np.asarray(ty, np.float32)] + left


def in_three(table, axis):
    table = np.asarray(table, np.float32)
    high = table.astype(jnp.bfloat16)
    low = (table - high.astype(np.float32)).astype(jnp.bfloat16)
    return np.concatenate([high, low, high], axis=axis)


def parts(v, axis, order):
    high = v.astype(jnp.bfloat16)
    low = (v - high.astype(F32)).astype(jnp.bfloat16)
    return jnp.concatenate([(high, low)[k] for k in order], axis=axis)


def dot_right(v, table):
    return jnp.dot(parts(v, 1, (0, 0, 1)), table, preferred_element_type=F32)


def dot_left(table, v):
    return jnp.dot(table, parts(v, 0, (0, 0, 1)), preferred_element_type=F32)


def dot_pick(v, pick):
    high = v.astype(jnp.bfloat16)
    low = (v - high.astype(F32)).astype(jnp.bfloat16)
    pick = pick.astype(jnp.bfloat16)
    return jnp.dot(high, pick, preferred_element_type=F32) + jnp.dot(low, pick, preferred_element_type=F32)


def dot(a, b, dims=((1,), (0,))):
    return lax.dot_general(a, b, (dims, ((), ())), precision=lax.Precision.HIGHEST, preferred_element_type=F32)


def iota(shape, dim):
    return lax.broadcasted_iota(jnp.int32, shape, dim)


def rot(v):
    imag = (iota(v.shape, 1) // 32) % 2 == 1
    return jnp.where(imag, -pltpu.roll(v, 32, 1), pltpu.roll(v, 96, 1))


def diffusivity(p):
    return SOLID_DIFF + (LIQUID_DIFF - SOLID_DIFF) * 0.5 * (1.0 - jnp.tanh(p))


def around(ref, x):
    centre = ref[x]
    rows, depth = centre.shape
    return centre, [
        ref[x + 1],
        ref[x - 1],
        pltpu.roll(centre, rows - 1, 0),
        pltpu.roll(centre, 1, 0),
        pltpu.roll(centre, depth - 1, 1),
        pltpu.roll(centre, 1, 1),
    ]


def advance(p_ref, c_ref, d_ref, undercool, x):
    p, p_nb = around(p_ref, x)
    c, c_nb = around(c_ref, x)
    d, d_nb = around(d_ref, x)
    total = p_nb[0]
    for one in p_nb[1:]:
        total = total + one
    squares = 1.0 - p * p
    rate = total - 6.0 * p + p - p * p * p + COUPLING * squares * squares * (undercool - c)
    div = 0.0
    for dn, cn in zip(d_nb, c_nb):
        div = div + 0.5 * (d + dn) * (cn - c)
    speed = TRAP_RATE * jnp.abs(rate)
    keff = (PARTITION + speed) / (1.0 + speed)
    return p + TIME_STEP * rate, c + TIME_STEP * (div + 0.5 * (1.0 - keff) * c * rate)


def kernel(
    dims, ready, phase, solute, undercool, cotangent, weight, lift, local, bias, proj,
    zf, zg, zi, tx, ty, tyi, txi, txf, tyf,
    phase_far, solute_far, predicted_far, modes_far, spec_far, added_far,
    phase_out, solute_out, predicted_out, spec_out, added_out, modes_out, out_sem,
    yhi, ylo, from_ylo, from_yhi, from_corner, from_xlo, from_xhi,
    pad_p, pad_c, pad_d, pad_u, mid_p, mid_c, mid_d, flat, cells, cot, total, coef, lifted, blend, field, sums,
    send1, recv1, send2, recv2, send3, recv3, send4, recv4, recv5, send6, recv6, send7, recv7,
    send8, recv8, recv9, send10, recv10, send11, recv11, send12, recv12,
    halo_send, halo_recv, send_sem, recv_sem, recv6_sem,
):
    gx, gy, group = dims
    ix, iy = lax.axis_index("gx"), lax.axis_index("gy")
    east, west = lax.rem(ix + 1, gx), lax.rem(ix + gx - 1, gx)
    north, south = lax.rem(iy + 1, gy), lax.rem(iy + gy - 1, gy)
    width = lift.shape[1]
    pairs = width // 2
    kx, ky = 2 * gx, gy
    rows = gy // 4
    team, member = iy // 4, lax.rem(iy, 4)
    square = width * width
    barrier = pltpu.get_barrier_semaphore()

    def greet(axis, mine, count):
        def one(j, carry):
            pl.semaphore_signal(barrier, inc=1, device_id={axis: lax.rem(mine + j, count)}, device_id_type=MESH)
            return carry

        lax.fori_loop(1, count, one, 0)

    for a in (east, west):
        for b in (north, south):
            pl.semaphore_signal(barrier, inc=1, device_id={"gx": a, "gy": b}, device_id_type=MESH)
    greet("gx", ix, gx)
    greet("gy", iy, gy)

    ready(0, 1, 2)
    row = iota((8, 8, phase.shape[2]), 1)
    p, c, u = phase[...], solute[...], undercool[...]
    yhi[...] = jnp.where(row >= 6, p, jnp.where(row >= 4, pltpu.roll(c, 6, 1), pltpu.roll(u, 4, 1)))
    ylo[...] = jnp.where(row < 2, p, jnp.where(row < 4, pltpu.roll(c, 2, 1), pltpu.roll(u, 4, 1)))
    pad_p[2:10, 8:16, :] = p
    pad_c[2:10, 8:16, :] = c
    pad_u[1:9, 8:16, :] = u

    depth = phase.shape[2]
    src, dst = iota((128, 128), 0), iota((128, 128), 1)
    outer = jnp.where(iota((width, square), 1) // width == iota((width, square), 0), 1.0, 0.0)

    def factors_of_channels():
        ready(5, 6, 7, 8, 3)
        inner = iota((width, square), 1) % width == iota((width, square), 0)
        eye = iota((width, width), 0) == iota((width, width), 1)

        def column(v):
            return jnp.sum(jnp.where(eye, jnp.broadcast_to(v, (width, width)), 0.0), axis=1, keepdims=True)

        def full(v):
            return jnp.broadcast_to(jnp.broadcast_to(v, (width, 128)).reshape(width, 1, 128), (width, 8, 128))

        for k in range(2):
            one = column(lift[k : k + 1, :])
            lifted[k : k + 1, :] = jnp.sum(jnp.where(inner, one, 0.0), axis=0, keepdims=True)
            mixed = jnp.sum(local[...] * lift[k : k + 1, :], axis=1, keepdims=True)
            coef[k * width : (k + 1) * width] = full(mixed)
        for k, vector in ((2, bias), (3, proj)):
            one = column(vector[...])
            coef[k * width : (k + 1) * width] = full(one)
        sums[...] = jnp.zeros_like(sums)
        total[...] = jnp.zeros_like(total)
        for x in range(8):
            for h in range(2):
                flat[h, 8 * x : 8 * x + 8, :] = cotangent[x, :, 128 * h : 128 * h + 128]
        for y in range(8):
            for h in range(2):
                cot[8 * y : 8 * y + 8, 128 * h : 128 * h + 128] = flat[h, pl.ds(y, 8, stride=8), :]

    def weights_of_fields():
        ready(4)
        fold = jnp.where(iota((square, width), 0) // width == iota((square, width), 1), 1.0, 0.0)
        for k in range(2):
            both = dot_pick(weight[...] * lifted[k : k + 1, :], fold)
            both = jnp.concatenate([both, jnp.zeros((128, 128 - width), F32)], axis=1).T
            for part in range(2):
                for x in range(2):
                    value = 0.0
                    for par in range(2):
                        pick = (src % 32 == dst % 32) & (src // 32 == part * 2 + x) & (dst // 64 == par)
                        value = value + dot_pick(both[par * pairs : (par + 1) * pairs], jnp.where(pick, 1.0, 0.0))
                    blend[2 * k + part, pl.ds(x, pairs, stride=2), :] = value

    factors_of_channels()
    pl.semaphore_wait(barrier, 4 + gx - 1 + gy - 1)

    def push(source_ref, target_ref, slot, where):
        copy = pltpu.make_async_remote_copy(
            src_ref=source_ref,
            dst_ref=target_ref,
            send_sem=halo_send.at[slot],
            recv_sem=halo_recv.at[slot],
            device_id=where,
            device_id_type=MESH,
        )
        copy.start()
        return copy

    copies = [
        push(yhi, from_ylo, 0, {"gy": north}),
        push(ylo, from_yhi, 1, {"gy": south}),
        push(yhi.at[7], from_corner.at[0], 2, {"gx": east, "gy": north}),
        push(yhi.at[0], from_corner.at[1], 3, {"gx": west, "gy": north}),
        push(ylo.at[7], from_corner.at[2], 4, {"gx": east, "gy": south}),
        push(ylo.at[0], from_corner.at[3], 5, {"gx": west, "gy": south}),
        push(phase.at[6:8], from_xlo.at[0:2], 6, {"gx": east}),
        push(solute.at[6:8], from_xlo.at[2:4], 7, {"gx": east}),
        push(undercool.at[7:8], from_xlo.at[4:5], 8, {"gx": east}),
        push(phase.at[0:2], from_xhi.at[0:2], 9, {"gx": west}),
        push(solute.at[0:2], from_xhi.at[2:4], 10, {"gx": west}),
        push(undercool.at[0:1], from_xhi.at[4:5], 11, {"gx": west}),
    ]
    for copy in copies:
        copy.wait_recv()

    def lay(rows, low, planes):
        at = slice(0, 8) if low else slice(16, 24)
        turn = 1 if low else -1
        pad_p[planes, at, :] = rows
        pad_c[planes, at, :] = pltpu.roll(rows, (2 * turn) % 8, 1)
        pad_u[slice(planes.start - 1, planes.stop - 1), at, :] = pltpu.roll(rows, 4, 1)

    lay(from_ylo[...], True, slice(2, 10))
    lay(from_yhi[...], False, slice(2, 10))
    lay(from_corner[0:1], True, slice(1, 2))
    lay(from_corner[1:2], True, slice(10, 11))
    lay(from_corner[2:3], False, slice(1, 2))
    lay(from_corner[3:4], False, slice(10, 11))
    pad_p[0:2, 8:16, :] = from_xlo[0:2]
    pad_c[0:2, 8:16, :] = from_xlo[2:4]
    pad_u[0:1, 8:16, :] = from_xlo[4:5]
    pad_p[10:12, 8:16, :] = from_xhi[0:2]
    pad_c[10:12, 8:16, :] = from_xhi[2:4]
    pad_u[9:10, 8:16, :] = from_xhi[4:5]

    def first_diff(x, carry):
        pad_d[x] = diffusivity(pad_p[x])
        return carry

    def first(x, carry):
        new_p, new_c = advance(pad_p, pad_c, pad_d, pad_u[x], x + 1)
        mid_p[x] = new_p
        mid_c[x] = new_c
        mid_d[x] = diffusivity(new_p)
        return carry

    def second(x, carry):
        new_p, new_c = advance(mid_p, mid_c, mid_d, pad_u[x + 1], x + 1)
        new_p, new_c = new_p[8:16], new_c[8:16]
        phase_out[x] = new_p
        solute_out[x] = new_c
        at = pl.multiple_of(8 * x, 8)
        for h in range(2):
            flat[h, pl.ds(at, 8), :] = new_p[:, 128 * h : 128 * h + 128]
            flat[2 + h, pl.ds(at, 8), :] = new_c[:, 128 * h : 128 * h + 128] - SOLUTE_MEAN
        return carry

    lax.fori_loop(0, 12, first_diff, 0)
    lax.fori_loop(0, 10, first, 0)
    lax.fori_loop(0, 8, second, 0)
    writes = [pltpu.make_async_copy(phase_out, phase_far, out_sem.at[0]), pltpu.make_async_copy(solute_out, solute_far, out_sem.at[1])]
    for one in writes:
        one.start()
    for y in range(8):
        for h in range(4):
            cells[8 * y : 8 * y + 8, 128 * h : 128 * h + 128] = flat[h, pl.ds(y, 8, stride=8), :]

    def exchange(axis, phase_id, sends, receives):
        mine, count = {"gx": (ix, gx), "gy": (iy, gy), "team": (member, 4)}[axis]
        pltpu.make_async_copy(sends(mine), receives(mine), recv_sem.at[phase_id]).start()

        def one(j, carry):
            peer = lax.rem(mine + j, count)
            pltpu.make_async_remote_copy(
                src_ref=sends(peer),
                dst_ref=receives(mine),
                send_sem=send_sem.at[phase_id],
                recv_sem=recv_sem.at[phase_id],
                device_id={"gy": 4 * team + peer} if axis == "team" else {axis: peer},
                device_id_type=MESH,
            ).start()
            return carry

        lax.fori_loop(1, count, one, 0)

    def arrived(phase_id, whole):
        pltpu.make_async_copy(whole, whole, recv_sem.at[phase_id]).wait()

    ready(9, 12, 13)
    along = dot_right(cells[...], zf[...])
    lines = jnp.concatenate([along[8 * y : 8 * y + 8] for y in range(8)], axis=1)
    wave = dot(tx[ix].T, lines)
    for y in range(8):
        at = slice(128 * y, 128 * y + 128)
        send1[pl.ds(y, kx, stride=8), :] = wave[:kx, at] + rot(wave[kx:, at])
    exchange("gx", 1, lambda q: send1.at[pl.ds(pl.multiple_of(16 * q, 16), 16)], lambda q: recv1.at[q])
    weights_of_fields()
    arrived(1, recv1)
    got = recv1[0]
    for q in range(1, gx):
        got = got + recv1[q]
    wave = dot(ty[iy].T, got)
    wave = wave[: 2 * ky] + rot(wave[2 * ky :])
    send2[...] = wave.reshape(2 * ky, 1, 128)
    exchange("gy", 2, lambda q: send2.at[pl.ds(2 * q, 2)], lambda q: recv2.at[pl.ds(2 * q, 2)])
    arrived(2, recv2)
    got = recv2[...].reshape(gy, 2, 128).sum(0)
    spec_out[...] = got

    even = iota((gy, 128), 0) % 2 == 0
    spread = jnp.where(even, jnp.broadcast_to(got[0:1], (gy, 128)), jnp.broadcast_to(got[1:2], (gy, 128)))
    turned = pltpu.roll(spread, 64, 1)
    low = iota((gy, 128), 1) < 64
    value = 0.0
    for k in range(2):
        one = jnp.where(low, spread, turned) if k == 0 else jnp.where(low, turned, spread)
        value = value + blend[2 * k] * one - blend[2 * k + 1] * rot(one)
    send3[...] = value.reshape(4, rows, 128)
    exchange("gy", 3, lambda q: send3.at[lax.rem(q, 4)], lambda q: recv3.at[pl.ds(pl.multiple_of(rows * q, rows), rows)])
    ready(14, 15, 16, 17, 10, 11)

    arrived(3, recv3)
    lines = []
    for r in range(rows):
        got = recv3[pl.ds(r, ky, stride=rows), :]
        lines.append(jnp.concatenate([got, rot(got)], axis=0))
    wave = dot_left(tyi[team], jnp.concatenate(lines, axis=1))
    for r in range(rows):
        send4[:, r] = wave[:, 128 * r : 128 * r + 128].reshape(4, 8, 128)
    exchange("team", 4, lambda q: send4.at[q], lambda q: recv4.at[pl.ds(rows * q, rows)])
    arrived(4, recv4)
    exchange("gx", 5, lambda q: recv4.at[pl.ds(2 * q, 2)], lambda q: recv5.at[pl.ds(2 * q, 2)])
    arrived(5, recv5)
    lines = []
    for y in range(8):
        got = recv5[:, y, :]
        lines.append(jnp.concatenate([got, rot(got)], axis=0))
    wave = dot_left(txi[...], jnp.concatenate(lines, axis=1))
    for y in range(8):
        send6[:, y] = wave[:, 128 * y : 128 * y + 128].reshape(gx, 8, 128)

    pltpu.make_async_copy(send6.at[ix], recv6.at[ix], recv6_sem.at[ix]).start()

    def give(j, carry):
        peer = lax.rem(ix + j, gx)
        pltpu.make_async_remote_copy(
            src_ref=send6.at[peer],
            dst_ref=recv6.at[ix],
            send_sem=send_sem.at[6],
            recv_sem=recv6_sem.at[ix],
            device_id={"gx": peer},
            device_id_type=MESH,
        ).start()
        return carry

    lax.fori_loop(1, gx, give, 0)

    def wide(o):
        one = jnp.concatenate([coef[o], coef[o]], axis=1)
        return jnp.concatenate([one, one], axis=0)

    def step(j, carry):
        owners = [lax.rem(ix + gx - (j * group + t), gx) for t in range(group)]
        for owner in owners:
            pltpu.make_async_copy(recv6.at[owner], recv6.at[owner], recv6_sem.at[owner]).wait()
        got = jnp.concatenate([recv6[owner].reshape(64, 128) for owner in owners], axis=0)
        field[...] = dot_right(got, zi[...])
        for t, owner in enumerate(owners):
            def block(r, acc):
                at = pl.ds(pl.multiple_of(16 * r, 16), 16)
                here = pl.ds(pl.multiple_of(64 * t + 16 * r, 16), 16)
                p, c, w = cells[at, :depth], cells[at, depth:], cot[at, :]
                acc = list(acc)
                out = total[at, :]
                for par in range(2):
                    m0, m1, b, q = (wide(k * width + par * pairs + owner) for k in range(4))
                    side = slice(par * depth, (par + 1) * depth)
                    pre = field[here, side] + m0 * p + m1 * c + b
                    power = pre * pre
                    half = 0.5 + 0.5 * jnp.tanh(pre * (GELU_K + (GELU_K * GELU_C) * power))
                    act = pre * half
                    slope = half + act * (1.0 - half) * (2.0 * GELU_K + (6.0 * GELU_K * GELU_C) * power)
                    out = out + q * act
                    grad = q * w * slope
                    field[here, side] = grad
                    for k, v in enumerate((grad * p, grad * c, act * w)):
                        acc[3 * par + k] = acc[3 * par + k] + (v[:8] + v[8:])
                total[at, :] = out
                return tuple(acc)

            zero = jnp.zeros((8, depth), F32)
            acc = lax.fori_loop(0, 4, block, (zero,) * 6)
            for par in range(2):
                for k in range(3):
                    one = jnp.sum(acc[3 * par + k], axis=0, keepdims=True)
                    sums[k * width + par * pairs + owner] = one[:, :128] + one[:, 128:]
        wave = dot_right(field[...], zg[...])
        for t, owner in enumerate(owners):
            send7[owner] = wave[64 * t : 64 * t + 64].reshape(8, 8, 128)

            @pl.when(owner == ix)
            def _():
                pltpu.make_async_copy(send7.at[owner], recv7.at[ix], recv_sem.at[7]).start()

            @pl.when(owner != ix)
            def _():
                pltpu.make_async_remote_copy(
                    src_ref=send7.at[owner],
                    dst_ref=recv7.at[ix],
                    send_sem=send_sem.at[7],
                    recv_sem=recv_sem.at[7],
                    device_id={"gx": owner},
                    device_id_type=MESH,
                ).start()

        return carry

    lax.fori_loop(0, gx // group, step, 0)
    for h in range(2):
        flat[h] = total[:, 128 * h : 128 * h + 128]
    for x in range(8):
        for h in range(2):
            predicted_out[x, :, 128 * h : 128 * h + 128] = flat[h, pl.ds(x, 8, stride=8), :]
    writes.append(pltpu.make_async_copy(predicted_out, predicted_far, out_sem.at[2]))
    added = dot(jnp.ones((8, 128), F32), sums[...].reshape(128, 128), ((1,), (1,)))
    send12[...] = added[0:1].reshape(1, 1, 128)
    exchange("gx", 12, lambda q: send12, lambda q: recv12.at[pl.ds(q, 1)])
    writes.append(pltpu.make_async_copy(spec_out, spec_far, out_sem.at[3]))
    for one in writes[2:]:
        one.start()

    arrived(7, recv7)
    lines = [recv7[:, y].reshape(8 * gx, 128) for y in range(8)]
    wave = dot_left(txf[...], jnp.concatenate(lines, axis=1))
    for y in range(8):
        at = slice(128 * y, 128 * y + 128)
        one = wave[:kx, at] + rot(wave[kx:, at])
        for k in range(2):
            send8[pl.ds(8 * k + y, gx, stride=16), :] = one[k * gx : (k + 1) * gx]
    exchange("gx", 8, lambda q: send8.at[pl.ds(pl.multiple_of(16 * q, 16), 16)], lambda q: recv8.at[pl.ds(pl.multiple_of(16 * q, 16), 16)])
    arrived(12, recv12)
    send11[...] = recv12[...].reshape(gx, 128).sum(0, keepdims=True).reshape(1, 1, 128)
    exchange("gy", 11, lambda q: send11, lambda q: recv11.at[pl.ds(q, 1)])
    arrived(8, recv8)
    block = 8 * rows
    exchange(
        "team", 9,
        lambda q: recv8.at[pl.ds(pl.multiple_of(block * q, block), block)],
        lambda q: recv9.at[pl.ds(pl.multiple_of(block * q, block), block)],
    )
    arrived(9, recv9)
    lines = []
    for r in range(rows):
        lines.append(jnp.concatenate([recv9[block * m + 8 * r : block * m + 8 * r + 8] for m in range(4)], axis=0))
    wave = dot_left(tyf[team], jnp.concatenate(lines, axis=1))
    for r in range(rows):
        at = slice(128 * r, 128 * r + 128)
        send10[pl.ds(r, ky, stride=rows), :] = wave[:ky, at] + rot(wave[ky:, at])
    part = lambda ref: lambda q: ref.at[pl.ds(pl.multiple_of(rows * q, rows), rows)]
    exchange("gy", 10, part(send10), part(recv10))
    arrived(11, recv11)
    added_out[...] = recv11[...].reshape(gy, 128).sum(0, keepdims=True)
    writes.append(pltpu.make_async_copy(added_out, added_far, out_sem.at[4]))
    writes[4].start()
    arrived(10, recv10)
    got = recv10[0:gy]
    for g in range(1, gy // 4):
        got = got + recv10[gy * g : gy * g + gy]
    modes_out[...] = got
    writes.append(pltpu.make_async_copy(modes_out, modes_far, out_sem.at[5]))
    writes[5].start()
    for one in writes:
        one.wait()

    for copy in copies:
        copy.wait_send()
    for phase_id, whole in (
        (1, recv1.at[1:gx]),
        (2, send2.at[2 : 2 * gy]),
        (3, recv3.at[rows : gy * rows]),
        (4, recv4.at[rows:gy]),
        (5, recv4.at[2 : 2 * gx]),
        (6, send6.at[1:gx]),
        (7, send7.at[1:gx]),
        (8, send8.at[16 : 16 * gx]),
        (9, recv9.at[block : 4 * block]),
        (10, send10.at[rows : gy * rows]),
        (11, recv11.at[1:gy]),
        (12, recv12.at[1:gx]),
    ):
        pltpu.make_async_copy(whole, whole, send_sem.at[phase_id]).wait()


def finish(
    scale, phase_in, solute_in, predicted_in, modes_in, spec_in, added_in, lift_in,
    phase_far, solute_far, predicted_far, spectral_far, local_far, proj_far,
    phase, solute, predicted, modes, spec, added, lift, spectral, local, proj, in_sem, out_sem,
):
    far_in = (phase_in, solute_in, predicted_in, modes_in, spec_in, added_in, lift_in)
    near = (phase, solute, predicted, modes, spec, added, lift)
    reads = [pltpu.make_async_copy(a, b, in_sem.at[k]) for k, (a, b) in enumerate(zip(far_in, near))]
    far_out = (phase_far, solute_far, predicted_far, spectral_far, local_far, proj_far)
    made = (phase, solute, predicted, spectral, local, proj)
    writes = [pltpu.make_async_copy(a, b, out_sem.at[k]) for k, (a, b) in enumerate(zip(made, far_out))]
    for k in (6, 4, 3, 5, 0, 1, 2):
        reads[k].start()
    width = lift.shape[1]
    pairs, square = width // 2, width * width
    outer = jnp.where(iota((width, square), 1) // width == iota((width, square), 0), 1.0, 0.0)
    inner = iota((width, square), 1) % width == iota((width, square), 0)
    eye = iota((width, width), 0) == iota((width, width), 1)
    src, dst = iota((128, 128), 0), iota((128, 128), 1)
    reads[6].wait()
    lifted = []
    for k in range(2):
        one = jnp.sum(jnp.where(eye, jnp.broadcast_to(lift[k : k + 1, :], (width, width)), 0.0), axis=1, keepdims=True)
        lifted.append(jnp.sum(jnp.where(inner, one, 0.0), axis=0, keepdims=True))
    reads[4].wait()
    reads[3].wait()
    for x in range(2):
        diagonal = jnp.where(src == dst, jnp.broadcast_to(spec[x : x + 1, :], (128, 128)), 0.0)
        column = jnp.sum(diagonal, axis=1, keepdims=True)
        source = column[:64] * lifted[0] + column[64:] * lifted[1]
        got = modes[pl.ds(x, pairs, stride=2), :]
        got = jnp.concatenate([got, pltpu.roll(got, 64, 1)], axis=0).T[:64]
        grad = dot_pick(got, outer)
        re, im = grad[:32], grad[32:]
        s_re, s_im = source[:32], source[32:]
        spectral[0, x, 0] = re * s_re + im * s_im
        spectral[1, x, 0] = im * s_re - re * s_im
    writes[3].start()
    for k in range(3):
        reads[k].wait()
        writes[k].start()
    reads[5].wait()
    scaled = added[...] * scale
    place = iota((width, 128), 1) - iota((width, 128), 0)
    value = 0.0
    for k in range(2):
        picked = jnp.where(place == k * width, jnp.broadcast_to(scaled, (width, 128)), 0.0)
        value = value + jnp.sum(picked, axis=1, keepdims=True) * lift[k : k + 1, :]
    local[...] = value
    pick = iota((128, width), 0) - iota((128, width), 1) == 2 * width
    column = jnp.sum(jnp.where(src == dst, jnp.broadcast_to(scaled, (128, 128)), 0.0), axis=1, keepdims=True)
    proj[...] = jnp.sum(jnp.where(pick, column, 0.0), axis=0, keepdims=True)
    writes[4].start()
    writes[5].start()
    for one in writes:
        one.wait()


def per_device(phase, solute, undercool, lift, weight, local, bias, proj, cotangent):
    gx, gy = lax.axis_size("gx"), lax.axis_size("gy")
    cx, cy, depth = phase.shape
    own_kx, own_ky, kz = weight.shape[1:4]
    width = lift.shape[0]
    square = width * width
    assert width == 2 * gx and gy == 2 * gx and (cx, cy, own_kx, own_ky, kz) == (8, 8, 2, 1, 32)
    consts = tables(gx, gy, cx, cy, depth, gx * own_kx, gy * own_ky, kz)
    group, rows = min(4, gx), gy // 4
    far_spec = pl.BlockSpec(memory_space=pl.ANY)
    buf = lambda *shape: pltpu.VMEM(shape, F32)
    tile = jax.ShapeDtypeStruct((cx, cy, depth), F32)
    shape = lambda *dims: jax.ShapeDtypeStruct(dims, F32)
    outs = (tile, tile, tile, shape(gy, 128), shape(2, 128), shape(1, 128))
    scratch = [
        buf(8, 8, depth), buf(8, 8, depth), buf(8, 8, depth), buf(2, 128), buf(1, 128), buf(gy, 128), pltpu.SemaphoreType.DMA((6,)),
        buf(8, 8, depth), buf(8, 8, depth), buf(8, 8, depth), buf(8, 8, depth), buf(4, 8, depth), buf(5, 8, depth), buf(5, 8, depth),
        buf(12, 24, depth), buf(12, 24, depth), buf(12, 24, depth), buf(10, 24, depth),
        buf(10, 24, depth), buf(10, 24, depth), buf(10, 24, depth),
        buf(4, 64, 128), buf(64, 2 * depth), buf(64, depth), buf(64, depth),
        buf(4 * width, 8, 128), buf(2, square), buf(4, gy, 128), buf(64 * group, 2 * depth), buf(128, 1, 128),
        buf(16 * gx, 128), buf(gx, 16, 128), buf(2 * gy, 1, 128), buf(2 * gy, 1, 128), buf(4, rows, 128), buf(gy * rows, 128),
        buf(4, rows, 8, 128), buf(gy, 8, 128), buf(2 * gx, 8, 128), buf(gx, 8, 8, 128), buf(gx, 8, 8, 128),
        buf(gx, 8, 8, 128), buf(gx, 8, 8, 128), buf(16 * gx, 128), buf(16 * gx, 128), buf(32 * rows, 128),
        buf(gy * rows, 128), buf(gy * rows, 128), buf(1, 1, 128), buf(gy, 1, 128), buf(1, 1, 128), buf(gx, 1, 128),
        pltpu.SemaphoreType.DMA((12,)), pltpu.SemaphoreType.DMA((12,)),
        pltpu.SemaphoreType.DMA((13,)), pltpu.SemaphoreType.DMA((13,)), pltpu.SemaphoreType.DMA((gx,)),
    ]
    args = [phase, solute, undercool, cotangent, weight.reshape(128, square), lift.T, local, bias.reshape(1, -1), proj.reshape(1, -1)]
    args += [jnp.asarray(t) for t in consts]
    scratch += [pltpu.VMEM(one.shape, one.dtype) for one in args] + [pltpu.SemaphoreType.DMA((len(args),))]
    count = len(args)

    def body(*refs):
        far, rest, near, sems = refs[:count], refs[count : -count - 1], refs[-count - 1 : -1], refs[-1]
        loads = [pltpu.make_async_copy(far[k], near[k], sems.at[k]) for k in range(count)]
        for k in (0, 1, 2, 5, 6, 7, 8, 3, 4, 9, 12, 13, 14, 15, 11, 10, 16, 17):
            loads[k].start()

        def ready(*which):
            for k in which:
                loads[k].wait()

        kernel((gx, gy, group), ready, *near, *rest)

    got = pl.pallas_call(
        body,
        out_shape=outs,
        in_specs=[far_spec] * count,
        out_specs=(far_spec,) * len(outs),
        scratch_shapes=scratch,
        compiler_params=pltpu.CompilerParams(collective_id=0, has_side_effects=True, vmem_limit_bytes=60 * 2**20),
        name="layer",
    )(*args)
    scale = 1.0 / math.sqrt(8 * gx * 8 * gy * depth)
    finals = (tile, tile, tile, shape(*weight.shape), shape(width, width), shape(1, width))
    got = pl.pallas_call(
        lambda *refs: finish(scale, *refs),
        out_shape=finals,
        in_specs=[far_spec] * 7,
        out_specs=(far_spec,) * 6,
        scratch_shapes=[
            buf(8, 8, depth), buf(8, 8, depth), buf(8, 8, depth), buf(gy, 128), buf(2, 128), buf(1, 128), buf(2, width),
            buf(*weight.shape), buf(width, width), buf(1, width),
            pltpu.SemaphoreType.DMA((7,)), pltpu.SemaphoreType.DMA((6,)),
        ],
        compiler_params=pltpu.CompilerParams(vmem_limit_bytes=60 * 2**20),
        name="finish",
    )(*got, lift.T)
    return (*got[:5], got[5].reshape(width))


def solution(mesh):
    tile, modes = P("gx", "gy", None), P(None, "gx", "gy", None, None)
    return jax.shard_map(
        per_device,
        mesh=mesh,
        in_specs=(tile, tile, tile, P(), modes, P(), P(), P(), tile),
        out_specs=(tile, tile, tile, modes, P(), P()),
        check_vma=False,
    )
```

```python
import math

import numpy as np

import jax
import jax.numpy as jnp
from jax import lax
from jax.experimental import pallas as pl
from jax.experimental.pallas import tpu as pltpu
from jax.sharding import PartitionSpec as P

TIME_STEP = 0.05
COUPLING = 2.0
SOLID_DIFF = 0.05
LIQUID_DIFF = 1.0
PARTITION = 0.15
TRAP_RATE = 4.0
SOLUTE_MEAN = 0.5
GELU_K = math.sqrt(2.0 / math.pi)
GELU_C = 0.044715
F32 = jnp.float32
MESH = pl.DeviceIdType.MESH


def signed(count):
    index = np.arange(count)
    return np.where(index < count // 2, index, index - count)


def trig(freqs, places, length, factor=1.0):
    angle = 2.0 * np.pi * ((freqs[:, None] * places[None, :]) % length) / length
    return np.cos(angle) * factor, np.sin(angle) * factor


def z_tables(modes, depth):
    cos, sin = trig(np.arange(modes), np.arange(depth), depth)
    lanes = 2 * modes
    weight = np.where(np.arange(modes) == 0, 1.0, 2.0) / depth
    both = np.stack([cos, -sin])

    def blocks(one):
        full = np.zeros((2 * depth, 2 * lanes))
        full[:depth, :lanes] = one
        full[depth:, lanes:] = one
        return full

    plain = both.reshape(lanes, depth).T
    heavy = (both * weight[None, :, None]).reshape(lanes, depth).T
    return blocks(plain), blocks(heavy), blocks(heavy).T


def tables(gx, gy, cx, cy, depth, kx, ky, kz):
    nx, ny = gx * cx, gy * cy
    own = kx // gx
    zf, zg, zi = z_tables(kz, depth)
    cosx, sinx = trig(signed(kx), np.arange(nx), nx)
    cosy, siny = trig(signed(ky), np.arange(ny), ny)
    tx = np.concatenate([cosx, sinx]).reshape(2 * kx, gx, cx).transpose(1, 2, 0)
    ty = np.zeros((gy, own, cy, 2, ky, own))
    both = np.stack([cosy, siny]).reshape(2, ky, gy, cy).transpose(2, 3, 0, 1)
    for k in range(own):
        ty[:, k, :, :, :, k] = both
    ty = ty.reshape(gy, own * cy, 2 * ky * own)
    team = 4 * cy
    tyi = (np.concatenate([cosy, -siny]).T / ny).reshape(ny // team, team, 2 * ky)
    txi = np.concatenate([cosx, -sinx]).T / nx
    txf = np.stack([cosx, sinx]).reshape(2, gx, own, nx).transpose(0, 2, 1, 3).reshape(2 * kx, nx) / nx
    tyf = (np.concatenate([cosy, siny]) / ny).reshape(2 * ky, ny // team, team).transpose(1, 0, 2)
    right = [in_three(t, 0) for t in (zf, zg, zi)]
    left = [in_three(t, t.ndim - 1) for t in (tyi, txi, txf, tyf)]
    return right + [np.asarray(tx, np.float32), np.asarray(ty, np.float32)] + left


def in_three(table, axis):
    table = np.asarray(table, np.float32)
    high = table.astype(jnp.bfloat16)
    low = (table - high.astype(np.float32)).astype(jnp.bfloat16)
    return np.concatenate([high, low, high], axis=axis)


def parts(v, axis, order):
    high = v.astype(jnp.bfloat16)
    low = (v - high.astype(F32)).astype(jnp.bfloat16)
    return jnp.concatenate([(high, low)[k] for k in order], axis=axis)


def dot_right(v, table):
    return jnp.dot(parts(v, 1, (0, 0, 1)), table, preferred_element_type=F32)


def dot_left(table, v):
    return jnp.dot(table, parts(v, 0, (0, 0, 1)), preferred_element_type=F32)


def dot_pick(v, pick):
    high = v.astype(jnp.bfloat16)
    low = (v - high.astype(F32)).astype(jnp.bfloat16)
    pick = pick.astype(jnp.bfloat16)
    return jnp.dot(high, pick, preferred_element_type=F32) + jnp.dot(low, pick, preferred_element_type=F32)


def dot(a, b, dims=((1,), (0,))):
    return lax.dot_general(a, b, (dims, ((), ())), precision=lax.Precision.HIGHEST, preferred_element_type=F32)


def iota(shape, dim):
    return lax.broadcasted_iota(jnp.int32, shape, dim)


def rot(v):
    imag = (iota(v.shape, 1) // 32) % 2 == 1
    return jnp.where(imag, -pltpu.roll(v, 32, 1), pltpu.roll(v, 96, 1))


def diffusivity(p):
    return SOLID_DIFF + (LIQUID_DIFF - SOLID_DIFF) * 0.5 * (1.0 - jnp.tanh(p))


def around(ref, x):
    centre = ref[x]
    rows, depth = centre.shape
    return centre, [
        ref[x + 1],
        ref[x - 1],
        pltpu.roll(centre, rows - 1, 0),
        pltpu.roll(centre, 1, 0),
        pltpu.roll(centre, depth - 1, 1),
        pltpu.roll(centre, 1, 1),
    ]


def advance(p_ref, c_ref, d_ref, undercool, x):
    p, p_nb = around(p_ref, x)
    c, c_nb = around(c_ref, x)
    d, d_nb = around(d_ref, x)
    total = p_nb[0]
    for one in p_nb[1:]:
        total = total + one
    squares = 1.0 - p * p
    rate = total - 6.0 * p + p - p * p * p + COUPLING * squares * squares * (undercool - c)
    div = 0.0
    for dn, cn in zip(d_nb, c_nb):
        div = div + 0.5 * (d + dn) * (cn - c)
    speed = TRAP_RATE * jnp.abs(rate)
    keff = (PARTITION + speed) / (1.0 + speed)
    return p + TIME_STEP * rate, c + TIME_STEP * (div + 0.5 * (1.0 - keff) * c * rate)


def partners(ix, gx, sign):
    if gx != 16:
        steps = [lax.rem(ix + gx + sign * k, gx) for k in range(gx)]
        return steps, None
    x, y, core = ix // 8, lax.rem(ix // 2, 4), lax.rem(ix, 2)
    xs = [8 * x, 8 * (1 - x)]
    ys = [2 * lax.rem(y + 4 + sign * d, 4) for d in range(4)]
    cores = [core, 1 - core]
    steps = [xs[dx] + ys[dy] + cores[c] for dx, dy in ((0, 0), (1, 0), (0, 2), (1, 2), (1, 1), (1, 3), (0, 1), (0, 3)) for c in range(2)]

    def group(j):
        found = []
        for b in range(2):
            dx = jnp.where(j < 2, b, 3 - j)
            dy = jnp.where(j < 2, 2 * j, 1 + 2 * b)
            at = jnp.where(dx == 1, xs[1], xs[0]) + 2 * lax.rem(y + 4 + sign * dy, 4)
            found += [at + cores[0], at + cores[1]]
        return found

    return steps, group


def kernel(
    dims, start, ready, phase, solute, undercool, cotangent, weight, lift, local, bias, proj,
    zf, zg, zi, tx, ty, tyi, txi, txf, tyf,
    phase_far, solute_far, predicted_far, modes_far, spec_far, added_far,
    phase_out, solute_out, predicted_out, spec_out, added_out, modes_out, out_sem,
    yhi, ylo, from_ylo, from_yhi, from_corner, from_xlo, from_xhi,
    pad_p, pad_c, pad_d, pad_u, mid_p, mid_c, mid_d, flat, cells, cot, total, coef, lifted, blend, field, sums,
    send1, recv1, send2, recv2, send3, recv3, send4, recv4, recv5, send6, recv6, send7, recv7,
    send8, recv8, recv9, send10, recv10, send11, recv11, send12, recv12,
    halo_send, halo_recv, send_sem, recv_sem, recv6_sem,
):
    gx, gy, group = dims
    ix, iy = lax.axis_index("gx"), lax.axis_index("gy")
    east, west = lax.rem(ix + 1, gx), lax.rem(ix + gx - 1, gx)
    north, south = lax.rem(iy + 1, gy), lax.rem(iy + gy - 1, gy)
    width = lift.shape[1]
    pairs = width // 2
    kx, ky = 2 * gx, gy
    rows = gy // 4
    team, member = iy // 4, lax.rem(iy, 4)
    square = width * width
    outward, _ = partners(ix, gx, 1)
    inward, inward_group = partners(ix, gx, -1)
    assert inward_group or gx <= group
    barrier = pltpu.get_barrier_semaphore()

    def greet(where):
        pl.semaphore_signal(barrier, inc=1, device_id=where, device_id_type=MESH)

    def greet_y(k, carry):
        greet({"gy": lax.rem(iy + gy // 2 + k, gy)})
        greet({"gy": lax.rem(iy + gy // 2 + gy - k, gy)})
        return carry

    def greet_x(j, carry):
        greet({"gx": lax.rem(ix + j, gx)})
        return carry

    greet({"gy": lax.rem(iy + gy // 2, gy)})
    lax.fori_loop(1, gy // 2, greet_y, 0)
    for a in (east, west):
        for b in (north, south):
            greet({"gx": a, "gy": b})
    lax.fori_loop(1, gx, greet_x, 0)
    start()

    ready(0, 1, 2)
    row = iota((8, 8, phase.shape[2]), 1)
    p, c, u = phase[...], solute[...], undercool[...]
    yhi[...] = jnp.where(row >= 6, p, jnp.where(row >= 4, pltpu.roll(c, 6, 1), pltpu.roll(u, 4, 1)))
    ylo[...] = jnp.where(row < 2, p, jnp.where(row < 4, pltpu.roll(c, 2, 1), pltpu.roll(u, 4, 1)))
    pad_p[2:10, 8:16, :] = p
    pad_c[2:10, 8:16, :] = c
    pad_u[1:9, 8:16, :] = u

    depth = phase.shape[2]
    src, dst = iota((128, 128), 0), iota((128, 128), 1)
    outer = jnp.where(iota((width, square), 1) // width == iota((width, square), 0), 1.0, 0.0)

    def factors_of_channels():
        ready(5, 6, 7, 8, 3)
        inner = iota((width, square), 1) % width == iota((width, square), 0)
        eye = iota((width, width), 0) == iota((width, width), 1)

        def column(v):
            return jnp.sum(jnp.where(eye, jnp.broadcast_to(v, (width, width)), 0.0), axis=1, keepdims=True)

        def full(v):
            return jnp.broadcast_to(jnp.broadcast_to(v, (width, 128)).reshape(width, 1, 128), (width, 8, 128))

        for k in range(2):
            one = column(lift[k : k + 1, :])
            lifted[k : k + 1, :] = jnp.sum(jnp.where(inner, one, 0.0), axis=0, keepdims=True)
            mixed = jnp.sum(local[...] * lift[k : k + 1, :], axis=1, keepdims=True)
            coef[k * width : (k + 1) * width] = full(mixed)
        for k, vector in ((2, bias), (3, proj)):
            one = column(vector[...])
            coef[k * width : (k + 1) * width] = full(one)
        sums[...] = jnp.zeros_like(sums)
        total[...] = jnp.zeros_like(total)
        for x in range(8):
            for h in range(2):
                flat[h, 8 * x : 8 * x + 8, :] = cotangent[x, :, 128 * h : 128 * h + 128]
        for y in range(8):
            for h in range(2):
                cot[8 * y : 8 * y + 8, 128 * h : 128 * h + 128] = flat[h, pl.ds(y, 8, stride=8), :]

    def weights_of_fields():
        ready(4)
        fold = jnp.where(iota((square, width), 0) // width == iota((square, width), 1), 1.0, 0.0)
        for k in range(2):
            both = dot_pick(weight[...] * lifted[k : k + 1, :], fold)
            both = jnp.concatenate([both, jnp.zeros((128, 128 - width), F32)], axis=1).T
            for part in range(2):
                for x in range(2):
                    value = 0.0
                    for par in range(2):
                        pick = (src % 32 == dst % 32) & (src // 32 == part * 2 + x) & (dst // 64 == par)
                        value = value + dot_pick(both[par * pairs : (par + 1) * pairs], jnp.where(pick, 1.0, 0.0))
                    blend[2 * k + part, pl.ds(x, pairs, stride=2), :] = value

    factors_of_channels()
    pl.semaphore_wait(barrier, 4 + gx - 1 + gy - 1)

    def push(source_ref, target_ref, slot, where):
        copy = pltpu.make_async_remote_copy(
            src_ref=source_ref,
            dst_ref=target_ref,
            send_sem=halo_send.at[slot],
            recv_sem=halo_recv.at[slot],
            device_id=where,
            device_id_type=MESH,
        )
        copy.start()
        return copy

    copies = [
        push(yhi, from_ylo, 0, {"gy": north}),
        push(ylo, from_yhi, 1, {"gy": south}),
        push(yhi.at[7], from_corner.at[0], 2, {"gx": east, "gy": north}),
        push(yhi.at[0], from_corner.at[1], 3, {"gx": west, "gy": north}),
        push(ylo.at[7], from_corner.at[2], 4, {"gx": east, "gy": south}),
        push(ylo.at[0], from_corner.at[3], 5, {"gx": west, "gy": south}),
        push(phase.at[6:8], from_xlo.at[0:2], 6, {"gx": east}),
        push(solute.at[6:8], from_xlo.at[2:4], 7, {"gx": east}),
        push(undercool.at[7:8], from_xlo.at[4:5], 8, {"gx": east}),
        push(phase.at[0:2], from_xhi.at[0:2], 9, {"gx": west}),
        push(solute.at[0:2], from_xhi.at[2:4], 10, {"gx": west}),
        push(undercool.at[0:1], from_xhi.at[4:5], 11, {"gx": west}),
    ]
    for copy in copies:
        copy.wait_recv()

    def lay(rows, low, planes):
        at = slice(0, 8) if low else slice(16, 24)
        turn = 1 if low else -1
        pad_p[planes, at, :] = rows
        pad_c[planes, at, :] = pltpu.roll(rows, (2 * turn) % 8, 1)
        pad_u[slice(planes.start - 1, planes.stop - 1), at, :] = pltpu.roll(rows, 4, 1)

    lay(from_ylo[...], True, slice(2, 10))
    lay(from_yhi[...], False, slice(2, 10))
    lay(from_corner[0:1], True, slice(1, 2))
    lay(from_corner[1:2], True, slice(10, 11))
    lay(from_corner[2:3], False, slice(1, 2))
    lay(from_corner[3:4], False, slice(10, 11))
    pad_p[0:2, 8:16, :] = from_xlo[0:2]
    pad_c[0:2, 8:16, :] = from_xlo[2:4]
    pad_u[0:1, 8:16, :] = from_xlo[4:5]
    pad_p[10:12, 8:16, :] = from_xhi[0:2]
    pad_c[10:12, 8:16, :] = from_xhi[2:4]
    pad_u[9:10, 8:16, :] = from_xhi[4:5]

    def first_diff(x, carry):
        pad_d[x] = diffusivity(pad_p[x])
        return carry

    def first(x, carry):
        new_p, new_c = advance(pad_p, pad_c, pad_d, pad_u[x], x + 1)
        mid_p[x] = new_p
        mid_c[x] = new_c
        mid_d[x] = diffusivity(new_p)
        return carry

    def second(x, carry):
        new_p, new_c = advance(mid_p, mid_c, mid_d, pad_u[x + 1], x + 1)
        new_p, new_c = new_p[8:16], new_c[8:16]
        phase_out[x] = new_p
        solute_out[x] = new_c
        at = pl.multiple_of(8 * x, 8)
        for h in range(2):
            flat[h, pl.ds(at, 8), :] = new_p[:, 128 * h : 128 * h + 128]
            flat[2 + h, pl.ds(at, 8), :] = new_c[:, 128 * h : 128 * h + 128] - SOLUTE_MEAN
        return carry

    lax.fori_loop(0, 12, first_diff, 0)
    lax.fori_loop(0, 10, first, 0)
    lax.fori_loop(0, 8, second, 0)
    writes = [pltpu.make_async_copy(phase_out, phase_far, out_sem.at[0]), pltpu.make_async_copy(solute_out, solute_far, out_sem.at[1])]
    for one in writes:
        one.start()
    for y in range(8):
        for h in range(4):
            cells[8 * y : 8 * y + 8, 128 * h : 128 * h + 128] = flat[h, pl.ds(y, 8, stride=8), :]

    def exchange(axis, phase_id, sends, receives):
        mine, count = {"gx": (ix, gx), "gy": (iy, gy), "team": (member, 4)}[axis]
        pltpu.make_async_copy(sends(mine), receives(mine), recv_sem.at[phase_id]).start()

        def to(peer):
            pltpu.make_async_remote_copy(
                src_ref=sends(peer),
                dst_ref=receives(mine),
                send_sem=send_sem.at[phase_id],
                recv_sem=recv_sem.at[phase_id],
                device_id={"gy": 4 * team + peer} if axis == "team" else {axis: peer},
                device_id_type=MESH,
            ).start()

        def both_ways(k, carry):
            to(lax.rem(iy + gy // 2 + k, gy))
            to(lax.rem(iy + gy // 2 + gy - k, gy))
            return carry

        if axis == "gy":
            to(lax.rem(iy + gy // 2, gy))
            lax.fori_loop(1, gy // 2, both_ways, 0)
        elif axis == "gx":
            for k in range(1, gx):
                to(outward[1 + (k + 2) % (gx - 1)])
        else:
            for k in (2, 1, 3):
                to(lax.rem(member + k, 4))

    def arrived(phase_id, whole):
        pltpu.make_async_copy(whole, whole, recv_sem.at[phase_id]).wait()

    ready(9, 12, 13)
    along = dot_right(cells[...], zf[...])
    lines = jnp.concatenate([along[8 * y : 8 * y + 8] for y in range(8)], axis=1)
    wave = dot(tx[ix].T, lines)
    for y in range(8):
        at = slice(128 * y, 128 * y + 128)
        send1[pl.ds(y, kx, stride=8), :] = wave[:kx, at] + rot(wave[kx:, at])
    exchange("gx", 1, lambda q: send1.at[pl.ds(pl.multiple_of(16 * q, 16), 16)], lambda q: recv1.at[q])
    weights_of_fields()
    arrived(1, recv1)
    got = recv1[0]
    for q in range(1, gx):
        got = got + recv1[q]
    wave = dot(ty[iy].T, got)
    wave = wave[: 2 * ky] + rot(wave[2 * ky :])
    send2[...] = wave.reshape(2 * ky, 1, 128)
    exchange("gy", 2, lambda q: send2.at[pl.ds(2 * q, 2)], lambda q: recv2.at[pl.ds(2 * q, 2)])
    arrived(2, recv2)
    got = recv2[...].reshape(gy, 2, 128).sum(0)
    spec_out[...] = got

    even = iota((gy, 128), 0) % 2 == 0
    spread = jnp.where(even, jnp.broadcast_to(got[0:1], (gy, 128)), jnp.broadcast_to(got[1:2], (gy, 128)))
    turned = pltpu.roll(spread, 64, 1)
    low = iota((gy, 128), 1) < 64
    value = 0.0
    for k in range(2):
        one = jnp.where(low, spread, turned) if k == 0 else jnp.where(low, turned, spread)
        value = value + blend[2 * k] * one - blend[2 * k + 1] * rot(one)
    send3[...] = value.reshape(4, rows, 128)
    exchange("gy", 3, lambda q: send3.at[lax.rem(q, 4)], lambda q: recv3.at[pl.ds(pl.multiple_of(rows * q, rows), rows)])
    ready(14, 15, 16, 17, 10, 11)

    arrived(3, recv3)
    lines = []
    for r in range(rows):
        got = recv3[pl.ds(r, ky, stride=rows), :]
        lines.append(jnp.concatenate([got, rot(got)], axis=0))
    wave = dot_left(tyi[team], jnp.concatenate(lines, axis=1))
    for r in range(rows):
        send4[:, r] = wave[:, 128 * r : 128 * r + 128].reshape(4, 8, 128)
    exchange("team", 4, lambda q: send4.at[q], lambda q: recv4.at[pl.ds(rows * q, rows)])
    arrived(4, recv4)
    exchange("gx", 5, lambda q: recv4.at[pl.ds(2 * q, 2)], lambda q: recv5.at[pl.ds(2 * q, 2)])
    arrived(5, recv5)
    lines = []
    for y in range(8):
        got = recv5[:, y, :]
        lines.append(jnp.concatenate([got, rot(got)], axis=0))
    wave = dot_left(txi[...], jnp.concatenate(lines, axis=1))
    for y in range(8):
        send6[:, y] = wave[:, 128 * y : 128 * y + 128].reshape(gx, 8, 128)

    pltpu.make_async_copy(send6.at[ix], recv6.at[ix], recv6_sem.at[ix]).start()

    for peer in outward[1:]:
        pltpu.make_async_remote_copy(
            src_ref=send6.at[peer],
            dst_ref=recv6.at[ix],
            send_sem=send_sem.at[6],
            recv_sem=recv6_sem.at[ix],
            device_id={"gx": peer},
            device_id_type=MESH,
        ).start()

    def wide(o):
        one = jnp.concatenate([coef[o], coef[o]], axis=1)
        return jnp.concatenate([one, one], axis=0)

    def step(j, carry):
        owners = inward_group(j) if inward_group else inward
        for owner in owners:
            pltpu.make_async_copy(recv6.at[owner], recv6.at[owner], recv6_sem.at[owner]).wait()
        got = jnp.concatenate([recv6[owner].reshape(64, 128) for owner in owners], axis=0)
        field[...] = dot_right(got, zi[...])
        for t, owner in enumerate(owners):
            def block(r, acc):
                at = pl.ds(pl.multiple_of(16 * r, 16), 16)
                here = pl.ds(pl.multiple_of(64 * t + 16 * r, 16), 16)
                p, c, w = cells[at, :depth], cells[at, depth:], cot[at, :]
                acc = list(acc)
                out = total[at, :]
                for par in range(2):
                    m0, m1, b, q = (wide(k * width + par * pairs + owner) for k in range(4))
                    side = slice(par * depth, (par + 1) * depth)
                    pre = field[here, side] + m0 * p + m1 * c + b
                    power = pre * pre
                    half = 0.5 + 0.5 * jnp.tanh(pre * (GELU_K + (GELU_K * GELU_C) * power))
                    act = pre * half
                    slope = half + act * (1.0 - half) * (2.0 * GELU_K + (6.0 * GELU_K * GELU_C) * power)
                    out = out + q * act
                    grad = q * w * slope
                    field[here, side] = grad
                    for k, v in enumerate((grad * p, grad * c, act * w)):
                        acc[3 * par + k] = acc[3 * par + k] + (v[:8] + v[8:])
                total[at, :] = out
                return tuple(acc)

            zero = jnp.zeros((8, depth), F32)
            acc = lax.fori_loop(0, 4, block, (zero,) * 6)
            for par in range(2):
                for k in range(3):
                    one = jnp.sum(acc[3 * par + k], axis=0, keepdims=True)
                    sums[k * width + par * pairs + owner] = one[:, :128] + one[:, 128:]
        wave = dot_right(field[...], zg[...])
        for t, owner in enumerate(owners):
            send7[owner] = wave[64 * t : 64 * t + 64].reshape(8, 8, 128)

            @pl.when(owner == ix)
            def _():
                pltpu.make_async_copy(send7.at[owner], recv7.at[ix], recv_sem.at[7]).start()

            @pl.when(owner != ix)
            def _():
                pltpu.make_async_remote_copy(
                    src_ref=send7.at[owner],
                    dst_ref=recv7.at[ix],
                    send_sem=send_sem.at[7],
                    recv_sem=recv_sem.at[7],
                    device_id={"gx": owner},
                    device_id_type=MESH,
                ).start()

        return carry

    lax.fori_loop(0, gx // group, step, 0)
    for h in range(2):
        flat[h] = total[:, 128 * h : 128 * h + 128]
    for x in range(8):
        for h in range(2):
            predicted_out[x, :, 128 * h : 128 * h + 128] = flat[h, pl.ds(x, 8, stride=8), :]
    writes.append(pltpu.make_async_copy(predicted_out, predicted_far, out_sem.at[2]))
    added = dot(jnp.ones((8, 128), F32), sums[...].reshape(128, 128), ((1,), (1,)))
    send12[...] = added[0:1].reshape(1, 1, 128)
    exchange("gx", 12, lambda q: send12, lambda q: recv12.at[pl.ds(q, 1)])
    writes.append(pltpu.make_async_copy(spec_out, spec_far, out_sem.at[3]))
    for one in writes[2:]:
        one.start()

    arrived(7, recv7)
    lines = [recv7[:, y].reshape(8 * gx, 128) for y in range(8)]
    wave = dot_left(txf[...], jnp.concatenate(lines, axis=1))
    for y in range(8):
        at = slice(128 * y, 128 * y + 128)
        one = wave[:kx, at] + rot(wave[kx:, at])
        for k in range(2):
            send8[pl.ds(8 * k + y, gx, stride=16), :] = one[k * gx : (k + 1) * gx]
    exchange("gx", 8, lambda q: send8.at[pl.ds(pl.multiple_of(16 * q, 16), 16)], lambda q: recv8.at[pl.ds(pl.multiple_of(16 * q, 16), 16)])
    arrived(12, recv12)
    send11[...] = recv12[...].reshape(gx, 128).sum(0, keepdims=True).reshape(1, 1, 128)
    exchange("gy", 11, lambda q: send11, lambda q: recv11.at[pl.ds(q, 1)])
    arrived(8, recv8)
    block = 8 * rows
    exchange(
        "team", 9,
        lambda q: recv8.at[pl.ds(pl.multiple_of(block * q, block), block)],
        lambda q: recv9.at[pl.ds(pl.multiple_of(block * q, block), block)],
    )
    arrived(9, recv9)
    lines = []
    for r in range(rows):
        lines.append(jnp.concatenate([recv9[block * m + 8 * r : block * m + 8 * r + 8] for m in range(4)], axis=0))
    wave = dot_left(tyf[team], jnp.concatenate(lines, axis=1))
    for r in range(rows):
        at = slice(128 * r, 128 * r + 128)
        send10[pl.ds(r, ky, stride=rows), :] = wave[:ky, at] + rot(wave[ky:, at])
    part = lambda ref: lambda q: ref.at[pl.ds(pl.multiple_of(rows * q, rows), rows)]
    exchange("gy", 10, part(send10), part(recv10))
    arrived(11, recv11)
    added_out[...] = recv11[...].reshape(gy, 128).sum(0, keepdims=True)
    writes.append(pltpu.make_async_copy(added_out, added_far, out_sem.at[4]))
    writes[4].start()
    arrived(10, recv10)
    got = recv10[0:gy]
    for g in range(1, gy // 4):
        got = got + recv10[gy * g : gy * g + gy]
    modes_out[...] = got
    writes.append(pltpu.make_async_copy(modes_out, modes_far, out_sem.at[5]))
    writes[5].start()
    for one in writes:
        one.wait()

    for copy in copies:
        copy.wait_send()
    for phase_id, whole in (
        (1, recv1.at[1:gx]),
        (2, send2.at[2 : 2 * gy]),
        (3, recv3.at[rows : gy * rows]),
        (4, recv4.at[rows:gy]),
        (5, recv4.at[2 : 2 * gx]),
        (6, send6.at[1:gx]),
        (7, send7.at[1:gx]),
        (8, send8.at[16 : 16 * gx]),
        (9, recv9.at[block : 4 * block]),
        (10, send10.at[rows : gy * rows]),
        (11, recv11.at[1:gy]),
        (12, recv12.at[1:gx]),
    ):
        pltpu.make_async_copy(whole, whole, send_sem.at[phase_id]).wait()


def finish(
    scale, phase_in, solute_in, predicted_in, modes_in, spec_in, added_in, lift_in,
    phase_far, solute_far, predicted_far, spectral_far, local_far, proj_far,
    phase, solute, predicted, modes, spec, added, lift, spectral, local, proj, in_sem, out_sem,
):
    far_in = (phase_in, solute_in, predicted_in, modes_in, spec_in, added_in, lift_in)
    near = (phase, solute, predicted, modes, spec, added, lift)
    reads = [pltpu.make_async_copy(a, b, in_sem.at[k]) for k, (a, b) in enumerate(zip(far_in, near))]
    far_out = (phase_far, solute_far, predicted_far, spectral_far, local_far, proj_far)
    made = (phase, solute, predicted, spectral, local, proj)
    writes = [pltpu.make_async_copy(a, b, out_sem.at[k]) for k, (a, b) in enumerate(zip(made, far_out))]
    for k in (6, 4, 3, 5, 0, 1, 2):
        reads[k].start()
    width = lift.shape[1]
    pairs, square = width // 2, width * width
    outer = jnp.where(iota((width, square), 1) // width == iota((width, square), 0), 1.0, 0.0)
    inner = iota((width, square), 1) % width == iota((width, square), 0)
    eye = iota((width, width), 0) == iota((width, width), 1)
    src, dst = iota((128, 128), 0), iota((128, 128), 1)
    reads[6].wait()
    lifted = []
    for k in range(2):
        one = jnp.sum(jnp.where(eye, jnp.broadcast_to(lift[k : k + 1, :], (width, width)), 0.0), axis=1, keepdims=True)
        lifted.append(jnp.sum(jnp.where(inner, one, 0.0), axis=0, keepdims=True))
    reads[4].wait()
    reads[3].wait()
    for x in range(2):
        diagonal = jnp.where(src == dst, jnp.broadcast_to(spec[x : x + 1, :], (128, 128)), 0.0)
        column = jnp.sum(diagonal, axis=1, keepdims=True)
        source = column[:64] * lifted[0] + column[64:] * lifted[1]
        got = modes[pl.ds(x, pairs, stride=2), :]
        got = jnp.concatenate([got, pltpu.roll(got, 64, 1)], axis=0).T[:64]
        grad = dot_pick(got, outer)
        re, im = grad[:32], grad[32:]
        s_re, s_im = source[:32], source[32:]
        spectral[0, x, 0] = re * s_re + im * s_im
        spectral[1, x, 0] = im * s_re - re * s_im
    writes[3].start()
    for k in range(3):
        reads[k].wait()
        writes[k].start()
    reads[5].wait()
    scaled = added[...] * scale
    place = iota((width, 128), 1) - iota((width, 128), 0)
    value = 0.0
    for k in range(2):
        picked = jnp.where(place == k * width, jnp.broadcast_to(scaled, (width, 128)), 0.0)
        value = value + jnp.sum(picked, axis=1, keepdims=True) * lift[k : k + 1, :]
    local[...] = value
    pick = iota((128, width), 0) - iota((128, width), 1) == 2 * width
    column = jnp.sum(jnp.where(src == dst, jnp.broadcast_to(scaled, (128, 128)), 0.0), axis=1, keepdims=True)
    proj[...] = jnp.sum(jnp.where(pick, column, 0.0), axis=0, keepdims=True)
    writes[4].start()
    writes[5].start()
    for one in writes:
        one.wait()


def per_device(phase, solute, undercool, lift, weight, local, bias, proj, cotangent):
    gx, gy = lax.axis_size("gx"), lax.axis_size("gy")
    cx, cy, depth = phase.shape
    own_kx, own_ky, kz = weight.shape[1:4]
    width = lift.shape[0]
    square = width * width
    assert width == 2 * gx and gy == 2 * gx and (cx, cy, own_kx, own_ky, kz) == (8, 8, 2, 1, 32)
    consts = tables(gx, gy, cx, cy, depth, gx * own_kx, gy * own_ky, kz)
    group, rows = min(4, gx), gy // 4
    far_spec = pl.BlockSpec(memory_space=pl.ANY)
    buf = lambda *shape: pltpu.VMEM(shape, F32)
    tile = jax.ShapeDtypeStruct((cx, cy, depth), F32)
    shape = lambda *dims: jax.ShapeDtypeStruct(dims, F32)
    outs = (tile, tile, tile, shape(gy, 128), shape(2, 128), shape(1, 128))
    scratch = [
        buf(8, 8, depth), buf(8, 8, depth), buf(8, 8, depth), buf(2, 128), buf(1, 128), buf(gy, 128), pltpu.SemaphoreType.DMA((6,)),
        buf(8, 8, depth), buf(8, 8, depth), buf(8, 8, depth), buf(8, 8, depth), buf(4, 8, depth), buf(5, 8, depth), buf(5, 8, depth),
        buf(12, 24, depth), buf(12, 24, depth), buf(12, 24, depth), buf(10, 24, depth),
        buf(10, 24, depth), buf(10, 24, depth), buf(10, 24, depth),
        buf(4, 64, 128), buf(64, 2 * depth), buf(64, depth), buf(64, depth),
        buf(4 * width, 8, 128), buf(2, square), buf(4, gy, 128), buf(64 * group, 2 * depth), buf(128, 1, 128),
        buf(16 * gx, 128), buf(gx, 16, 128), buf(2 * gy, 1, 128), buf(2 * gy, 1, 128), buf(4, rows, 128), buf(gy * rows, 128),
        buf(4, rows, 8, 128), buf(gy, 8, 128), buf(2 * gx, 8, 128), buf(gx, 8, 8, 128), buf(gx, 8, 8, 128),
        buf(gx, 8, 8, 128), buf(gx, 8, 8, 128), buf(16 * gx, 128), buf(16 * gx, 128), buf(32 * rows, 128),
        buf(gy * rows, 128), buf(gy * rows, 128), buf(1, 1, 128), buf(gy, 1, 128), buf(1, 1, 128), buf(gx, 1, 128),
        pltpu.SemaphoreType.DMA((12,)), pltpu.SemaphoreType.DMA((12,)),
        pltpu.SemaphoreType.DMA((13,)), pltpu.SemaphoreType.DMA((13,)), pltpu.SemaphoreType.DMA((gx,)),
    ]
    args = [phase, solute, undercool, cotangent, weight.reshape(128, square), lift.T, local, bias.reshape(1, -1), proj.reshape(1, -1)]
    args += [jnp.asarray(t) for t in consts]
    scratch += [pltpu.VMEM(one.shape, one.dtype) for one in args] + [pltpu.SemaphoreType.DMA((len(args),))]
    count = len(args)

    def body(*refs):
        far, rest, near, sems = refs[:count], refs[count : -count - 1], refs[-count - 1 : -1], refs[-1]
        loads = [pltpu.make_async_copy(far[k], near[k], sems.at[k]) for k in range(count)]

        def start():
            for k in (0, 1, 2, 5, 6, 7, 8, 3, 4, 9, 12, 13, 14, 15, 11, 10, 16, 17):
                loads[k].start()

        def ready(*which):
            for k in which:
                loads[k].wait()

        kernel((gx, gy, group), start, ready, *near, *rest)

    got = pl.pallas_call(
        body,
        out_shape=outs,
        in_specs=[far_spec] * count,
        out_specs=(far_spec,) * len(outs),
        scratch_shapes=scratch,
        compiler_params=pltpu.CompilerParams(collective_id=0, has_side_effects=True, vmem_limit_bytes=60 * 2**20),
        name="layer",
    )(*args)
    scale = 1.0 / math.sqrt(8 * gx * 8 * gy * depth)
    finals = (tile, tile, tile, shape(*weight.shape), shape(width, width), shape(1, width))
    got = pl.pallas_call(
        lambda *refs: finish(scale, *refs),
        out_shape=finals,
        in_specs=[far_spec] * 7,
        out_specs=(far_spec,) * 6,
        scratch_shapes=[
            buf(8, 8, depth), buf(8, 8, depth), buf(8, 8, depth), buf(gy, 128), buf(2, 128), buf(1, 128), buf(2, width),
            buf(*weight.shape), buf(width, width), buf(1, width),
            pltpu.SemaphoreType.DMA((7,)), pltpu.SemaphoreType.DMA((6,)),
        ],
        compiler_params=pltpu.CompilerParams(vmem_limit_bytes=60 * 2**20),
        name="finish",
    )(*got, lift.T)
    return (*got[:5], got[5].reshape(width))


def solution(mesh):
    tile, modes = P("gx", "gy", None), P(None, "gx", "gy", None, None)
    return jax.shard_map(
        per_device,
        mesh=mesh,
        in_specs=(tile, tile, tile, P(), modes, P(), P(), P(), tile),
        out_specs=(tile, tile, tile, modes, P(), P()),
        check_vma=False,
    )
```

```python
import math

import numpy as np

import jax
import jax.numpy as jnp
from jax import lax
from jax.experimental import pallas as pl
from jax.experimental.pallas import tpu as pltpu
from jax.sharding import PartitionSpec as P

TIME_STEP = 0.05
COUPLING = 2.0
SOLID_DIFF = 0.05
LIQUID_DIFF = 1.0
PARTITION = 0.15
TRAP_RATE = 4.0
SOLUTE_MEAN = 0.5
GELU_K = math.sqrt(2.0 / math.pi)
GELU_C = 0.044715
F32 = jnp.float32
MESH = pl.DeviceIdType.MESH


def signed(count):
    index = np.arange(count)
    return np.where(index < count // 2, index, index - count)


def trig(freqs, places, length, factor=1.0):
    angle = 2.0 * np.pi * ((freqs[:, None] * places[None, :]) % length) / length
    return np.cos(angle) * factor, np.sin(angle) * factor


def z_tables(modes, depth):
    cos, sin = trig(np.arange(modes), np.arange(depth), depth)
    lanes = 2 * modes
    weight = np.where(np.arange(modes) == 0, 1.0, 2.0) / depth
    both = np.stack([cos, -sin])

    def blocks(one):
        full = np.zeros((2 * depth, 2 * lanes))
        full[:depth, :lanes] = one
        full[depth:, lanes:] = one
        return full

    plain = both.reshape(lanes, depth).T
    heavy = (both * weight[None, :, None]).reshape(lanes, depth).T
    return blocks(plain), blocks(heavy), blocks(heavy).T


def tables(gx, gy, cx, cy, depth, kx, ky, kz):
    nx, ny = gx * cx, gy * cy
    own = kx // gx
    zf, zg, zi = z_tables(kz, depth)
    cosx, sinx = trig(signed(kx), np.arange(nx), nx)
    cosy, siny = trig(signed(ky), np.arange(ny), ny)
    tx = np.concatenate([cosx, sinx]).reshape(2 * kx, gx, cx).transpose(1, 2, 0)
    ty = np.zeros((gy, own, cy, 2, ky, own))
    both = np.stack([cosy, siny]).reshape(2, ky, gy, cy).transpose(2, 3, 0, 1)
    for k in range(own):
        ty[:, k, :, :, :, k] = both
    ty = ty.reshape(gy, own * cy, 2 * ky * own)
    team = 4 * cy
    tyi = (np.concatenate([cosy, -siny]).T / ny).reshape(ny // team, team, 2 * ky)
    txi = np.concatenate([cosx, -sinx]).T / nx
    txf = np.stack([cosx, sinx]).reshape(2, gx, own, nx).transpose(0, 2, 1, 3).reshape(2 * kx, nx) / nx
    tyf = (np.concatenate([cosy, siny]) / ny).reshape(2 * ky, ny // team, team).transpose(1, 0, 2)
    right = [in_three(t, 0) for t in (zf, zg, zi)]
    left = [in_three(t, t.ndim - 1) for t in (tyi, txi, txf, tyf)]
    return right + [np.asarray(tx, np.float32), np.asarray(ty, np.float32)] + left


def in_three(table, axis):
    table = np.asarray(table, np.float32)
    high = table.astype(jnp.bfloat16)
    low = (table - high.astype(np.float32)).astype(jnp.bfloat16)
    return np.concatenate([high, low, high], axis=axis)


def parts(v, axis, order):
    high = v.astype(jnp.bfloat16)
    low = (v - high.astype(F32)).astype(jnp.bfloat16)
    return jnp.concatenate([(high, low)[k] for k in order], axis=axis)


def dot_right(v, table):
    return jnp.dot(parts(v, 1, (0, 0, 1)), table, preferred_element_type=F32)


def dot_left(table, v):
    return jnp.dot(table, parts(v, 0, (0, 0, 1)), preferred_element_type=F32)


def dot_pick(v, pick):
    high = v.astype(jnp.bfloat16)
    low = (v - high.astype(F32)).astype(jnp.bfloat16)
    pick = pick.astype(jnp.bfloat16)
    return jnp.dot(high, pick, preferred_element_type=F32) + jnp.dot(low, pick, preferred_element_type=F32)


def dot(a, b, dims=((1,), (0,))):
    return lax.dot_general(a, b, (dims, ((), ())), precision=lax.Precision.HIGHEST, preferred_element_type=F32)


def iota(shape, dim):
    return lax.broadcasted_iota(jnp.int32, shape, dim)


def rot(v):
    imag = (iota(v.shape, 1) // 32) % 2 == 1
    return jnp.where(imag, -pltpu.roll(v, 32, 1), pltpu.roll(v, 96, 1))


def diffusivity(p):
    return SOLID_DIFF + (LIQUID_DIFF - SOLID_DIFF) * 0.5 * (1.0 - jnp.tanh(p))


def around(ref, x):
    centre = ref[x]
    rows, depth = centre.shape
    return centre, [
        ref[x + 1],
        ref[x - 1],
        pltpu.roll(centre, rows - 1, 0),
        pltpu.roll(centre, 1, 0),
        pltpu.roll(centre, depth - 1, 1),
        pltpu.roll(centre, 1, 1),
    ]


def advance(p_ref, c_ref, d_ref, undercool, x):
    p, p_nb = around(p_ref, x)
    c, c_nb = around(c_ref, x)
    d, d_nb = around(d_ref, x)
    total = p_nb[0]
    for one in p_nb[1:]:
        total = total + one
    squares = 1.0 - p * p
    rate = total - 6.0 * p + p - p * p * p + COUPLING * squares * squares * (undercool - c)
    div = 0.0
    for dn, cn in zip(d_nb, c_nb):
        div = div + 0.5 * (d + dn) * (cn - c)
    speed = TRAP_RATE * jnp.abs(rate)
    keff = (PARTITION + speed) / (1.0 + speed)
    return p + TIME_STEP * rate, c + TIME_STEP * (div + 0.5 * (1.0 - keff) * c * rate)


def partners(ix, gx, sign):
    if gx != 16:
        steps = [lax.rem(ix + gx + sign * k, gx) for k in range(gx)]
        return steps, None
    x, y, core = ix // 8, lax.rem(ix // 2, 4), lax.rem(ix, 2)
    xs = [8 * x, 8 * (1 - x)]
    ys = [2 * lax.rem(y + 4 + sign * d, 4) for d in range(4)]
    cores = [core, 1 - core]
    steps = [xs[dx] + ys[dy] + cores[c] for dx, dy in ((0, 0), (1, 0), (0, 2), (1, 2), (1, 1), (1, 3), (0, 1), (0, 3)) for c in range(2)]

    def group(j):
        found = []
        for b in range(2):
            dx = jnp.where(j < 2, b, 3 - j)
            dy = jnp.where(j < 2, 2 * j, 1 + 2 * b)
            at = jnp.where(dx == 1, xs[1], xs[0]) + 2 * lax.rem(y + 4 + sign * dy, 4)
            found += [at + cores[0], at + cores[1]]
        return found

    return steps, group


def kernel(
    dims, start, ready, phase, solute, undercool, cotangent, weight, lift, local, bias, proj,
    zf, zg, zi, tx, ty, tyi, txi, txf, tyf,
    phase_far, solute_far, predicted_far, modes_far, spec_far, added_far,
    phase_out, solute_out, predicted_out, spec_out, added_out, modes_out, out_sem,
    yhi, ylo, from_ylo, from_yhi, from_corner, from_xlo, from_xhi,
    pad_p, pad_c, pad_d, pad_u, mid_p, mid_c, mid_d, flat, cells, cot, total, coef, lifted, blend, field, sums,
    send1, recv1, send2, recv2, send3, recv3, send4, recv5, send6, recv6, send7, recv7,
    send8, recv9, send10, recv10, send11, recv11, send12, recv12,
    halo_send, halo_recv, send_sem, recv_sem, recv6_sem,
):
    gx, gy, group = dims
    ix, iy = lax.axis_index("gx"), lax.axis_index("gy")
    east, west = lax.rem(ix + 1, gx), lax.rem(ix + gx - 1, gx)
    north, south = lax.rem(iy + 1, gy), lax.rem(iy + gy - 1, gy)
    width = lift.shape[1]
    pairs = width // 2
    kx, ky = 2 * gx, gy
    rows = gy // 4
    team, member = iy // 4, lax.rem(iy, 4)
    per = gx // 4
    holder = ix // per
    same = holder == member
    square = width * width
    outward, _ = partners(ix, gx, 1)
    inward, inward_group = partners(ix, gx, -1)
    assert inward_group or gx <= group
    barrier = pltpu.get_barrier_semaphore()

    def greet(where):
        pl.semaphore_signal(barrier, inc=1, device_id=where, device_id_type=MESH)

    def greet_y(k, carry):
        greet({"gy": lax.rem(iy + gy // 2 + k, gy)})
        greet({"gy": lax.rem(iy + gy // 2 + gy - k, gy)})
        return carry

    def greet_x(j, carry):
        greet({"gx": lax.rem(ix + j, gx)})
        return carry

    greet({"gy": lax.rem(iy + gy // 2, gy)})
    lax.fori_loop(1, gy // 2, greet_y, 0)
    for a in (east, west):
        for b in (north, south):
            greet({"gx": a, "gy": b})
    lax.fori_loop(1, gx, greet_x, 0)

    def greet_holders(q, carry):
        greet({"gx": q, "gy": 4 * team + holder})
        return carry

    def greet_owners(a, carry):
        for m in range(4):
            greet({"gx": per * member + a, "gy": 4 * team + m})
        return carry

    lax.fori_loop(0, gx, greet_holders, 0)
    lax.fori_loop(0, per, greet_owners, 0)
    start()

    ready(0, 1, 2)
    row = iota((8, 8, phase.shape[2]), 1)
    p, c, u = phase[...], solute[...], undercool[...]
    yhi[...] = jnp.where(row >= 6, p, jnp.where(row >= 4, pltpu.roll(c, 6, 1), pltpu.roll(u, 4, 1)))
    ylo[...] = jnp.where(row < 2, p, jnp.where(row < 4, pltpu.roll(c, 2, 1), pltpu.roll(u, 4, 1)))
    pad_p[2:10, 8:16, :] = p
    pad_c[2:10, 8:16, :] = c
    pad_u[1:9, 8:16, :] = u

    depth = phase.shape[2]
    src, dst = iota((128, 128), 0), iota((128, 128), 1)
    outer = jnp.where(iota((width, square), 1) // width == iota((width, square), 0), 1.0, 0.0)

    def factors_of_channels():
        ready(5, 6, 7, 8, 3)
        inner = iota((width, square), 1) % width == iota((width, square), 0)
        eye = iota((width, width), 0) == iota((width, width), 1)

        def column(v):
            return jnp.sum(jnp.where(eye, jnp.broadcast_to(v, (width, width)), 0.0), axis=1, keepdims=True)

        def full(v):
            return jnp.broadcast_to(jnp.broadcast_to(v, (width, 128)).reshape(width, 1, 128), (width, 8, 128))

        for k in range(2):
            one = column(lift[k : k + 1, :])
            lifted[k : k + 1, :] = jnp.sum(jnp.where(inner, one, 0.0), axis=0, keepdims=True)
            mixed = jnp.sum(local[...] * lift[k : k + 1, :], axis=1, keepdims=True)
            coef[k * width : (k + 1) * width] = full(mixed)
        for k, vector in ((2, bias), (3, proj)):
            one = column(vector[...])
            coef[k * width : (k + 1) * width] = full(one)
        sums[...] = jnp.zeros_like(sums)
        total[...] = jnp.zeros_like(total)
        for x in range(8):
            for h in range(2):
                flat[h, 8 * x : 8 * x + 8, :] = cotangent[x, :, 128 * h : 128 * h + 128]
        for y in range(8):
            for h in range(2):
                cot[8 * y : 8 * y + 8, 128 * h : 128 * h + 128] = flat[h, pl.ds(y, 8, stride=8), :]

    def weights_of_fields():
        ready(4)
        fold = jnp.where(iota((square, width), 0) // width == iota((square, width), 1), 1.0, 0.0)
        for k in range(2):
            both = dot_pick(weight[...] * lifted[k : k + 1, :], fold)
            both = jnp.concatenate([both, jnp.zeros((128, 128 - width), F32)], axis=1).T
            for part in range(2):
                for x in range(2):
                    value = 0.0
                    for par in range(2):
                        pick = (src % 32 == dst % 32) & (src // 32 == part * 2 + x) & (dst // 64 == par)
                        value = value + dot_pick(both[par * pairs : (par + 1) * pairs], jnp.where(pick, 1.0, 0.0))
                    blend[2 * k + part, pl.ds(x, pairs, stride=2), :] = value

    factors_of_channels()
    pl.semaphore_wait(barrier, 4 + gx - 1 + gy - 1 + 2 * gx)

    def push(source_ref, target_ref, slot, where):
        copy = pltpu.make_async_remote_copy(
            src_ref=source_ref,
            dst_ref=target_ref,
            send_sem=halo_send.at[slot],
            recv_sem=halo_recv.at[slot],
            device_id=where,
            device_id_type=MESH,
        )
        copy.start()
        return copy

    copies = [
        push(yhi, from_ylo, 0, {"gy": north}),
        push(ylo, from_yhi, 1, {"gy": south}),
        push(yhi.at[7], from_corner.at[0], 2, {"gx": east, "gy": north}),
        push(yhi.at[0], from_corner.at[1], 3, {"gx": west, "gy": north}),
        push(ylo.at[7], from_corner.at[2], 4, {"gx": east, "gy": south}),
        push(ylo.at[0], from_corner.at[3], 5, {"gx": west, "gy": south}),
        push(phase.at[6:8], from_xlo.at[0:2], 6, {"gx": east}),
        push(solute.at[6:8], from_xlo.at[2:4], 7, {"gx": east}),
        push(undercool.at[7:8], from_xlo.at[4:5], 8, {"gx": east}),
        push(phase.at[0:2], from_xhi.at[0:2], 9, {"gx": west}),
        push(solute.at[0:2], from_xhi.at[2:4], 10, {"gx": west}),
        push(undercool.at[0:1], from_xhi.at[4:5], 11, {"gx": west}),
    ]
    for copy in copies:
        copy.wait_recv()

    def lay(rows, low, planes):
        at = slice(0, 8) if low else slice(16, 24)
        turn = 1 if low else -1
        pad_p[planes, at, :] = rows
        pad_c[planes, at, :] = pltpu.roll(rows, (2 * turn) % 8, 1)
        pad_u[slice(planes.start - 1, planes.stop - 1), at, :] = pltpu.roll(rows, 4, 1)

    lay(from_ylo[...], True, slice(2, 10))
    lay(from_yhi[...], False, slice(2, 10))
    lay(from_corner[0:1], True, slice(1, 2))
    lay(from_corner[1:2], True, slice(10, 11))
    lay(from_corner[2:3], False, slice(1, 2))
    lay(from_corner[3:4], False, slice(10, 11))
    pad_p[0:2, 8:16, :] = from_xlo[0:2]
    pad_c[0:2, 8:16, :] = from_xlo[2:4]
    pad_u[0:1, 8:16, :] = from_xlo[4:5]
    pad_p[10:12, 8:16, :] = from_xhi[0:2]
    pad_c[10:12, 8:16, :] = from_xhi[2:4]
    pad_u[9:10, 8:16, :] = from_xhi[4:5]

    def first_diff(x, carry):
        pad_d[x] = diffusivity(pad_p[x])
        return carry

    def first(x, carry):
        new_p, new_c = advance(pad_p, pad_c, pad_d, pad_u[x], x + 1)
        mid_p[x] = new_p
        mid_c[x] = new_c
        mid_d[x] = diffusivity(new_p)
        return carry

    def second(x, carry):
        new_p, new_c = advance(mid_p, mid_c, mid_d, pad_u[x + 1], x + 1)
        new_p, new_c = new_p[8:16], new_c[8:16]
        phase_out[x] = new_p
        solute_out[x] = new_c
        at = pl.multiple_of(8 * x, 8)
        for h in range(2):
            flat[h, pl.ds(at, 8), :] = new_p[:, 128 * h : 128 * h + 128]
            flat[2 + h, pl.ds(at, 8), :] = new_c[:, 128 * h : 128 * h + 128] - SOLUTE_MEAN
        return carry

    lax.fori_loop(0, 12, first_diff, 0)
    lax.fori_loop(0, 10, first, 0)
    lax.fori_loop(0, 8, second, 0)
    writes = [pltpu.make_async_copy(phase_out, phase_far, out_sem.at[0]), pltpu.make_async_copy(solute_out, solute_far, out_sem.at[1])]
    for one in writes:
        one.start()
    for y in range(8):
        for h in range(4):
            cells[8 * y : 8 * y + 8, 128 * h : 128 * h + 128] = flat[h, pl.ds(y, 8, stride=8), :]

    def exchange(axis, phase_id, sends, receives):
        mine = ix if axis == "gx" else iy
        pltpu.make_async_copy(sends(mine), receives(mine), recv_sem.at[phase_id]).start()

        def to(peer):
            pltpu.make_async_remote_copy(
                src_ref=sends(peer),
                dst_ref=receives(mine),
                send_sem=send_sem.at[phase_id],
                recv_sem=recv_sem.at[phase_id],
                device_id={axis: peer},
                device_id_type=MESH,
            ).start()

        def both_ways(k, carry):
            to(lax.rem(iy + gy // 2 + k, gy))
            to(lax.rem(iy + gy // 2 + gy - k, gy))
            return carry

        if axis == "gy":
            to(lax.rem(iy + gy // 2, gy))
            lax.fori_loop(1, gy // 2, both_ways, 0)
        else:
            for k in range(1, gx):
                to(outward[1 + (k + 2) % (gx - 1)])

    def straight(phase_id, source_ref, target_ref, q, m, own):
        def far():
            pltpu.make_async_remote_copy(
                src_ref=source_ref,
                dst_ref=target_ref,
                send_sem=send_sem.at[phase_id],
                recv_sem=recv_sem.at[phase_id],
                device_id={"gx": q, "gy": 4 * team + m},
                device_id_type=MESH,
            ).start()

        if own is None:
            far()
        else:
            pl.when(own)(lambda: pltpu.make_async_copy(source_ref, target_ref, recv_sem.at[phase_id]).start())
            pl.when(jnp.logical_not(own))(far)

    def arrived(phase_id, whole):
        pltpu.make_async_copy(whole, whole, recv_sem.at[phase_id]).wait()

    ready(9, 12, 13)
    along = dot_right(cells[...], zf[...])
    lines = jnp.concatenate([along[8 * y : 8 * y + 8] for y in range(8)], axis=1)
    wave = dot(tx[ix].T, lines)
    for y in range(8):
        at = slice(128 * y, 128 * y + 128)
        send1[pl.ds(y, kx, stride=8), :] = wave[:kx, at] + rot(wave[kx:, at])
    exchange("gx", 1, lambda q: send1.at[pl.ds(pl.multiple_of(16 * q, 16), 16)], lambda q: recv1.at[q])
    weights_of_fields()
    arrived(1, recv1)
    got = recv1[0]
    for q in range(1, gx):
        got = got + recv1[q]
    wave = dot(ty[iy].T, got)
    wave = wave[: 2 * ky] + rot(wave[2 * ky :])
    send2[...] = wave.reshape(2 * ky, 1, 128)
    exchange("gy", 2, lambda q: send2.at[pl.ds(2 * q, 2)], lambda q: recv2.at[pl.ds(2 * q, 2)])
    arrived(2, recv2)
    got = recv2[...].reshape(gy, 2, 128).sum(0)
    spec_out[...] = got

    even = iota((gy, 128), 0) % 2 == 0
    spread = jnp.where(even, jnp.broadcast_to(got[0:1], (gy, 128)), jnp.broadcast_to(got[1:2], (gy, 128)))
    turned = pltpu.roll(spread, 64, 1)
    low = iota((gy, 128), 1) < 64
    value = 0.0
    for k in range(2):
        one = jnp.where(low, spread, turned) if k == 0 else jnp.where(low, turned, spread)
        value = value + blend[2 * k] * one - blend[2 * k + 1] * rot(one)
    send3[...] = value.reshape(4, rows, 128)
    exchange("gy", 3, lambda q: send3.at[lax.rem(q, 4)], lambda q: recv3.at[pl.ds(pl.multiple_of(rows * q, rows), rows)])
    ready(14, 15, 16, 17, 10, 11)

    arrived(3, recv3)
    lines = []
    for r in range(rows):
        got = recv3[pl.ds(r, ky, stride=rows), :]
        lines.append(jnp.concatenate([got, rot(got)], axis=0))
    wave = dot_left(tyi[team], jnp.concatenate(lines, axis=1))
    for r in range(rows):
        send4[:, r] = wave[:, 128 * r : 128 * r + 128].reshape(4, 8, 128)
    for d in (2, 1, 3, 0):
        m = lax.rem(member + d, 4)
        for a in range(per):
            q = per * member + a
            straight(4, send4.at[m, 2 * a : 2 * a + 2], recv5.at[pl.ds(2 * ix, 2)], q, m, q == ix if d == 0 else None)
    arrived(4, recv5)
    lines = []
    for y in range(8):
        got = recv5[:, y, :]
        lines.append(jnp.concatenate([got, rot(got)], axis=0))
    wave = dot_left(txi[...], jnp.concatenate(lines, axis=1))
    for y in range(8):
        send6[:, y] = wave[:, 128 * y : 128 * y + 128].reshape(gx, 8, 128)

    pltpu.make_async_copy(send6.at[ix], recv6.at[ix], recv6_sem.at[ix]).start()

    for peer in outward[1:]:
        pltpu.make_async_remote_copy(
            src_ref=send6.at[peer],
            dst_ref=recv6.at[ix],
            send_sem=send_sem.at[6],
            recv_sem=recv6_sem.at[ix],
            device_id={"gx": peer},
            device_id_type=MESH,
        ).start()

    def wide(o):
        one = jnp.concatenate([coef[o], coef[o]], axis=1)
        return jnp.concatenate([one, one], axis=0)

    def step(j, carry):
        owners = inward_group(j) if inward_group else inward
        for owner in owners:
            pltpu.make_async_copy(recv6.at[owner], recv6.at[owner], recv6_sem.at[owner]).wait()
        got = jnp.concatenate([recv6[owner].reshape(64, 128) for owner in owners], axis=0)
        field[...] = dot_right(got, zi[...])
        for t, owner in enumerate(owners):
            def block(r, acc):
                at = pl.ds(pl.multiple_of(16 * r, 16), 16)
                here = pl.ds(pl.multiple_of(64 * t + 16 * r, 16), 16)
                p, c, w = cells[at, :depth], cells[at, depth:], cot[at, :]
                acc = list(acc)
                out = total[at, :]
                for par in range(2):
                    m0, m1, b, q = (wide(k * width + par * pairs + owner) for k in range(4))
                    side = slice(par * depth, (par + 1) * depth)
                    pre = field[here, side] + m0 * p + m1 * c + b
                    power = pre * pre
                    half = 0.5 + 0.5 * jnp.tanh(pre * (GELU_K + (GELU_K * GELU_C) * power))
                    act = pre * half
                    slope = half + act * (1.0 - half) * (2.0 * GELU_K + (6.0 * GELU_K * GELU_C) * power)
                    out = out + q * act
                    grad = q * w * slope
                    field[here, side] = grad
                    for k, v in enumerate((grad * p, grad * c, act * w)):
                        acc[3 * par + k] = acc[3 * par + k] + (v[:8] + v[8:])
                total[at, :] = out
                return tuple(acc)

            zero = jnp.zeros((8, depth), F32)
            acc = lax.fori_loop(0, 4, block, (zero,) * 6)
            for par in range(2):
                for k in range(3):
                    one = jnp.sum(acc[3 * par + k], axis=0, keepdims=True)
                    sums[k * width + par * pairs + owner] = one[:, :128] + one[:, 128:]
        wave = dot_right(field[...], zg[...])
        for t, owner in enumerate(owners):
            send7[owner] = wave[64 * t : 64 * t + 64].reshape(8, 8, 128)

            @pl.when(owner == ix)
            def _():
                pltpu.make_async_copy(send7.at[owner], recv7.at[ix], recv_sem.at[7]).start()

            @pl.when(owner != ix)
            def _():
                pltpu.make_async_remote_copy(
                    src_ref=send7.at[owner],
                    dst_ref=recv7.at[ix],
                    send_sem=send_sem.at[7],
                    recv_sem=recv_sem.at[7],
                    device_id={"gx": owner},
                    device_id_type=MESH,
                ).start()

        return carry

    lax.fori_loop(0, gx // group, step, 0)
    for h in range(2):
        flat[h] = total[:, 128 * h : 128 * h + 128]
    for x in range(8):
        for h in range(2):
            predicted_out[x, :, 128 * h : 128 * h + 128] = flat[h, pl.ds(x, 8, stride=8), :]
    writes.append(pltpu.make_async_copy(predicted_out, predicted_far, out_sem.at[2]))
    added = dot(jnp.ones((8, 128), F32), sums[...].reshape(128, 128), ((1,), (1,)))
    send12[...] = added[0:1].reshape(1, 1, 128)
    exchange("gx", 12, lambda q: send12, lambda q: recv12.at[pl.ds(q, 1)])
    writes.append(pltpu.make_async_copy(spec_out, spec_far, out_sem.at[3]))
    for one in writes[2:]:
        one.start()

    arrived(7, recv7)
    lines = [recv7[:, y].reshape(8 * gx, 128) for y in range(8)]
    wave = dot_left(txf[...], jnp.concatenate(lines, axis=1))
    for y in range(8):
        at = slice(128 * y, 128 * y + 128)
        one = wave[:kx, at] + rot(wave[kx:, at])
        for k in range(2):
            send8[pl.ds(8 * k + y, gx, stride=16), :] = one[k * gx : (k + 1) * gx]
    block = 8 * rows
    for k in range(gx):
        at = 1 + (k + 3) % (gx - 1) if k < gx - 1 else 0
        q = outward[at]
        straight(
            9,
            send8.at[pl.ds(pl.multiple_of(16 * q, 16), 16)],
            recv9.at[pl.ds(pl.multiple_of(block * member + 16 * lax.rem(ix, per), 16), 16)],
            q,
            holder,
            same if at == 0 else None,
        )
    arrived(12, recv12)
    send11[...] = recv12[...].reshape(gx, 128).sum(0, keepdims=True).reshape(1, 1, 128)
    exchange("gy", 11, lambda q: send11, lambda q: recv11.at[pl.ds(q, 1)])
    arrived(9, recv9)
    lines = []
    for r in range(rows):
        lines.append(jnp.concatenate([recv9[block * m + 8 * r : block * m + 8 * r + 8] for m in range(4)], axis=0))
    wave = dot_left(tyf[team], jnp.concatenate(lines, axis=1))
    for r in range(rows):
        at = slice(128 * r, 128 * r + 128)
        send10[pl.ds(r, ky, stride=rows), :] = wave[:ky, at] + rot(wave[ky:, at])
    part = lambda ref: lambda q: ref.at[pl.ds(pl.multiple_of(rows * q, rows), rows)]
    exchange("gy", 10, part(send10), part(recv10))
    arrived(11, recv11)
    added_out[...] = recv11[...].reshape(gy, 128).sum(0, keepdims=True)
    writes.append(pltpu.make_async_copy(added_out, added_far, out_sem.at[4]))
    writes[4].start()
    arrived(10, recv10)
    got = recv10[0:gy]
    for g in range(1, gy // 4):
        got = got + recv10[gy * g : gy * g + gy]
    modes_out[...] = got
    writes.append(pltpu.make_async_copy(modes_out, modes_far, out_sem.at[5]))
    writes[5].start()
    for one in writes:
        one.wait()

    for copy in copies:
        copy.wait_send()
    for phase_id, whole in (
        (1, recv1.at[1:gx]),
        (2, send2.at[2 : 2 * gy]),
        (3, recv3.at[rows : gy * rows]),
        (4, recv5.at[2 : 2 * gx]),
        (6, send6.at[1:gx]),
        (7, send7.at[1:gx]),
        (9, send8.at[16 : 16 * gx]),
        (10, send10.at[rows : gy * rows]),
        (11, recv11.at[1:gy]),
        (12, recv12.at[1:gx]),
    ):
        pltpu.make_async_copy(whole, whole, send_sem.at[phase_id]).wait()

    @pl.when(jnp.logical_not(same))
    def _():
        for phase_id, whole in ((4, recv5.at[0:2]), (9, send8.at[0:16])):
            pltpu.make_async_copy(whole, whole, send_sem.at[phase_id]).wait()


def finish(
    scale, phase_in, solute_in, predicted_in, modes_in, spec_in, added_in, lift_in,
    phase_far, solute_far, predicted_far, spectral_far, local_far, proj_far,
    phase, solute, predicted, modes, spec, added, lift, spectral, local, proj, in_sem, out_sem,
):
    far_in = (phase_in, solute_in, predicted_in, modes_in, spec_in, added_in, lift_in)
    near = (phase, solute, predicted, modes, spec, added, lift)
    reads = [pltpu.make_async_copy(a, b, in_sem.at[k]) for k, (a, b) in enumerate(zip(far_in, near))]
    far_out = (phase_far, solute_far, predicted_far, spectral_far, local_far, proj_far)
    made = (phase, solute, predicted, spectral, local, proj)
    writes = [pltpu.make_async_copy(a, b, out_sem.at[k]) for k, (a, b) in enumerate(zip(made, far_out))]
    for k in (6, 4, 3, 5, 0, 1, 2):
        reads[k].start()
    width = lift.shape[1]
    pairs, square = width // 2, width * width
    outer = jnp.where(iota((width, square), 1) // width == iota((width, square), 0), 1.0, 0.0)
    inner = iota((width, square), 1) % width == iota((width, square), 0)
    eye = iota((width, width), 0) == iota((width, width), 1)
    src, dst = iota((128, 128), 0), iota((128, 128), 1)
    reads[6].wait()
    lifted = []
    for k in range(2):
        one = jnp.sum(jnp.where(eye, jnp.broadcast_to(lift[k : k + 1, :], (width, width)), 0.0), axis=1, keepdims=True)
        lifted.append(jnp.sum(jnp.where(inner, one, 0.0), axis=0, keepdims=True))
    reads[4].wait()
    reads[3].wait()
    for x in range(2):
        diagonal = jnp.where(src == dst, jnp.broadcast_to(spec[x : x + 1, :], (128, 128)), 0.0)
        column = jnp.sum(diagonal, axis=1, keepdims=True)
        source = column[:64] * lifted[0] + column[64:] * lifted[1]
        got = modes[pl.ds(x, pairs, stride=2), :]
        got = jnp.concatenate([got, pltpu.roll(got, 64, 1)], axis=0).T[:64]
        grad = dot_pick(got, outer)
        re, im = grad[:32], grad[32:]
        s_re, s_im = source[:32], source[32:]
        spectral[0, x, 0] = re * s_re + im * s_im
        spectral[1, x, 0] = im * s_re - re * s_im
    writes[3].start()
    for k in range(3):
        reads[k].wait()
        writes[k].start()
    reads[5].wait()
    scaled = added[...] * scale
    place = iota((width, 128), 1) - iota((width, 128), 0)
    value = 0.0
    for k in range(2):
        picked = jnp.where(place == k * width, jnp.broadcast_to(scaled, (width, 128)), 0.0)
        value = value + jnp.sum(picked, axis=1, keepdims=True) * lift[k : k + 1, :]
    local[...] = value
    pick = iota((128, width), 0) - iota((128, width), 1) == 2 * width
    column = jnp.sum(jnp.where(src == dst, jnp.broadcast_to(scaled, (128, 128)), 0.0), axis=1, keepdims=True)
    proj[...] = jnp.sum(jnp.where(pick, column, 0.0), axis=0, keepdims=True)
    writes[4].start()
    writes[5].start()
    for one in writes:
        one.wait()


def per_device(phase, solute, undercool, lift, weight, local, bias, proj, cotangent):
    gx, gy = lax.axis_size("gx"), lax.axis_size("gy")
    cx, cy, depth = phase.shape
    own_kx, own_ky, kz = weight.shape[1:4]
    width = lift.shape[0]
    square = width * width
    assert width == 2 * gx and gy == 2 * gx and (cx, cy, own_kx, own_ky, kz) == (8, 8, 2, 1, 32)
    consts = tables(gx, gy, cx, cy, depth, gx * own_kx, gy * own_ky, kz)
    group, rows = min(4, gx), gy // 4
    far_spec = pl.BlockSpec(memory_space=pl.ANY)
    buf = lambda *shape: pltpu.VMEM(shape, F32)
    tile = jax.ShapeDtypeStruct((cx, cy, depth), F32)
    shape = lambda *dims: jax.ShapeDtypeStruct(dims, F32)
    outs = (tile, tile, tile, shape(gy, 128), shape(2, 128), shape(1, 128))
    scratch = [
        buf(8, 8, depth), buf(8, 8, depth), buf(8, 8, depth), buf(2, 128), buf(1, 128), buf(gy, 128), pltpu.SemaphoreType.DMA((6,)),
        buf(8, 8, depth), buf(8, 8, depth), buf(8, 8, depth), buf(8, 8, depth), buf(4, 8, depth), buf(5, 8, depth), buf(5, 8, depth),
        buf(12, 24, depth), buf(12, 24, depth), buf(12, 24, depth), buf(10, 24, depth),
        buf(10, 24, depth), buf(10, 24, depth), buf(10, 24, depth),
        buf(4, 64, 128), buf(64, 2 * depth), buf(64, depth), buf(64, depth),
        buf(4 * width, 8, 128), buf(2, square), buf(4, gy, 128), buf(64 * group, 2 * depth), buf(128, 1, 128),
        buf(16 * gx, 128), buf(gx, 16, 128), buf(2 * gy, 1, 128), buf(2 * gy, 1, 128), buf(4, rows, 128), buf(gy * rows, 128),
        buf(4, rows, 8, 128), buf(2 * gx, 8, 128), buf(gx, 8, 8, 128), buf(gx, 8, 8, 128),
        buf(gx, 8, 8, 128), buf(gx, 8, 8, 128), buf(16 * gx, 128), buf(32 * rows, 128),
        buf(gy * rows, 128), buf(gy * rows, 128), buf(1, 1, 128), buf(gy, 1, 128), buf(1, 1, 128), buf(gx, 1, 128),
        pltpu.SemaphoreType.DMA((12,)), pltpu.SemaphoreType.DMA((12,)),
        pltpu.SemaphoreType.DMA((13,)), pltpu.SemaphoreType.DMA((13,)), pltpu.SemaphoreType.DMA((gx,)),
    ]
    args = [phase, solute, undercool, cotangent, weight.reshape(128, square), lift.T, local, bias.reshape(1, -1), proj.reshape(1, -1)]
    args += [jnp.asarray(t) for t in consts]
    scratch += [pltpu.VMEM(one.shape, one.dtype) for one in args] + [pltpu.SemaphoreType.DMA((len(args),))]
    count = len(args)

    def body(*refs):
        far, rest, near, sems = refs[:count], refs[count : -count - 1], refs[-count - 1 : -1], refs[-1]
        loads = [pltpu.make_async_copy(far[k], near[k], sems.at[k]) for k in range(count)]

        def start():
            for k in (0, 1, 2, 5, 6, 7, 8, 3, 4, 9, 12, 13, 14, 15, 11, 10, 16, 17):
                loads[k].start()

        def ready(*which):
            for k in which:
                loads[k].wait()

        kernel((gx, gy, group), start, ready, *near, *rest)

    got = pl.pallas_call(
        body,
        out_shape=outs,
        in_specs=[far_spec] * count,
        out_specs=(far_spec,) * len(outs),
        scratch_shapes=scratch,
        compiler_params=pltpu.CompilerParams(collective_id=0, has_side_effects=True, vmem_limit_bytes=60 * 2**20),
        name="layer",
    )(*args)
    scale = 1.0 / math.sqrt(8 * gx * 8 * gy * depth)
    finals = (tile, tile, tile, shape(*weight.shape), shape(width, width), shape(1, width))
    got = pl.pallas_call(
        lambda *refs: finish(scale, *refs),
        out_shape=finals,
        in_specs=[far_spec] * 7,
        out_specs=(far_spec,) * 6,
        scratch_shapes=[
            buf(8, 8, depth), buf(8, 8, depth), buf(8, 8, depth), buf(gy, 128), buf(2, 128), buf(1, 128), buf(2, width),
            buf(*weight.shape), buf(width, width), buf(1, width),
            pltpu.SemaphoreType.DMA((7,)), pltpu.SemaphoreType.DMA((6,)),
        ],
        compiler_params=pltpu.CompilerParams(vmem_limit_bytes=60 * 2**20),
        name="finish",
    )(*got, lift.T)
    return (*got[:5], got[5].reshape(width))


def solution(mesh):
    tile, modes = P("gx", "gy", None), P(None, "gx", "gy", None, None)
    return jax.shard_map(
        per_device,
        mesh=mesh,
        in_specs=(tile, tile, tile, P(), modes, P(), P(), P(), tile),
        out_specs=(tile, tile, tile, modes, P(), P()),
        check_vma=False,
    )
```

```python
import math

import numpy as np

import jax
import jax.numpy as jnp
from jax import lax
from jax.experimental import pallas as pl
from jax.experimental.pallas import tpu as pltpu
from jax.sharding import PartitionSpec as P

TIME_STEP = 0.05
COUPLING = 2.0
SOLID_DIFF = 0.05
LIQUID_DIFF = 1.0
PARTITION = 0.15
TRAP_RATE = 4.0
SOLUTE_MEAN = 0.5
GELU_K = math.sqrt(2.0 / math.pi)
GELU_C = 0.044715
F32 = jnp.float32
MESH = pl.DeviceIdType.MESH


def signed(count):
    index = np.arange(count)
    return np.where(index < count // 2, index, index - count)


def trig(freqs, places, length, factor=1.0):
    angle = 2.0 * np.pi * ((freqs[:, None] * places[None, :]) % length) / length
    return np.cos(angle) * factor, np.sin(angle) * factor


def z_tables(modes, depth):
    cos, sin = trig(np.arange(modes), np.arange(depth), depth)
    lanes = 2 * modes
    weight = np.where(np.arange(modes) == 0, 1.0, 2.0) / depth
    both = np.stack([cos, -sin])

    def blocks(one):
        full = np.zeros((2 * depth, 2 * lanes))
        full[:depth, :lanes] = one
        full[depth:, lanes:] = one
        return full

    plain = both.reshape(lanes, depth).T
    heavy = (both * weight[None, :, None]).reshape(lanes, depth).T
    return blocks(plain), blocks(heavy), blocks(heavy).T


def tables(gx, gy, cx, cy, depth, kx, ky, kz):
    nx, ny = gx * cx, gy * cy
    own = kx // gx
    zf, zg, zi = z_tables(kz, depth)
    cosx, sinx = trig(signed(kx), np.arange(nx), nx)
    cosy, siny = trig(signed(ky), np.arange(ny), ny)
    tx = np.concatenate([cosx, sinx]).reshape(2 * kx, gx, cx).transpose(1, 2, 0)
    ty = np.zeros((gy, own, cy, 2, ky, own))
    both = np.stack([cosy, siny]).reshape(2, ky, gy, cy).transpose(2, 3, 0, 1)
    for k in range(own):
        ty[:, k, :, :, :, k] = both
    ty = ty.reshape(gy, own * cy, 2 * ky * own)
    team = 4 * cy
    tyi = (np.concatenate([cosy, -siny]).T / ny).reshape(ny // team, team, 2 * ky)
    txi = np.concatenate([cosx, -sinx]).T / nx
    txf = np.stack([cosx, sinx]).reshape(2, gx, own, nx).transpose(0, 2, 1, 3).reshape(2 * kx, nx) / nx
    tyf = (np.concatenate([cosy, siny]) / ny).reshape(2 * ky, ny // team, team).transpose(1, 0, 2)
    right = [in_three(t, 0) for t in (zf, zg, zi)]
    left = [in_three(t, t.ndim - 1) for t in (tyi, txi, txf, tyf)]
    return right + [np.asarray(tx, np.float32), np.asarray(ty, np.float32)] + left


def in_three(table, axis):
    table = np.asarray(table, np.float32)
    high = table.astype(jnp.bfloat16)
    low = (table - high.astype(np.float32)).astype(jnp.bfloat16)
    return np.concatenate([high, low, high], axis=axis)


def parts(v, axis, order):
    high = v.astype(jnp.bfloat16)
    low = (v - high.astype(F32)).astype(jnp.bfloat16)
    return jnp.concatenate([(high, low)[k] for k in order], axis=axis)


def dot_right(v, table):
    return jnp.dot(parts(v, 1, (0, 0, 1)), table, preferred_element_type=F32)


def dot_left(table, v):
    return jnp.dot(table, parts(v, 0, (0, 0, 1)), preferred_element_type=F32)


def dot_pick(v, pick):
    high = v.astype(jnp.bfloat16)
    low = (v - high.astype(F32)).astype(jnp.bfloat16)
    pick = pick.astype(jnp.bfloat16)
    return jnp.dot(high, pick, preferred_element_type=F32) + jnp.dot(low, pick, preferred_element_type=F32)


def dot(a, b, dims=((1,), (0,))):
    return lax.dot_general(a, b, (dims, ((), ())), precision=lax.Precision.HIGHEST, preferred_element_type=F32)


def iota(shape, dim):
    return lax.broadcasted_iota(jnp.int32, shape, dim)


def rot(v):
    imag = (iota(v.shape, 1) // 32) % 2 == 1
    return jnp.where(imag, -pltpu.roll(v, 32, 1), pltpu.roll(v, 96, 1))


def diffusivity(p):
    return SOLID_DIFF + (LIQUID_DIFF - SOLID_DIFF) * 0.5 * (1.0 - jnp.tanh(p))


def around(ref, x):
    centre = ref[x]
    rows, depth = centre.shape
    return centre, [
        ref[x + 1],
        ref[x - 1],
        pltpu.roll(centre, rows - 1, 0),
        pltpu.roll(centre, 1, 0),
        pltpu.roll(centre, depth - 1, 1),
        pltpu.roll(centre, 1, 1),
    ]


def advance(p_ref, c_ref, d_ref, undercool, x):
    p, p_nb = around(p_ref, x)
    c, c_nb = around(c_ref, x)
    d, d_nb = around(d_ref, x)
    total = p_nb[0]
    for one in p_nb[1:]:
        total = total + one
    squares = 1.0 - p * p
    rate = total - 6.0 * p + p - p * p * p + COUPLING * squares * squares * (undercool - c)
    div = 0.0
    for dn, cn in zip(d_nb, c_nb):
        div = div + 0.5 * (d + dn) * (cn - c)
    speed = TRAP_RATE * jnp.abs(rate)
    keff = (PARTITION + speed) / (1.0 + speed)
    return p + TIME_STEP * rate, c + TIME_STEP * (div + 0.5 * (1.0 - keff) * c * rate)


def partners(ix, gx, sign):
    if gx != 16:
        steps = [lax.rem(ix + gx + sign * k, gx) for k in range(gx)]
        return steps, None
    x, y, core = ix // 8, lax.rem(ix // 2, 4), lax.rem(ix, 2)
    xs = [8 * x, 8 * (1 - x)]
    ys = [2 * lax.rem(y + 4 + sign * d, 4) for d in range(4)]
    cores = [core, 1 - core]
    steps = [xs[dx] + ys[dy] + cores[c] for dx, dy in ((0, 0), (1, 0), (0, 2), (1, 2), (1, 1), (1, 3), (0, 1), (0, 3)) for c in range(2)]

    def group(j):
        found = []
        for b in range(2):
            dx = jnp.where(j < 2, b, 3 - j)
            dy = jnp.where(j < 2, 2 * j, 1 + 2 * b)
            at = jnp.where(dx == 1, xs[1], xs[0]) + 2 * lax.rem(y + 4 + sign * dy, 4)
            found += [at + cores[0], at + cores[1]]
        return found

    return steps, group


def kernel(
    dims, start, ready, phase, solute, undercool, cotangent, weight, lift, local, bias, proj,
    zf, zg, zi, tx, ty, tyi, txi, txf, tyf,
    phase_far, solute_far, predicted_far, modes_far, spec_far, added_far,
    phase_out, solute_out, predicted_out, spec_out, added_out, modes_out, out_sem,
    yhi, ylo, thin, weave, from_ylo, from_yhi, from_corner, from_xlo, from_xhi,
    pad_p, pad_c, pad_d, pad_u, mid_p, mid_c, mid_d, flat, cells, cot, total, coef, lifted, blend, field, sums,
    send1, recv1, send2, recv2, send3, recv3, send4, recv5, send6, recv6, send7, recv7,
    send8, recv9, send10, recv10, send11, recv11, send12, recv12,
    halo_send, halo_recv, send_sem, recv_sem, recv6_sem,
):
    gx, gy, group = dims
    ix, iy = lax.axis_index("gx"), lax.axis_index("gy")
    east, west = lax.rem(ix + 1, gx), lax.rem(ix + gx - 1, gx)
    north, south = lax.rem(iy + 1, gy), lax.rem(iy + gy - 1, gy)
    width = lift.shape[1]
    pairs = width // 2
    kx, ky = 2 * gx, gy
    rows = gy // 4
    team, member = iy // 4, lax.rem(iy, 4)
    per = gx // 4
    holder = ix // per
    same = holder == member
    square = width * width
    outward, _ = partners(ix, gx, 1)
    inward, inward_group = partners(ix, gx, -1)
    assert inward_group or gx <= group
    barrier = pltpu.get_barrier_semaphore()

    def greet(where):
        pl.semaphore_signal(barrier, inc=1, device_id=where, device_id_type=MESH)

    def greet_y(k, carry):
        greet({"gy": lax.rem(iy + gy // 2 + k, gy)})
        greet({"gy": lax.rem(iy + gy // 2 + gy - k, gy)})
        return carry

    def greet_x(j, carry):
        greet({"gx": lax.rem(ix + j, gx)})
        return carry

    greet({"gy": lax.rem(iy + gy // 2, gy)})
    lax.fori_loop(1, gy // 2, greet_y, 0)
    for a in (east, west):
        for b in (north, south):
            greet({"gx": a, "gy": b})
    lax.fori_loop(1, gx, greet_x, 0)

    def greet_holders(q, carry):
        greet({"gx": q, "gy": 4 * team + holder})
        return carry

    def greet_owners(a, carry):
        for m in range(4):
            greet({"gx": per * member + a, "gy": 4 * team + m})
        return carry

    lax.fori_loop(0, gx, greet_holders, 0)
    lax.fori_loop(0, per, greet_owners, 0)
    start()

    ready(0, 1, 2)
    row = iota((8, 8, phase.shape[2]), 1)
    p, c, u = phase[...], solute[...], undercool[...]
    yhi[...] = jnp.where(row >= 6, p, jnp.where(row >= 4, pltpu.roll(c, 6, 1), pltpu.roll(u, 4, 1)))
    ylo[...] = jnp.where(row < 2, p, jnp.where(row < 4, pltpu.roll(c, 2, 1), pltpu.roll(u, 4, 1)))
    for k, (rows_ref, first) in enumerate(((yhi, 3), (ylo, 0))):
        for h in range(2):
            weave[h] = rows_ref[:, :, 128 * h : 128 * h + 128].reshape(64, 128)
            for r in range(5):
                thin[k, r, :, 128 * h : 128 * h + 128] = weave[h, pl.ds(first + r, 8, stride=8), :]
    pad_p[2:10, 8:16, :] = p
    pad_c[2:10, 8:16, :] = c
    pad_u[1:9, 8:16, :] = u

    depth = phase.shape[2]
    src, dst = iota((128, 128), 0), iota((128, 128), 1)
    outer = jnp.where(iota((width, square), 1) // width == iota((width, square), 0), 1.0, 0.0)

    def factors_of_channels():
        ready(5, 6, 7, 8, 3)
        inner = iota((width, square), 1) % width == iota((width, square), 0)
        eye = iota((width, width), 0) == iota((width, width), 1)

        def column(v):
            return jnp.sum(jnp.where(eye, jnp.broadcast_to(v, (width, width)), 0.0), axis=1, keepdims=True)

        def full(v):
            return jnp.broadcast_to(jnp.broadcast_to(v, (width, 128)).reshape(width, 1, 128), (width, 8, 128))

        for k in range(2):
            one = column(lift[k : k + 1, :])
            lifted[k : k + 1, :] = jnp.sum(jnp.where(inner, one, 0.0), axis=0, keepdims=True)
            mixed = jnp.sum(local[...] * lift[k : k + 1, :], axis=1, keepdims=True)
            coef[k * width : (k + 1) * width] = full(mixed)
        for k, vector in ((2, bias), (3, proj)):
            one = column(vector[...])
            coef[k * width : (k + 1) * width] = full(one)
        sums[...] = jnp.zeros_like(sums)
        total[...] = jnp.zeros_like(total)
        for x in range(8):
            for h in range(2):
                flat[h, 8 * x : 8 * x + 8, :] = cotangent[x, :, 128 * h : 128 * h + 128]
        for y in range(8):
            for h in range(2):
                cot[8 * y : 8 * y + 8, 128 * h : 128 * h + 128] = flat[h, pl.ds(y, 8, stride=8), :]

    def weights_of_fields():
        ready(4)
        fold = jnp.where(iota((square, width), 0) // width == iota((square, width), 1), 1.0, 0.0)
        for k in range(2):
            both = dot_pick(weight[...] * lifted[k : k + 1, :], fold)
            both = jnp.concatenate([both, jnp.zeros((128, 128 - width), F32)], axis=1).T
            for part in range(2):
                for x in range(2):
                    value = 0.0
                    for par in range(2):
                        pick = (src % 32 == dst % 32) & (src // 32 == part * 2 + x) & (dst // 64 == par)
                        value = value + dot_pick(both[par * pairs : (par + 1) * pairs], jnp.where(pick, 1.0, 0.0))
                    blend[2 * k + part, pl.ds(x, pairs, stride=2), :] = value

    factors_of_channels()
    pl.semaphore_wait(barrier, 4 + gx - 1 + gy - 1 + 2 * gx)

    def push(source_ref, target_ref, slot, where):
        copy = pltpu.make_async_remote_copy(
            src_ref=source_ref,
            dst_ref=target_ref,
            send_sem=halo_send.at[slot],
            recv_sem=halo_recv.at[slot],
            device_id=where,
            device_id_type=MESH,
        )
        copy.start()
        return copy

    copies = [
        push(thin.at[0], from_ylo, 0, {"gy": north}),
        push(thin.at[1], from_yhi, 1, {"gy": south}),
        push(yhi.at[7], from_corner.at[0], 2, {"gx": east, "gy": north}),
        push(yhi.at[0], from_corner.at[1], 3, {"gx": west, "gy": north}),
        push(ylo.at[7], from_corner.at[2], 4, {"gx": east, "gy": south}),
        push(ylo.at[0], from_corner.at[3], 5, {"gx": west, "gy": south}),
        push(phase.at[6:8], from_xlo.at[0:2], 6, {"gx": east}),
        push(solute.at[6:8], from_xlo.at[2:4], 7, {"gx": east}),
        push(undercool.at[7:8], from_xlo.at[4:5], 8, {"gx": east}),
        push(phase.at[0:2], from_xhi.at[0:2], 9, {"gx": west}),
        push(solute.at[0:2], from_xhi.at[2:4], 10, {"gx": west}),
        push(undercool.at[0:1], from_xhi.at[4:5], 11, {"gx": west}),
    ]
    for copy in copies:
        copy.wait_recv()

    def lay(rows, low, planes):
        at = slice(0, 8) if low else slice(16, 24)
        turn = 1 if low else -1
        pad_p[planes, at, :] = rows
        pad_c[planes, at, :] = pltpu.roll(rows, (2 * turn) % 8, 1)
        pad_u[slice(planes.start - 1, planes.stop - 1), at, :] = pltpu.roll(rows, 4, 1)

    def planes_of(got, first):
        halves = []
        for h in range(2):
            for r in range(5):
                weave[h, pl.ds(first + r, 8, stride=8), :] = got[r, :, 128 * h : 128 * h + 128]
            halves.append(weave[h].reshape(8, 8, 128))
        return jnp.concatenate(halves, axis=2)

    lay(planes_of(from_ylo, 3), True, slice(2, 10))
    lay(planes_of(from_yhi, 0), False, slice(2, 10))
    lay(from_corner[0:1], True, slice(1, 2))
    lay(from_corner[1:2], True, slice(10, 11))
    lay(from_corner[2:3], False, slice(1, 2))
    lay(from_corner[3:4], False, slice(10, 11))
    pad_p[0:2, 8:16, :] = from_xlo[0:2]
    pad_c[0:2, 8:16, :] = from_xlo[2:4]
    pad_u[0:1, 8:16, :] = from_xlo[4:5]
    pad_p[10:12, 8:16, :] = from_xhi[0:2]
    pad_c[10:12, 8:16, :] = from_xhi[2:4]
    pad_u[9:10, 8:16, :] = from_xhi[4:5]

    def first_diff(x, carry):
        pad_d[x] = diffusivity(pad_p[x])
        return carry

    def first(x, carry):
        new_p, new_c = advance(pad_p, pad_c, pad_d, pad_u[x], x + 1)
        mid_p[x] = new_p
        mid_c[x] = new_c
        mid_d[x] = diffusivity(new_p)
        return carry

    def second(x, carry):
        new_p, new_c = advance(mid_p, mid_c, mid_d, pad_u[x + 1], x + 1)
        new_p, new_c = new_p[8:16], new_c[8:16]
        phase_out[x] = new_p
        solute_out[x] = new_c
        at = pl.multiple_of(8 * x, 8)
        for h in range(2):
            flat[h, pl.ds(at, 8), :] = new_p[:, 128 * h : 128 * h + 128]
            flat[2 + h, pl.ds(at, 8), :] = new_c[:, 128 * h : 128 * h + 128] - SOLUTE_MEAN
        return carry

    lax.fori_loop(0, 12, first_diff, 0)
    lax.fori_loop(0, 10, first, 0)
    lax.fori_loop(0, 8, second, 0)
    writes = [pltpu.make_async_copy(phase_out, phase_far, out_sem.at[0]), pltpu.make_async_copy(solute_out, solute_far, out_sem.at[1])]
    for one in writes:
        one.start()
    for y in range(8):
        for h in range(4):
            cells[8 * y : 8 * y + 8, 128 * h : 128 * h + 128] = flat[h, pl.ds(y, 8, stride=8), :]

    def exchange(axis, phase_id, sends, receives):
        mine = ix if axis == "gx" else iy
        pltpu.make_async_copy(sends(mine), receives(mine), recv_sem.at[phase_id]).start()

        def to(peer):
            pltpu.make_async_remote_copy(
                src_ref=sends(peer),
                dst_ref=receives(mine),
                send_sem=send_sem.at[phase_id],
                recv_sem=recv_sem.at[phase_id],
                device_id={axis: peer},
                device_id_type=MESH,
            ).start()

        def both_ways(k, carry):
            to(lax.rem(iy + gy // 2 + k, gy))
            to(lax.rem(iy + gy // 2 + gy - k, gy))
            return carry

        if axis == "gy":
            to(lax.rem(iy + gy // 2, gy))
            lax.fori_loop(1, gy // 2, both_ways, 0)
        else:
            for k in range(1, gx):
                to(outward[1 + (k + 2) % (gx - 1)])

    def straight(phase_id, source_ref, target_ref, q, m, own):
        def far():
            pltpu.make_async_remote_copy(
                src_ref=source_ref,
                dst_ref=target_ref,
                send_sem=send_sem.at[phase_id],
                recv_sem=recv_sem.at[phase_id],
                device_id={"gx": q, "gy": 4 * team + m},
                device_id_type=MESH,
            ).start()

        if own is None:
            far()
        else:
            pl.when(own)(lambda: pltpu.make_async_copy(source_ref, target_ref, recv_sem.at[phase_id]).start())
            pl.when(jnp.logical_not(own))(far)

    def arrived(phase_id, whole):
        pltpu.make_async_copy(whole, whole, recv_sem.at[phase_id]).wait()

    ready(9, 12, 13)
    along = dot_right(cells[...], zf[...])
    lines = jnp.concatenate([along[8 * y : 8 * y + 8] for y in range(8)], axis=1)
    wave = dot(tx[ix].T, lines)
    for y in range(8):
        at = slice(128 * y, 128 * y + 128)
        send1[pl.ds(y, kx, stride=8), :] = wave[:kx, at] + rot(wave[kx:, at])
    exchange("gx", 1, lambda q: send1.at[pl.ds(pl.multiple_of(16 * q, 16), 16)], lambda q: recv1.at[q])
    weights_of_fields()
    arrived(1, recv1)
    got = recv1[0]
    for q in range(1, gx):
        got = got + recv1[q]
    wave = dot(ty[iy].T, got)
    wave = wave[: 2 * ky] + rot(wave[2 * ky :])
    send2[...] = wave.reshape(2 * ky, 1, 128)
    exchange("gy", 2, lambda q: send2.at[pl.ds(2 * q, 2)], lambda q: recv2.at[pl.ds(2 * q, 2)])
    arrived(2, recv2)
    got = recv2[...].reshape(gy, 2, 128).sum(0)
    spec_out[...] = got

    even = iota((gy, 128), 0) % 2 == 0
    spread = jnp.where(even, jnp.broadcast_to(got[0:1], (gy, 128)), jnp.broadcast_to(got[1:2], (gy, 128)))
    turned = pltpu.roll(spread, 64, 1)
    low = iota((gy, 128), 1) < 64
    value = 0.0
    for k in range(2):
        one = jnp.where(low, spread, turned) if k == 0 else jnp.where(low, turned, spread)
        value = value + blend[2 * k] * one - blend[2 * k + 1] * rot(one)
    send3[...] = value.reshape(4, rows, 128)
    exchange("gy", 3, lambda q: send3.at[lax.rem(q, 4)], lambda q: recv3.at[pl.ds(pl.multiple_of(rows * q, rows), rows)])
    ready(14, 15, 16, 17, 10, 11)

    arrived(3, recv3)
    lines = []
    for r in range(rows):
        got = recv3[pl.ds(r, ky, stride=rows), :]
        lines.append(jnp.concatenate([got, rot(got)], axis=0))
    wave = dot_left(tyi[team], jnp.concatenate(lines, axis=1))
    for r in range(rows):
        send4[:, r] = wave[:, 128 * r : 128 * r + 128].reshape(4, 8, 128)
    for d in (2, 1, 3, 0):
        m = lax.rem(member + d, 4)
        for a in range(per):
            q = per * member + a
            straight(4, send4.at[m, 2 * a : 2 * a + 2], recv5.at[pl.ds(2 * ix, 2)], q, m, q == ix if d == 0 else None)
    arrived(4, recv5)
    lines = []
    for y in range(8):
        got = recv5[:, y, :]
        lines.append(jnp.concatenate([got, rot(got)], axis=0))
    wave = dot_left(txi[...], jnp.concatenate(lines, axis=1))
    for y in range(8):
        send6[:, y] = wave[:, 128 * y : 128 * y + 128].reshape(gx, 8, 128)

    pltpu.make_async_copy(send6.at[ix], recv6.at[ix], recv6_sem.at[ix]).start()

    for peer in outward[1:]:
        pltpu.make_async_remote_copy(
            src_ref=send6.at[peer],
            dst_ref=recv6.at[ix],
            send_sem=send_sem.at[6],
            recv_sem=recv6_sem.at[ix],
            device_id={"gx": peer},
            device_id_type=MESH,
        ).start()

    def wide(o):
        one = jnp.concatenate([coef[o], coef[o]], axis=1)
        return jnp.concatenate([one, one], axis=0)

    def step(j, carry):
        owners = inward_group(j) if inward_group else inward
        for owner in owners:
            pltpu.make_async_copy(recv6.at[owner], recv6.at[owner], recv6_sem.at[owner]).wait()
        got = jnp.concatenate([recv6[owner].reshape(64, 128) for owner in owners], axis=0)
        field[...] = dot_right(got, zi[...])
        for t, owner in enumerate(owners):
            def block(r, acc):
                at = pl.ds(pl.multiple_of(16 * r, 16), 16)
                here = pl.ds(pl.multiple_of(64 * t + 16 * r, 16), 16)
                p, c, w = cells[at, :depth], cells[at, depth:], cot[at, :]
                acc = list(acc)
                out = total[at, :]
                for par in range(2):
                    m0, m1, b, q = (wide(k * width + par * pairs + owner) for k in range(4))
                    side = slice(par * depth, (par + 1) * depth)
                    pre = field[here, side] + m0 * p + m1 * c + b
                    power = pre * pre
                    half = 0.5 + 0.5 * jnp.tanh(pre * (GELU_K + (GELU_K * GELU_C) * power))
                    act = pre * half
                    slope = half + act * (1.0 - half) * (2.0 * GELU_K + (6.0 * GELU_K * GELU_C) * power)
                    out = out + q * act
                    grad = q * w * slope
                    field[here, side] = grad
                    for k, v in enumerate((grad * p, grad * c, act * w)):
                        acc[3 * par + k] = acc[3 * par + k] + (v[:8] + v[8:])
                total[at, :] = out
                return tuple(acc)

            zero = jnp.zeros((8, depth), F32)
            acc = lax.fori_loop(0, 4, block, (zero,) * 6)
            for par in range(2):
                for k in range(3):
                    one = jnp.sum(acc[3 * par + k], axis=0, keepdims=True)
                    sums[k * width + par * pairs + owner] = one[:, :128] + one[:, 128:]
        wave = dot_right(field[...], zg[...])
        for t, owner in enumerate(owners):
            send7[owner] = wave[64 * t : 64 * t + 64].reshape(8, 8, 128)

            @pl.when(owner == ix)
            def _():
                pltpu.make_async_copy(send7.at[owner], recv7.at[ix], recv_sem.at[7]).start()

            @pl.when(owner != ix)
            def _():
                pltpu.make_async_remote_copy(
                    src_ref=send7.at[owner],
                    dst_ref=recv7.at[ix],
                    send_sem=send_sem.at[7],
                    recv_sem=recv_sem.at[7],
                    device_id={"gx": owner},
                    device_id_type=MESH,
                ).start()

        return carry

    lax.fori_loop(0, gx // group, step, 0)
    for h in range(2):
        flat[h] = total[:, 128 * h : 128 * h + 128]
    for x in range(8):
        for h in range(2):
            predicted_out[x, :, 128 * h : 128 * h + 128] = flat[h, pl.ds(x, 8, stride=8), :]
    writes.append(pltpu.make_async_copy(predicted_out, predicted_far, out_sem.at[2]))
    added = dot(jnp.ones((8, 128), F32), sums[...].reshape(128, 128), ((1,), (1,)))
    send12[...] = added[0:1].reshape(1, 1, 128)
    exchange("gx", 12, lambda q: send12, lambda q: recv12.at[pl.ds(q, 1)])
    writes.append(pltpu.make_async_copy(spec_out, spec_far, out_sem.at[3]))
    for one in writes[2:]:
        one.start()

    arrived(7, recv7)
    lines = [recv7[:, y].reshape(8 * gx, 128) for y in range(8)]
    wave = dot_left(txf[...], jnp.concatenate(lines, axis=1))
    for y in range(8):
        at = slice(128 * y, 128 * y + 128)
        one = wave[:kx, at] + rot(wave[kx:, at])
        for k in range(2):
            send8[pl.ds(8 * k + y, gx, stride=16), :] = one[k * gx : (k + 1) * gx]
    block = 8 * rows
    for k in range(gx):
        at = 1 + (k + 3) % (gx - 1) if k < gx - 1 else 0
        q = outward[at]
        straight(
            9,
            send8.at[pl.ds(pl.multiple_of(16 * q, 16), 16)],
            recv9.at[pl.ds(pl.multiple_of(block * member + 16 * lax.rem(ix, per), 16), 16)],
            q,
            holder,
            same if at == 0 else None,
        )
    arrived(12, recv12)
    send11[...] = recv12[...].reshape(gx, 128).sum(0, keepdims=True).reshape(1, 1, 128)
    exchange("gy", 11, lambda q: send11, lambda q: recv11.at[pl.ds(q, 1)])
    arrived(9, recv9)
    lines = []
    for r in range(rows):
        lines.append(jnp.concatenate([recv9[block * m + 8 * r : block * m + 8 * r + 8] for m in range(4)], axis=0))
    wave = dot_left(tyf[team], jnp.concatenate(lines, axis=1))
    for r in range(rows):
        at = slice(128 * r, 128 * r + 128)
        send10[pl.ds(r, ky, stride=rows), :] = wave[:ky, at] + rot(wave[ky:, at])
    part = lambda ref: lambda q: ref.at[pl.ds(pl.multiple_of(rows * q, rows), rows)]
    exchange("gy", 10, part(send10), part(recv10))
    arrived(11, recv11)
    added_out[...] = recv11[...].reshape(gy, 128).sum(0, keepdims=True)
    writes.append(pltpu.make_async_copy(added_out, added_far, out_sem.at[4]))
    writes[4].start()
    arrived(10, recv10)
    got = recv10[0:gy]
    for g in range(1, gy // 4):
        got = got + recv10[gy * g : gy * g + gy]
    modes_out[...] = got
    writes.append(pltpu.make_async_copy(modes_out, modes_far, out_sem.at[5]))
    writes[5].start()
    for one in writes:
        one.wait()

    for copy in copies:
        copy.wait_send()
    for phase_id, whole in (
        (1, recv1.at[1:gx]),
        (2, send2.at[2 : 2 * gy]),
        (3, recv3.at[rows : gy * rows]),
        (4, recv5.at[2 : 2 * gx]),
        (6, send6.at[1:gx]),
        (7, send7.at[1:gx]),
        (9, send8.at[16 : 16 * gx]),
        (10, send10.at[rows : gy * rows]),
        (11, recv11.at[1:gy]),
        (12, recv12.at[1:gx]),
    ):
        pltpu.make_async_copy(whole, whole, send_sem.at[phase_id]).wait()

    @pl.when(jnp.logical_not(same))
    def _():
        for phase_id, whole in ((4, recv5.at[0:2]), (9, send8.at[0:16])):
            pltpu.make_async_copy(whole, whole, send_sem.at[phase_id]).wait()


def finish(
    scale, phase_in, solute_in, predicted_in, modes_in, spec_in, added_in, lift_in,
    phase_far, solute_far, predicted_far, spectral_far, local_far, proj_far,
    phase, solute, predicted, modes, spec, added, lift, spectral, local, proj, in_sem, out_sem,
):
    far_in = (phase_in, solute_in, predicted_in, modes_in, spec_in, added_in, lift_in)
    near = (phase, solute, predicted, modes, spec, added, lift)
    reads = [pltpu.make_async_copy(a, b, in_sem.at[k]) for k, (a, b) in enumerate(zip(far_in, near))]
    far_out = (phase_far, solute_far, predicted_far, spectral_far, local_far, proj_far)
    made = (phase, solute, predicted, spectral, local, proj)
    writes = [pltpu.make_async_copy(a, b, out_sem.at[k]) for k, (a, b) in enumerate(zip(made, far_out))]
    for k in (6, 4, 3, 5, 0, 1, 2):
        reads[k].start()
    width = lift.shape[1]
    pairs, square = width // 2, width * width
    outer = jnp.where(iota((width, square), 1) // width == iota((width, square), 0), 1.0, 0.0)
    inner = iota((width, square), 1) % width == iota((width, square), 0)
    eye = iota((width, width), 0) == iota((width, width), 1)
    src, dst = iota((128, 128), 0), iota((128, 128), 1)
    reads[6].wait()
    lifted = []
    for k in range(2):
        one = jnp.sum(jnp.where(eye, jnp.broadcast_to(lift[k : k + 1, :], (width, width)), 0.0), axis=1, keepdims=True)
        lifted.append(jnp.sum(jnp.where(inner, one, 0.0), axis=0, keepdims=True))
    reads[4].wait()
    reads[3].wait()
    for x in range(2):
        diagonal = jnp.where(src == dst, jnp.broadcast_to(spec[x : x + 1, :], (128, 128)), 0.0)
        column = jnp.sum(diagonal, axis=1, keepdims=True)
        source = column[:64] * lifted[0] + column[64:] * lifted[1]
        got = modes[pl.ds(x, pairs, stride=2), :]
        got = jnp.concatenate([got, pltpu.roll(got, 64, 1)], axis=0).T[:64]
        grad = dot_pick(got, outer)
        re, im = grad[:32], grad[32:]
        s_re, s_im = source[:32], source[32:]
        spectral[0, x, 0] = re * s_re + im * s_im
        spectral[1, x, 0] = im * s_re - re * s_im
    writes[3].start()
    for k in range(3):
        reads[k].wait()
        writes[k].start()
    reads[5].wait()
    scaled = added[...] * scale
    place = iota((width, 128), 1) - iota((width, 128), 0)
    value = 0.0
    for k in range(2):
        picked = jnp.where(place == k * width, jnp.broadcast_to(scaled, (width, 128)), 0.0)
        value = value + jnp.sum(picked, axis=1, keepdims=True) * lift[k : k + 1, :]
    local[...] = value
    pick = iota((128, width), 0) - iota((128, width), 1) == 2 * width
    column = jnp.sum(jnp.where(src == dst, jnp.broadcast_to(scaled, (128, 128)), 0.0), axis=1, keepdims=True)
    proj[...] = jnp.sum(jnp.where(pick, column, 0.0), axis=0, keepdims=True)
    writes[4].start()
    writes[5].start()
    for one in writes:
        one.wait()


def per_device(phase, solute, undercool, lift, weight, local, bias, proj, cotangent):
    gx, gy = lax.axis_size("gx"), lax.axis_size("gy")
    cx, cy, depth = phase.shape
    own_kx, own_ky, kz = weight.shape[1:4]
    width = lift.shape[0]
    square = width * width
    assert width == 2 * gx and gy == 2 * gx and (cx, cy, own_kx, own_ky, kz) == (8, 8, 2, 1, 32)
    consts = tables(gx, gy, cx, cy, depth, gx * own_kx, gy * own_ky, kz)
    group, rows = min(4, gx), gy // 4
    far_spec = pl.BlockSpec(memory_space=pl.ANY)
    buf = lambda *shape: pltpu.VMEM(shape, F32)
    tile = jax.ShapeDtypeStruct((cx, cy, depth), F32)
    shape = lambda *dims: jax.ShapeDtypeStruct(dims, F32)
    outs = (tile, tile, tile, shape(gy, 128), shape(2, 128), shape(1, 128))
    scratch = [
        buf(8, 8, depth), buf(8, 8, depth), buf(8, 8, depth), buf(2, 128), buf(1, 128), buf(gy, 128), pltpu.SemaphoreType.DMA((6,)),
        buf(8, 8, depth), buf(8, 8, depth), buf(2, 5, 8, depth), buf(2, 64, 128), buf(5, 8, depth), buf(5, 8, depth), buf(4, 8, depth), buf(5, 8, depth), buf(5, 8, depth),
        buf(12, 24, depth), buf(12, 24, depth), buf(12, 24, depth), buf(10, 24, depth),
        buf(10, 24, depth), buf(10, 24, depth), buf(10, 24, depth),
        buf(4, 64, 128), buf(64, 2 * depth), buf(64, depth), buf(64, depth),
        buf(4 * width, 8, 128), buf(2, square), buf(4, gy, 128), buf(64 * group, 2 * depth), buf(128, 1, 128),
        buf(16 * gx, 128), buf(gx, 16, 128), buf(2 * gy, 1, 128), buf(2 * gy, 1, 128), buf(4, rows, 128), buf(gy * rows, 128),
        buf(4, rows, 8, 128), buf(2 * gx, 8, 128), buf(gx, 8, 8, 128), buf(gx, 8, 8, 128),
        buf(gx, 8, 8, 128), buf(gx, 8, 8, 128), buf(16 * gx, 128), buf(32 * rows, 128),
        buf(gy * rows, 128), buf(gy * rows, 128), buf(1, 1, 128), buf(gy, 1, 128), buf(1, 1, 128), buf(gx, 1, 128),
        pltpu.SemaphoreType.DMA((12,)), pltpu.SemaphoreType.DMA((12,)),
        pltpu.SemaphoreType.DMA((13,)), pltpu.SemaphoreType.DMA((13,)), pltpu.SemaphoreType.DMA((gx,)),
    ]
    args = [phase, solute, undercool, cotangent, weight.reshape(128, square), lift.T, local, bias.reshape(1, -1), proj.reshape(1, -1)]
    args += [jnp.asarray(t) for t in consts]
    scratch += [pltpu.VMEM(one.shape, one.dtype) for one in args] + [pltpu.SemaphoreType.DMA((len(args),))]
    count = len(args)

    def body(*refs):
        far, rest, near, sems = refs[:count], refs[count : -count - 1], refs[-count - 1 : -1], refs[-1]
        loads = [pltpu.make_async_copy(far[k], near[k], sems.at[k]) for k in range(count)]

        def start():
            for k in (0, 1, 2, 5, 6, 7, 8, 3, 4, 9, 12, 13, 14, 15, 11, 10, 16, 17):
                loads[k].start()

        def ready(*which):
            for k in which:
                loads[k].wait()

        kernel((gx, gy, group), start, ready, *near, *rest)

    got = pl.pallas_call(
        body,
        out_shape=outs,
        in_specs=[far_spec] * count,
        out_specs=(far_spec,) * len(outs),
        scratch_shapes=scratch,
        compiler_params=pltpu.CompilerParams(collective_id=0, has_side_effects=True, vmem_limit_bytes=60 * 2**20),
        name="layer",
    )(*args)
    scale = 1.0 / math.sqrt(8 * gx * 8 * gy * depth)
    finals = (tile, tile, tile, shape(*weight.shape), shape(width, width), shape(1, width))
    got = pl.pallas_call(
        lambda *refs: finish(scale, *refs),
        out_shape=finals,
        in_specs=[far_spec] * 7,
        out_specs=(far_spec,) * 6,
        scratch_shapes=[
            buf(8, 8, depth), buf(8, 8, depth), buf(8, 8, depth), buf(gy, 128), buf(2, 128), buf(1, 128), buf(2, width),
            buf(*weight.shape), buf(width, width), buf(1, width),
            pltpu.SemaphoreType.DMA((7,)), pltpu.SemaphoreType.DMA((6,)),
        ],
        compiler_params=pltpu.CompilerParams(vmem_limit_bytes=60 * 2**20),
        name="finish",
    )(*got, lift.T)
    return (*got[:5], got[5].reshape(width))


def solution(mesh):
    tile, modes = P("gx", "gy", None), P(None, "gx", "gy", None, None)
    return jax.shard_map(
        per_device,
        mesh=mesh,
        in_specs=(tile, tile, tile, P(), modes, P(), P(), P(), tile),
        out_specs=(tile, tile, tile, modes, P(), P()),
        check_vma=False,
    )
```

```python
import math

import numpy as np

import jax
import jax.numpy as jnp
from jax import lax
from jax.experimental import pallas as pl
from jax.experimental.pallas import tpu as pltpu
from jax.sharding import PartitionSpec as P

TIME_STEP = 0.05
COUPLING = 2.0
SOLID_DIFF = 0.05
LIQUID_DIFF = 1.0
PARTITION = 0.15
TRAP_RATE = 4.0
SOLUTE_MEAN = 0.5
GELU_K = math.sqrt(2.0 / math.pi)
GELU_C = 0.044715
F32 = jnp.float32
MESH = pl.DeviceIdType.MESH


def signed(count):
    index = np.arange(count)
    return np.where(index < count // 2, index, index - count)


def trig(freqs, places, length, factor=1.0):
    angle = 2.0 * np.pi * ((freqs[:, None] * places[None, :]) % length) / length
    return np.cos(angle) * factor, np.sin(angle) * factor


def z_tables(modes, depth):
    cos, sin = trig(np.arange(modes), np.arange(depth), depth)
    lanes = 2 * modes
    weight = np.where(np.arange(modes) == 0, 1.0, 2.0) / depth
    both = np.stack([cos, -sin])

    def blocks(one):
        full = np.zeros((2 * depth, 2 * lanes))
        full[:depth, :lanes] = one
        full[depth:, lanes:] = one
        return full

    plain = both.reshape(lanes, depth).T
    heavy = (both * weight[None, :, None]).reshape(lanes, depth).T
    return blocks(plain), blocks(heavy), blocks(heavy).T


def tables(gx, gy, cx, cy, depth, kx, ky, kz):
    nx, ny = gx * cx, gy * cy
    own = kx // gx
    zf, zg, zi = z_tables(kz, depth)
    cosx, sinx = trig(signed(kx), np.arange(nx), nx)
    cosy, siny = trig(signed(ky), np.arange(ny), ny)
    tx = np.concatenate([cosx, sinx]).reshape(2 * kx, gx, cx).transpose(1, 2, 0)
    ty = np.zeros((gy, own, cy, 2, ky, own))
    both = np.stack([cosy, siny]).reshape(2, ky, gy, cy).transpose(2, 3, 0, 1)
    for k in range(own):
        ty[:, k, :, :, :, k] = both
    ty = ty.reshape(gy, own * cy, 2 * ky * own)
    team = 4 * cy
    tyi = (np.concatenate([cosy, -siny]).T / ny).reshape(ny // team, team, 2 * ky)
    txi = np.concatenate([cosx, -sinx]).T / nx
    txf = np.stack([cosx, sinx]).reshape(2, gx, own, nx).transpose(0, 2, 1, 3).reshape(2 * kx, nx) / nx
    tyf = (np.concatenate([cosy, siny]) / ny).reshape(2 * ky, ny // team, team).transpose(1, 0, 2)
    right = [in_three(t, 0) for t in (zf, zg, zi)]
    left = [in_three(t, t.ndim - 1) for t in (tyi, txi, txf, tyf)]
    return right + [np.asarray(tx, np.float32), np.asarray(ty, np.float32)] + left


def in_three(table, axis):
    table = np.asarray(table, np.float32)
    high = table.astype(jnp.bfloat16)
    low = (table - high.astype(np.float32)).astype(jnp.bfloat16)
    return np.concatenate([high, low, high], axis=axis)


def parts(v, axis, order):
    high = v.astype(jnp.bfloat16)
    low = (v - high.astype(F32)).astype(jnp.bfloat16)
    return jnp.concatenate([(high, low)[k] for k in order], axis=axis)


def dot_right(v, table):
    return jnp.dot(parts(v, 1, (0, 0, 1)), table, preferred_element_type=F32)


def dot_left(table, v):
    return jnp.dot(table, parts(v, 0, (0, 0, 1)), preferred_element_type=F32)


def dot_pick(v, pick):
    high = v.astype(jnp.bfloat16)
    low = (v - high.astype(F32)).astype(jnp.bfloat16)
    pick = pick.astype(jnp.bfloat16)
    return jnp.dot(high, pick, preferred_element_type=F32) + jnp.dot(low, pick, preferred_element_type=F32)


def dot(a, b, dims=((1,), (0,))):
    return lax.dot_general(a, b, (dims, ((), ())), precision=lax.Precision.HIGHEST, preferred_element_type=F32)


def iota(shape, dim):
    return lax.broadcasted_iota(jnp.int32, shape, dim)


def rot(v):
    imag = (iota(v.shape, 1) // 32) % 2 == 1
    return jnp.where(imag, -pltpu.roll(v, 32, 1), pltpu.roll(v, 96, 1))


def diffusivity(p):
    return SOLID_DIFF + (LIQUID_DIFF - SOLID_DIFF) * 0.5 * (1.0 - jnp.tanh(p))


def around(ref, x):
    centre = ref[x]
    rows, depth = centre.shape
    return centre, [
        ref[x + 1],
        ref[x - 1],
        pltpu.roll(centre, rows - 1, 0),
        pltpu.roll(centre, 1, 0),
        pltpu.roll(centre, depth - 1, 1),
        pltpu.roll(centre, 1, 1),
    ]


def advance(p_ref, c_ref, d_ref, undercool, x):
    p, p_nb = around(p_ref, x)
    c, c_nb = around(c_ref, x)
    d, d_nb = around(d_ref, x)
    total = p_nb[0]
    for one in p_nb[1:]:
        total = total + one
    squares = 1.0 - p * p
    rate = total - 6.0 * p + p - p * p * p + COUPLING * squares * squares * (undercool - c)
    div = 0.0
    for dn, cn in zip(d_nb, c_nb):
        div = div + (d + dn) * (cn - c)
    speed = TRAP_RATE * jnp.abs(rate)
    keff = (PARTITION + speed) / (1.0 + speed)
    return p + TIME_STEP * rate, c + TIME_STEP * 0.5 * (div + (1.0 - keff) * c * rate)


def partners(ix, gx, sign):
    if gx != 16:
        steps = [lax.rem(ix + gx + sign * k, gx) for k in range(gx)]
        return steps, None
    x, y, core = ix // 8, lax.rem(ix // 2, 4), lax.rem(ix, 2)
    xs = [8 * x, 8 * (1 - x)]
    ys = [2 * lax.rem(y + 4 + sign * d, 4) for d in range(4)]
    cores = [core, 1 - core]
    steps = [xs[dx] + ys[dy] + cores[c] for dx, dy in ((0, 0), (1, 0), (0, 2), (1, 2), (1, 1), (1, 3), (0, 1), (0, 3)) for c in range(2)]

    def group(j):
        found = []
        for b in range(2):
            dx = jnp.where(j < 2, b, 3 - j)
            dy = jnp.where(j < 2, 2 * j, 1 + 2 * b)
            at = jnp.where(dx == 1, xs[1], xs[0]) + 2 * lax.rem(y + 4 + sign * dy, 4)
            found += [at + cores[0], at + cores[1]]
        return found

    return steps, group


def kernel(
    dims, start, ready, phase, solute, undercool, cotangent, weight, lift, local, bias, proj,
    zf, zg, zi, tx, ty, tyi, txi, txf, tyf,
    phase_far, solute_far, predicted_far, modes_far, spec_far, added_far,
    phase_out, solute_out, predicted_out, spec_out, added_out, modes_out, out_sem,
    yhi, ylo, thin, weave, from_ylo, from_yhi, from_corner, from_xlo, from_xhi,
    pad_p, pad_c, pad_d, pad_u, mid_p, mid_c, mid_d, flat, cells, cot, total, coef, lifted, blend, field, sums,
    send1, recv1, send2, recv2, send3, recv3, send4, recv5, send6, recv6, send7, recv7,
    send8, recv9, send10, recv10, send11, recv11, send12, recv12,
    halo_send, halo_recv, send_sem, recv_sem, recv6_sem,
):
    gx, gy, group = dims
    ix, iy = lax.axis_index("gx"), lax.axis_index("gy")
    east, west = lax.rem(ix + 1, gx), lax.rem(ix + gx - 1, gx)
    north, south = lax.rem(iy + 1, gy), lax.rem(iy + gy - 1, gy)
    width = lift.shape[1]
    pairs = width // 2
    kx, ky = 2 * gx, gy
    rows = gy // 4
    team, member = iy // 4, lax.rem(iy, 4)
    per = gx // 4
    holder = ix // per
    same = holder == member
    square = width * width
    outward, _ = partners(ix, gx, 1)
    inward, inward_group = partners(ix, gx, -1)
    assert inward_group or gx <= group
    barrier = pltpu.get_barrier_semaphore()

    def greet(where):
        pl.semaphore_signal(barrier, inc=1, device_id=where, device_id_type=MESH)

    def greet_y(k, carry):
        greet({"gy": lax.rem(iy + gy // 2 + k, gy)})
        greet({"gy": lax.rem(iy + gy // 2 + gy - k, gy)})
        return carry

    def greet_x(j, carry):
        greet({"gx": lax.rem(ix + j, gx)})
        return carry

    greet({"gy": lax.rem(iy + gy // 2, gy)})
    lax.fori_loop(1, gy // 2, greet_y, 0)
    for a in (east, west):
        for b in (north, south):
            greet({"gx": a, "gy": b})
    lax.fori_loop(1, gx, greet_x, 0)

    def greet_holders(q, carry):
        greet({"gx": q, "gy": 4 * team + holder})
        return carry

    def greet_owners(a, carry):
        for m in range(4):
            greet({"gx": per * member + a, "gy": 4 * team + m})
        return carry

    lax.fori_loop(0, gx, greet_holders, 0)
    lax.fori_loop(0, per, greet_owners, 0)
    start()

    ready(0, 1, 2)
    row = iota((8, 8, phase.shape[2]), 1)
    p, c, u = phase[...], solute[...], undercool[...]
    yhi[...] = jnp.where(row >= 6, p, jnp.where(row >= 4, pltpu.roll(c, 6, 1), pltpu.roll(u, 4, 1)))
    ylo[...] = jnp.where(row < 2, p, jnp.where(row < 4, pltpu.roll(c, 2, 1), pltpu.roll(u, 4, 1)))
    for k, (rows_ref, first) in enumerate(((yhi, 3), (ylo, 0))):
        for h in range(2):
            weave[h] = rows_ref[:, :, 128 * h : 128 * h + 128].reshape(64, 128)
            for r in range(5):
                thin[k, r, :, 128 * h : 128 * h + 128] = weave[h, pl.ds(first + r, 8, stride=8), :]
    pad_p[2:10, 8:16, :] = p
    pad_c[2:10, 8:16, :] = c
    pad_u[1:9, 8:16, :] = u

    depth = phase.shape[2]
    src, dst = iota((128, 128), 0), iota((128, 128), 1)
    outer = jnp.where(iota((width, square), 1) // width == iota((width, square), 0), 1.0, 0.0)

    def factors_of_channels():
        ready(5, 6, 7, 8, 3)
        inner = iota((width, square), 1) % width == iota((width, square), 0)
        eye = iota((width, width), 0) == iota((width, width), 1)

        def column(v):
            return jnp.sum(jnp.where(eye, jnp.broadcast_to(v, (width, width)), 0.0), axis=1, keepdims=True)

        def full(v):
            return jnp.broadcast_to(jnp.broadcast_to(v, (width, 128)).reshape(width, 1, 128), (width, 8, 128))

        for k in range(2):
            one = column(lift[k : k + 1, :])
            lifted[k : k + 1, :] = jnp.sum(jnp.where(inner, one, 0.0), axis=0, keepdims=True)
            mixed = jnp.sum(local[...] * lift[k : k + 1, :], axis=1, keepdims=True)
            coef[k * width : (k + 1) * width] = full(mixed)
        for k, vector in ((2, bias), (3, proj)):
            one = column(vector[...])
            coef[k * width : (k + 1) * width] = full(one)
        sums[...] = jnp.zeros_like(sums)
        total[...] = jnp.zeros_like(total)
        for x in range(8):
            for h in range(2):
                flat[h, 8 * x : 8 * x + 8, :] = cotangent[x, :, 128 * h : 128 * h + 128]
        for y in range(8):
            for h in range(2):
                cot[8 * y : 8 * y + 8, 128 * h : 128 * h + 128] = flat[h, pl.ds(y, 8, stride=8), :]

    def weights_of_fields():
        ready(4)
        fold = jnp.where(iota((square, width), 0) // width == iota((square, width), 1), 1.0, 0.0)
        for k in range(2):
            both = dot_pick(weight[...] * lifted[k : k + 1, :], fold)
            both = jnp.concatenate([both, jnp.zeros((128, 128 - width), F32)], axis=1).T
            for part in range(2):
                for x in range(2):
                    value = 0.0
                    for par in range(2):
                        pick = (src % 32 == dst % 32) & (src // 32 == part * 2 + x) & (dst // 64 == par)
                        value = value + dot_pick(both[par * pairs : (par + 1) * pairs], jnp.where(pick, 1.0, 0.0))
                    blend[2 * k + part, pl.ds(x, pairs, stride=2), :] = value

    factors_of_channels()
    pl.semaphore_wait(barrier, 4 + gx - 1 + gy - 1 + 2 * gx)

    def push(source_ref, target_ref, slot, where):
        copy = pltpu.make_async_remote_copy(
            src_ref=source_ref,
            dst_ref=target_ref,
            send_sem=halo_send.at[slot],
            recv_sem=halo_recv.at[slot],
            device_id=where,
            device_id_type=MESH,
        )
        copy.start()
        return copy

    copies = [
        push(thin.at[0], from_ylo, 0, {"gy": north}),
        push(thin.at[1], from_yhi, 1, {"gy": south}),
        push(yhi.at[7], from_corner.at[0], 2, {"gx": east, "gy": north}),
        push(yhi.at[0], from_corner.at[1], 3, {"gx": west, "gy": north}),
        push(ylo.at[7], from_corner.at[2], 4, {"gx": east, "gy": south}),
        push(ylo.at[0], from_corner.at[3], 5, {"gx": west, "gy": south}),
        push(phase.at[6:8], from_xlo.at[0:2], 6, {"gx": east}),
        push(solute.at[6:8], from_xlo.at[2:4], 7, {"gx": east}),
        push(undercool.at[7:8], from_xlo.at[4:5], 8, {"gx": east}),
        push(phase.at[0:2], from_xhi.at[0:2], 9, {"gx": west}),
        push(solute.at[0:2], from_xhi.at[2:4], 10, {"gx": west}),
        push(undercool.at[0:1], from_xhi.at[4:5], 11, {"gx": west}),
    ]
    for copy in copies:
        copy.wait_recv()

    def lay(rows, low, planes):
        at = slice(0, 8) if low else slice(16, 24)
        turn = 1 if low else -1
        pad_p[planes, at, :] = rows
        pad_c[planes, at, :] = pltpu.roll(rows, (2 * turn) % 8, 1)
        pad_u[slice(planes.start - 1, planes.stop - 1), at, :] = pltpu.roll(rows, 4, 1)

    def planes_of(got, first):
        halves = []
        for h in range(2):
            for r in range(5):
                weave[h, pl.ds(first + r, 8, stride=8), :] = got[r, :, 128 * h : 128 * h + 128]
            halves.append(weave[h].reshape(8, 8, 128))
        return jnp.concatenate(halves, axis=2)

    lay(planes_of(from_ylo, 3), True, slice(2, 10))
    lay(planes_of(from_yhi, 0), False, slice(2, 10))
    lay(from_corner[0:1], True, slice(1, 2))
    lay(from_corner[1:2], True, slice(10, 11))
    lay(from_corner[2:3], False, slice(1, 2))
    lay(from_corner[3:4], False, slice(10, 11))
    pad_p[0:2, 8:16, :] = from_xlo[0:2]
    pad_c[0:2, 8:16, :] = from_xlo[2:4]
    pad_u[0:1, 8:16, :] = from_xlo[4:5]
    pad_p[10:12, 8:16, :] = from_xhi[0:2]
    pad_c[10:12, 8:16, :] = from_xhi[2:4]
    pad_u[9:10, 8:16, :] = from_xhi[4:5]

    def first_diff(x, carry):
        pad_d[x] = diffusivity(pad_p[x])
        return carry

    def first(x, carry):
        new_p, new_c = advance(pad_p, pad_c, pad_d, pad_u[x], x + 1)
        mid_p[x] = new_p
        mid_c[x] = new_c
        mid_d[x] = diffusivity(new_p)
        return carry

    def second(x, carry):
        new_p, new_c = advance(mid_p, mid_c, mid_d, pad_u[x + 1], x + 1)
        new_p, new_c = new_p[8:16], new_c[8:16]
        phase_out[x] = new_p
        solute_out[x] = new_c
        at = pl.multiple_of(8 * x, 8)
        for h in range(2):
            flat[h, pl.ds(at, 8), :] = new_p[:, 128 * h : 128 * h + 128]
            flat[2 + h, pl.ds(at, 8), :] = new_c[:, 128 * h : 128 * h + 128] - SOLUTE_MEAN
        return carry

    lax.fori_loop(0, 12, first_diff, 0, unroll=2)
    lax.fori_loop(0, 10, first, 0)
    lax.fori_loop(0, 8, second, 0)
    writes = [pltpu.make_async_copy(phase_out, phase_far, out_sem.at[0]), pltpu.make_async_copy(solute_out, solute_far, out_sem.at[1])]
    for one in writes:
        one.start()
    for y in range(8):
        for h in range(4):
            cells[8 * y : 8 * y + 8, 128 * h : 128 * h + 128] = flat[h, pl.ds(y, 8, stride=8), :]

    def exchange(axis, phase_id, sends, receives):
        mine = ix if axis == "gx" else iy
        pltpu.make_async_copy(sends(mine), receives(mine), recv_sem.at[phase_id]).start()

        def to(peer):
            pltpu.make_async_remote_copy(
                src_ref=sends(peer),
                dst_ref=receives(mine),
                send_sem=send_sem.at[phase_id],
                recv_sem=recv_sem.at[phase_id],
                device_id={axis: peer},
                device_id_type=MESH,
            ).start()

        def both_ways(k, carry):
            to(lax.rem(iy + gy // 2 + k, gy))
            to(lax.rem(iy + gy // 2 + gy - k, gy))
            return carry

        if axis == "gy":
            to(lax.rem(iy + gy // 2, gy))
            lax.fori_loop(1, gy // 2, both_ways, 0)
        else:
            for k in range(1, gx):
                to(outward[1 + (k + 2) % (gx - 1)])

    def straight(phase_id, source_ref, target_ref, q, m, own):
        def far():
            pltpu.make_async_remote_copy(
                src_ref=source_ref,
                dst_ref=target_ref,
                send_sem=send_sem.at[phase_id],
                recv_sem=recv_sem.at[phase_id],
                device_id={"gx": q, "gy": 4 * team + m},
                device_id_type=MESH,
            ).start()

        if own is None:
            far()
        else:
            pl.when(own)(lambda: pltpu.make_async_copy(source_ref, target_ref, recv_sem.at[phase_id]).start())
            pl.when(jnp.logical_not(own))(far)

    def arrived(phase_id, whole):
        pltpu.make_async_copy(whole, whole, recv_sem.at[phase_id]).wait()

    ready(9, 12, 13)
    along = dot_right(cells[...], zf[...])
    lines = jnp.concatenate([along[8 * y : 8 * y + 8] for y in range(8)], axis=1)
    wave = dot(tx[ix].T, lines)
    for y in range(8):
        at = slice(128 * y, 128 * y + 128)
        send1[pl.ds(y, kx, stride=8), :] = wave[:kx, at] + rot(wave[kx:, at])
    exchange("gx", 1, lambda q: send1.at[pl.ds(pl.multiple_of(16 * q, 16), 16)], lambda q: recv1.at[q])
    weights_of_fields()
    arrived(1, recv1)
    got = recv1[0]
    for q in range(1, gx):
        got = got + recv1[q]
    wave = dot(ty[iy].T, got)
    wave = wave[: 2 * ky] + rot(wave[2 * ky :])
    send2[...] = wave.reshape(2 * ky, 1, 128)
    exchange("gy", 2, lambda q: send2.at[pl.ds(2 * q, 2)], lambda q: recv2.at[pl.ds(2 * q, 2)])
    arrived(2, recv2)
    got = recv2[...].reshape(gy, 2, 128).sum(0)
    spec_out[...] = got

    even = iota((gy, 128), 0) % 2 == 0
    spread = jnp.where(even, jnp.broadcast_to(got[0:1], (gy, 128)), jnp.broadcast_to(got[1:2], (gy, 128)))
    turned = pltpu.roll(spread, 64, 1)
    low = iota((gy, 128), 1) < 64
    value = 0.0
    for k in range(2):
        one = jnp.where(low, spread, turned) if k == 0 else jnp.where(low, turned, spread)
        value = value + blend[2 * k] * one - blend[2 * k + 1] * rot(one)
    send3[...] = value.reshape(4, rows, 128)
    exchange("gy", 3, lambda q: send3.at[lax.rem(q, 4)], lambda q: recv3.at[pl.ds(pl.multiple_of(rows * q, rows), rows)])
    ready(14, 15, 16, 17, 10, 11)

    arrived(3, recv3)
    lines = []
    for r in range(rows):
        got = recv3[pl.ds(r, ky, stride=rows), :]
        lines.append(jnp.concatenate([got, rot(got)], axis=0))
    wave = dot_left(tyi[team], jnp.concatenate(lines, axis=1))
    for r in range(rows):
        send4[:, r] = wave[:, 128 * r : 128 * r + 128].reshape(4, 8, 128)
    for d in (2, 1, 3, 0):
        m = lax.rem(member + d, 4)
        for a in range(per):
            q = per * member + a
            straight(4, send4.at[m, 2 * a : 2 * a + 2], recv5.at[pl.ds(2 * ix, 2)], q, m, q == ix if d == 0 else None)
    arrived(4, recv5)
    lines = []
    for y in range(8):
        got = recv5[:, y, :]
        lines.append(jnp.concatenate([got, rot(got)], axis=0))
    wave = dot_left(txi[...], jnp.concatenate(lines, axis=1))
    for y in range(8):
        send6[:, y] = wave[:, 128 * y : 128 * y + 128].reshape(gx, 8, 128)

    pltpu.make_async_copy(send6.at[ix], recv6.at[ix], recv6_sem.at[ix]).start()

    for peer in outward[1:]:
        pltpu.make_async_remote_copy(
            src_ref=send6.at[peer],
            dst_ref=recv6.at[ix],
            send_sem=send_sem.at[6],
            recv_sem=recv6_sem.at[ix],
            device_id={"gx": peer},
            device_id_type=MESH,
        ).start()

    def wide(o):
        one = jnp.concatenate([coef[o], coef[o]], axis=1)
        return jnp.concatenate([one, one], axis=0)

    def step(j, carry):
        owners = inward_group(j) if inward_group else inward
        for owner in owners:
            pltpu.make_async_copy(recv6.at[owner], recv6.at[owner], recv6_sem.at[owner]).wait()
        got = jnp.concatenate([recv6[owner].reshape(64, 128) for owner in owners], axis=0)
        field[...] = dot_right(got, zi[...])
        for t, owner in enumerate(owners):
            def block(r, acc):
                at = pl.ds(pl.multiple_of(16 * r, 16), 16)
                here = pl.ds(pl.multiple_of(64 * t + 16 * r, 16), 16)
                p, c, w = cells[at, :depth], cells[at, depth:], cot[at, :]
                acc = list(acc)
                out = total[at, :]
                for par in range(2):
                    m0, m1, b, q = (wide(k * width + par * pairs + owner) for k in range(4))
                    side = slice(par * depth, (par + 1) * depth)
                    pre = field[here, side] + m0 * p + m1 * c + b
                    power = pre * pre
                    half = 0.5 + 0.5 * jnp.tanh(pre * (GELU_K + (GELU_K * GELU_C) * power))
                    act = pre * half
                    slope = half + act * (1.0 - half) * (2.0 * GELU_K + (6.0 * GELU_K * GELU_C) * power)
                    out = out + q * act
                    grad = q * w * slope
                    field[here, side] = grad
                    for k, v in enumerate((grad * p, grad * c, act * w)):
                        acc[3 * par + k] = acc[3 * par + k] + (v[:8] + v[8:])
                total[at, :] = out
                return tuple(acc)

            zero = jnp.zeros((8, depth), F32)
            acc = lax.fori_loop(0, 4, block, (zero,) * 6, unroll=4)
            for par in range(2):
                for k in range(3):
                    one = jnp.sum(acc[3 * par + k], axis=0, keepdims=True)
                    sums[k * width + par * pairs + owner] = one[:, :128] + one[:, 128:]
        wave = dot_right(field[...], zg[...])
        for t, owner in enumerate(owners):
            send7[owner] = wave[64 * t : 64 * t + 64].reshape(8, 8, 128)

            @pl.when(owner == ix)
            def _():
                pltpu.make_async_copy(send7.at[owner], recv7.at[ix], recv_sem.at[7]).start()

            @pl.when(owner != ix)
            def _():
                pltpu.make_async_remote_copy(
                    src_ref=send7.at[owner],
                    dst_ref=recv7.at[ix],
                    send_sem=send_sem.at[7],
                    recv_sem=recv_sem.at[7],
                    device_id={"gx": owner},
                    device_id_type=MESH,
                ).start()

        return carry

    lax.fori_loop(0, gx // group, step, 0)
    for h in range(2):
        flat[h] = total[:, 128 * h : 128 * h + 128]
    for x in range(8):
        for h in range(2):
            predicted_out[x, :, 128 * h : 128 * h + 128] = flat[h, pl.ds(x, 8, stride=8), :]
    writes.append(pltpu.make_async_copy(predicted_out, predicted_far, out_sem.at[2]))
    added = dot(jnp.ones((8, 128), F32), sums[...].reshape(128, 128), ((1,), (1,)))
    send12[...] = added[0:1].reshape(1, 1, 128)
    exchange("gx", 12, lambda q: send12, lambda q: recv12.at[pl.ds(q, 1)])
    writes.append(pltpu.make_async_copy(spec_out, spec_far, out_sem.at[3]))
    for one in writes[2:]:
        one.start()

    arrived(7, recv7)
    lines = [recv7[:, y].reshape(8 * gx, 128) for y in range(8)]
    wave = dot_left(txf[...], jnp.concatenate(lines, axis=1))
    for y in range(8):
        at = slice(128 * y, 128 * y + 128)
        one = wave[:kx, at] + rot(wave[kx:, at])
        for k in range(2):
            send8[pl.ds(8 * k + y, gx, stride=16), :] = one[k * gx : (k + 1) * gx]
    block = 8 * rows
    for k in range(gx):
        at = 1 + (k + 3) % (gx - 1) if k < gx - 1 else 0
        q = outward[at]
        straight(
            9,
            send8.at[pl.ds(pl.multiple_of(16 * q, 16), 16)],
            recv9.at[pl.ds(pl.multiple_of(block * member + 16 * lax.rem(ix, per), 16), 16)],
            q,
            holder,
            same if at == 0 else None,
        )
    arrived(12, recv12)
    send11[...] = recv12[...].reshape(gx, 128).sum(0, keepdims=True).reshape(1, 1, 128)
    exchange("gy", 11, lambda q: send11, lambda q: recv11.at[pl.ds(q, 1)])
    arrived(9, recv9)
    lines = []
    for r in range(rows):
        lines.append(jnp.concatenate([recv9[block * m + 8 * r : block * m + 8 * r + 8] for m in range(4)], axis=0))
    wave = dot_left(tyf[team], jnp.concatenate(lines, axis=1))
    for r in range(rows):
        at = slice(128 * r, 128 * r + 128)
        send10[pl.ds(r, ky, stride=rows), :] = wave[:ky, at] + rot(wave[ky:, at])
    part = lambda ref: lambda q: ref.at[pl.ds(pl.multiple_of(rows * q, rows), rows)]
    exchange("gy", 10, part(send10), part(recv10))
    arrived(11, recv11)
    added_out[...] = recv11[...].reshape(gy, 128).sum(0, keepdims=True)
    writes.append(pltpu.make_async_copy(added_out, added_far, out_sem.at[4]))
    writes[4].start()
    arrived(10, recv10)
    got = recv10[0:gy]
    for g in range(1, gy // 4):
        got = got + recv10[gy * g : gy * g + gy]
    modes_out[...] = got
    writes.append(pltpu.make_async_copy(modes_out, modes_far, out_sem.at[5]))
    writes[5].start()
    for one in writes:
        one.wait()

    for copy in copies:
        copy.wait_send()
    for phase_id, whole in (
        (1, recv1.at[1:gx]),
        (2, send2.at[2 : 2 * gy]),
        (3, recv3.at[rows : gy * rows]),
        (4, recv5.at[2 : 2 * gx]),
        (6, send6.at[1:gx]),
        (7, send7.at[1:gx]),
        (9, send8.at[16 : 16 * gx]),
        (10, send10.at[rows : gy * rows]),
        (11, recv11.at[1:gy]),
        (12, recv12.at[1:gx]),
    ):
        pltpu.make_async_copy(whole, whole, send_sem.at[phase_id]).wait()

    @pl.when(jnp.logical_not(same))
    def _():
        for phase_id, whole in ((4, recv5.at[0:2]), (9, send8.at[0:16])):
            pltpu.make_async_copy(whole, whole, send_sem.at[phase_id]).wait()


def finish(
    scale, phase_in, solute_in, predicted_in, modes_in, spec_in, added_in, lift_in,
    phase_far, solute_far, predicted_far, spectral_far, local_far, proj_far,
    phase, solute, predicted, modes, spec, added, lift, spectral, local, proj, in_sem, out_sem,
):
    far_in = (phase_in, solute_in, predicted_in, modes_in, spec_in, added_in, lift_in)
    near = (phase, solute, predicted, modes, spec, added, lift)
    reads = [pltpu.make_async_copy(a, b, in_sem.at[k]) for k, (a, b) in enumerate(zip(far_in, near))]
    far_out = (phase_far, solute_far, predicted_far, spectral_far, local_far, proj_far)
    made = (phase, solute, predicted, spectral, local, proj)
    writes = [pltpu.make_async_copy(a, b, out_sem.at[k]) for k, (a, b) in enumerate(zip(made, far_out))]
    for k in (6, 4, 3, 5, 0, 1, 2):
        reads[k].start()
    width = lift.shape[1]
    pairs, square = width // 2, width * width
    outer = jnp.where(iota((width, square), 1) // width == iota((width, square), 0), 1.0, 0.0)
    inner = iota((width, square), 1) % width == iota((width, square), 0)
    eye = iota((width, width), 0) == iota((width, width), 1)
    src, dst = iota((128, 128), 0), iota((128, 128), 1)
    reads[6].wait()
    lifted = []
    for k in range(2):
        one = jnp.sum(jnp.where(eye, jnp.broadcast_to(lift[k : k + 1, :], (width, width)), 0.0), axis=1, keepdims=True)
        lifted.append(jnp.sum(jnp.where(inner, one, 0.0), axis=0, keepdims=True))
    reads[4].wait()
    reads[3].wait()
    for x in range(2):
        diagonal = jnp.where(src == dst, jnp.broadcast_to(spec[x : x + 1, :], (128, 128)), 0.0)
        column = jnp.sum(diagonal, axis=1, keepdims=True)
        source = column[:64] * lifted[0] + column[64:] * lifted[1]
        got = modes[pl.ds(x, pairs, stride=2), :]
        got = jnp.concatenate([got, pltpu.roll(got, 64, 1)], axis=0).T[:64]
        grad = dot_pick(got, outer)
        re, im = grad[:32], grad[32:]
        s_re, s_im = source[:32], source[32:]
        spectral[0, x, 0] = re * s_re + im * s_im
        spectral[1, x, 0] = im * s_re - re * s_im
    writes[3].start()
    for k in range(3):
        reads[k].wait()
        writes[k].start()
    reads[5].wait()
    scaled = added[...] * scale
    place = iota((width, 128), 1) - iota((width, 128), 0)
    value = 0.0
    for k in range(2):
        picked = jnp.where(place == k * width, jnp.broadcast_to(scaled, (width, 128)), 0.0)
        value = value + jnp.sum(picked, axis=1, keepdims=True) * lift[k : k + 1, :]
    local[...] = value
    pick = iota((128, width), 0) - iota((128, width), 1) == 2 * width
    column = jnp.sum(jnp.where(src == dst, jnp.broadcast_to(scaled, (128, 128)), 0.0), axis=1, keepdims=True)
    proj[...] = jnp.sum(jnp.where(pick, column, 0.0), axis=0, keepdims=True)
    writes[4].start()
    writes[5].start()
    for one in writes:
        one.wait()


def per_device(phase, solute, undercool, lift, weight, local, bias, proj, cotangent):
    gx, gy = lax.axis_size("gx"), lax.axis_size("gy")
    cx, cy, depth = phase.shape
    own_kx, own_ky, kz = weight.shape[1:4]
    width = lift.shape[0]
    square = width * width
    assert width == 2 * gx and gy == 2 * gx and (cx, cy, own_kx, own_ky, kz) == (8, 8, 2, 1, 32)
    consts = tables(gx, gy, cx, cy, depth, gx * own_kx, gy * own_ky, kz)
    group, rows = min(4, gx), gy // 4
    far_spec = pl.BlockSpec(memory_space=pl.ANY)
    buf = lambda *shape: pltpu.VMEM(shape, F32)
    tile = jax.ShapeDtypeStruct((cx, cy, depth), F32)
    shape = lambda *dims: jax.ShapeDtypeStruct(dims, F32)
    outs = (tile, tile, tile, shape(gy, 128), shape(2, 128), shape(1, 128))
    scratch = [
        buf(8, 8, depth), buf(8, 8, depth), buf(8, 8, depth), buf(2, 128), buf(1, 128), buf(gy, 128), pltpu.SemaphoreType.DMA((6,)),
        buf(8, 8, depth), buf(8, 8, depth), buf(2, 5, 8, depth), buf(2, 64, 128), buf(5, 8, depth), buf(5, 8, depth), buf(4, 8, depth), buf(5, 8, depth), buf(5, 8, depth),
        buf(12, 24, depth), buf(12, 24, depth), buf(12, 24, depth), buf(10, 24, depth),
        buf(10, 24, depth), buf(10, 24, depth), buf(10, 24, depth),
        buf(4, 64, 128), buf(64, 2 * depth), buf(64, depth), buf(64, depth),
        buf(4 * width, 8, 128), buf(2, square), buf(4, gy, 128), buf(64 * group, 2 * depth), buf(128, 1, 128),
        buf(16 * gx, 128), buf(gx, 16, 128), buf(2 * gy, 1, 128), buf(2 * gy, 1, 128), buf(4, rows, 128), buf(gy * rows, 128),
        buf(4, rows, 8, 128), buf(2 * gx, 8, 128), buf(gx, 8, 8, 128), buf(gx, 8, 8, 128),
        buf(gx, 8, 8, 128), buf(gx, 8, 8, 128), buf(16 * gx, 128), buf(32 * rows, 128),
        buf(gy * rows, 128), buf(gy * rows, 128), buf(1, 1, 128), buf(gy, 1, 128), buf(1, 1, 128), buf(gx, 1, 128),
        pltpu.SemaphoreType.DMA((12,)), pltpu.SemaphoreType.DMA((12,)),
        pltpu.SemaphoreType.DMA((13,)), pltpu.SemaphoreType.DMA((13,)), pltpu.SemaphoreType.DMA((gx,)),
    ]
    args = [phase, solute, undercool, cotangent, weight.reshape(128, square), lift.T, local, bias.reshape(1, -1), proj.reshape(1, -1)]
    args += [jnp.asarray(t) for t in consts]
    scratch += [pltpu.VMEM(one.shape, one.dtype) for one in args] + [pltpu.SemaphoreType.DMA((len(args),))]
    count = len(args)

    def body(*refs):
        far, rest, near, sems = refs[:count], refs[count : -count - 1], refs[-count - 1 : -1], refs[-1]
        loads = [pltpu.make_async_copy(far[k], near[k], sems.at[k]) for k in range(count)]

        def start():
            for k in (0, 1, 2, 5, 6, 7, 8, 3, 4, 9, 12, 13, 14, 15, 11, 10, 16, 17):
                loads[k].start()

        def ready(*which):
            for k in which:
                loads[k].wait()

        kernel((gx, gy, group), start, ready, *near, *rest)

    got = pl.pallas_call(
        body,
        out_shape=outs,
        in_specs=[far_spec] * count,
        out_specs=(far_spec,) * len(outs),
        scratch_shapes=scratch,
        compiler_params=pltpu.CompilerParams(collective_id=0, has_side_effects=True, vmem_limit_bytes=60 * 2**20),
        name="layer",
    )(*args)
    scale = 1.0 / math.sqrt(8 * gx * 8 * gy * depth)
    finals = (tile, tile, tile, shape(*weight.shape), shape(width, width), shape(1, width))
    got = pl.pallas_call(
        lambda *refs: finish(scale, *refs),
        out_shape=finals,
        in_specs=[far_spec] * 7,
        out_specs=(far_spec,) * 6,
        scratch_shapes=[
            buf(8, 8, depth), buf(8, 8, depth), buf(8, 8, depth), buf(gy, 128), buf(2, 128), buf(1, 128), buf(2, width),
            buf(*weight.shape), buf(width, width), buf(1, width),
            pltpu.SemaphoreType.DMA((7,)), pltpu.SemaphoreType.DMA((6,)),
        ],
        compiler_params=pltpu.CompilerParams(vmem_limit_bytes=60 * 2**20),
        name="finish",
    )(*got, lift.T)
    return (*got[:5], got[5].reshape(width))


def solution(mesh):
    tile, modes = P("gx", "gy", None), P(None, "gx", "gy", None, None)
    return jax.shard_map(
        per_device,
        mesh=mesh,
        in_specs=(tile, tile, tile, P(), modes, P(), P(), P(), tile),
        out_specs=(tile, tile, tile, modes, P(), P()),
        check_vma=False,
    )
```
